32 devices in a mesh: fsdp: 4 (over y, core), ctx: 4 (over z), tp: 2 (over x).
Axes of the slice: x: 2, y: 2, z: 4, core: 2. Of those that a mesh axis runs over, the one named last changes fastest.
Arguments:
- layer_input: bfloat16 [4, 1024, 1536], P('fsdp', 'ctx'), may hold values from -6 to 6
- segments: int32 [4, 1024], P('fsdp', 'ctx'), may hold values from 0 to 5, as said below
- positions: int32 [4, 1024], P('fsdp', 'ctx'), may hold values from 0 to 1023, as said below
- attn_gain: bfloat16 [1536], P(('fsdp', 'ctx')), may hold values from 0.099609375 to 1.8984375
- query_proj: bfloat16 [1536, 1536], P(('fsdp', 'ctx'), 'tp'), may hold values from -0.21875 to 0.21875
- key_proj: bfloat16 [1536, 768], P(('fsdp', 'ctx'), 'tp'), may hold values from -0.21875 to 0.21875
- value_proj: bfloat16 [1536, 768], P(('fsdp', 'ctx'), 'tp'), may hold values from -0.15625 to 0.15625
- out_proj: bfloat16 [1536, 1536], P('tp', ('fsdp', 'ctx')), may hold values from -1.25 to 1.25
- mlp_gain: bfloat16 [1536], P(('fsdp', 'ctx')), may hold values from 0.099609375 to 1.8984375
- gate_proj: bfloat16 [1536, 4096], P(('fsdp', 'ctx'), 'tp'), may hold values from -0.15625 to 0.15625
- up_proj: bfloat16 [1536, 4096], P(('fsdp', 'ctx'), 'tp'), may hold values from -0.15625 to 0.15625
- down_proj: bfloat16 [4096, 1536], P('tp', ('fsdp', 'ctx')), may hold values from -0.09375 to 0.09375
- out_grad: bfloat16 [4, 1024, 1536], P('fsdp', 'ctx'), may hold values from -6 to 6
Outputs:
- layer_output: bfloat16 [4, 1024, 1536], P('fsdp', 'ctx')
- input_grad: bfloat16 [4, 1024, 1536], P('fsdp', 'ctx')
- attn_gain_grad: float32 [1536], P(('fsdp', 'ctx'))
- query_proj_grad: float32 [1536, 1536], P(('fsdp', 'ctx'), 'tp')
- key_proj_grad: float32 [1536, 768], P(('fsdp', 'ctx'), 'tp')
- value_proj_grad: float32 [1536, 768], P(('fsdp', 'ctx'), 'tp')
- out_proj_grad: float32 [1536, 1536], P('tp', ('fsdp', 'ctx'))
- mlp_gain_grad: float32 [1536], P(('fsdp', 'ctx'))
- gate_proj_grad: float32 [1536, 4096], P(('fsdp', 'ctx'), 'tp')
- up_proj_grad: float32 [1536, 4096], P(('fsdp', 'ctx'), 'tp')
- down_proj_grad: float32 [4096, 1536], P('tp', ('fsdp', 'ctx'))
The draws below stay inside these ranges and needn't reach their ends.
Inputs may be any that keep to these rules, and one draw needn't show every extreme that they name: `segments`: numbers the documents of each sequence 0, 1, 2 and so on, never falling; every document has 200 to 2000 tokens except that the last of a sequence may be cut short. `positions`: each token's offset from the first token of its document.
All inputs are finite; a program needn't handle non-finite values.
Results may differ from the reference program's by a relative error of at most 0.018.
Values may be sent and summed in bfloat16 or wider, within the bound.
A program may use at most 192 MiB of HBM per device.

```python
from functools import partial
import jax
import jax.numpy as jnp
from jax import lax

D = 1536
HQ = 16
HK = 8
DH = 96
FF = 4096
DOC_MIN = 200
DOC_MAX = 2000
SEQ = 1024
SEQS = 4


def documents(key):
    count = SEQ // DOC_MIN + 1
    lengths = jax.random.randint(jax.random.fold_in(key, 7), (SEQS, count), DOC_MIN, DOC_MAX + 1).astype(jnp.int32)
    lengths = lengths.at[SEQS - 1, :].set(DOC_MIN)
    lengths = lengths.at[0, 0].set(DOC_MAX)
    ends = jnp.cumsum(lengths, axis=1).astype(jnp.int32)
    starts = (ends - lengths).astype(jnp.int32)
    token_index = jnp.arange(SEQ, dtype=jnp.int32)
    segment = jnp.sum((ends[:, None, :] <= token_index[None, :, None]).astype(jnp.int32), axis=2).astype(jnp.int32)
    first_token = jnp.take_along_axis(starts, segment, axis=1)
    return (segment, (token_index[None, :] - first_token).astype(jnp.int32))


def draw_segments(key, part):
    return documents(key)[0]


def draw_positions(key, part):
    return documents(key)[1]


def with_spikes(entries, key, source, target, shards_of, factor):
    def block_of(dim):
        return (jnp.arange(entries.shape[dim]) // (entries.shape[dim] // shards_of)).reshape((-1,) + (1,) * (entries.ndim - 1 - dim))

    first = jax.random.permutation(key, shards_of)[block_of(target)]
    far = (block_of(target) + shards_of // 2) % shards_of
    return jnp.where((block_of(source) == first) | (block_of(source) == far), factor * entries, entries)


def steps_of(stream_key, shape, split, least, high):
    level, own = 1.0, jax.random.fold_in(stream_key, 6)
    for axis_at, shards_of in split:
        steps = jnp.exp(jax.random.uniform(jax.random.fold_in(own, axis_at), (shards_of,), jnp.float32, least / len(split), high / len(split)))
        level = level * jnp.repeat(steps, shape[axis_at] // shards_of).reshape([-1 if axis == axis_at else 1 for axis in range(len(shape))])
    return level


def gaussian(rng, extent, spread, limit, cuts=(), kind=jnp.bfloat16):
    level = steps_of(rng, extent, cuts, -0.22, 0.18) if cuts else 1.0
    values = jax.random.normal(rng, extent, jnp.float32) * spread * level
    return jnp.minimum(jnp.maximum(values, -limit), limit).astype(kind)


def noise_with(key, extent, width, most, cuts, heavy, held_as=jnp.bfloat16):
    array = width * jax.random.normal(key, extent, jnp.float32)
    if cuts:
        array = array * steps_of(key, extent, cuts, -0.22, 0.18)
    return jnp.clip(with_spikes(array, jax.random.fold_in(key, 3), *heavy), -most, most).astype(held_as)


def setup_inputs(seed: int = 0) -> dict:
    key_of = jax.random.split(jax.random.key(seed), 14)
    layer_input = gaussian(key_of[0], (SEQS, SEQ, D), 1.0, 6.0, ((0, 4), (1, 4)))
    segments = draw_segments(jax.random.fold_in(key_of[13], 71), 0)
    positions = draw_positions(jax.random.fold_in(key_of[13], 71), 0)
    attn_gain = jnp.clip(1.0 + 0.18 * jax.random.normal(key_of[3], (D,), jnp.float32), 0.099609375, 1.8984375).astype(jnp.bfloat16)
    query_proj = gaussian(key_of[4], (D, HQ * DH), (D // 2) ** -0.5, 0.21875, ((0, 16), (1, 2)))
    key_proj = gaussian(key_of[5], (D, HK * DH), (D // 2) ** -0.5, 0.21875, ((0, 16), (1, 2)))
    value_proj = gaussian(key_of[6], (D, HK * DH), D ** -0.5, 0.15625, ((0, 16), (1, 2)))
    out_proj = gaussian(key_of[7], (HQ * DH, D), (max(HQ * DH // 64, 1)) ** -0.5, 1.25, ((0, 2), (1, 16)))
    mlp_gain = jnp.clip(1.0 + 0.18 * jax.random.normal(key_of[8], (D,), jnp.float32), 0.099609375, 1.8984375).astype(jnp.bfloat16)
    gate_proj = gaussian(key_of[9], (D, FF), D ** -0.5, 0.15625, ((0, 16), (1, 2)))
    up_proj = gaussian(key_of[10], (D, FF), D ** -0.5, 0.15625, ((0, 16), (1, 2)))
    down_proj = gaussian(key_of[11], (FF, D), FF ** -0.5, 0.09375, ((0, 2), (1, 16)))
    out_grad = noise_with(key_of[12], (SEQS, SEQ, D), 1.0, 6.0, ((0, 4), (1, 4)), (1, 2, 4, 2.0))
    return dict(layer_input=layer_input, segments=segments, positions=positions, attn_gain=attn_gain, query_proj=query_proj, key_proj=key_proj, value_proj=value_proj, out_proj=out_proj, mlp_gain=mlp_gain, gate_proj=gate_proj, up_proj=up_proj, down_proj=down_proj, out_grad=out_grad)


EPS = 1e-05
THETA = 100000.0
NEGATIVE = -1e+30

@jax.custom_vjp
def low(v):
    return lax.optimization_barrier(v.astype(jnp.bfloat16)).astype(jnp.float32)

@jax.custom_vjp
def low_back(v):
    return v

def low_keep(v):
    return (low(v), None)

def low_pass(kept, grad):
    return (grad,)

def back_keep(v):
    return (v, None)

def back_low(kept, grad):
    return (low(grad),)
low.defvjp(low_keep, low_pass)
low_back.defvjp(back_keep, back_low)

def precise(left, right):
    return jnp.dot(left, right, precision=lax.Precision.HIGHEST)

def rotary_tables(positions):
    half_dim = DH // 2
    freq_index = jnp.arange(half_dim, dtype=jnp.float32)
    inverse = THETA ** (-2.0 * freq_index / DH)
    angles = positions.astype(jnp.float32)[..., None] * inverse
    return (jnp.cos(angles), jnp.sin(angles))

def rotate(field_in, cos_table, sin_table):
    half_dim = field_in.shape[-1] // 2
    front_half = field_in[..., :half_dim]
    back_half = field_in[..., half_dim:]
    return jnp.concatenate([front_half * cos_table - back_half * sin_table, back_half * cos_table + front_half * sin_table], axis=-1)

def inverse_rms(values):
    return lax.rsqrt(lax.optimization_barrier(jnp.mean(values * values, axis=-1, keepdims=True)) + EPS)

def attend(allowed, block_item):
    queries, key_rows, value_rows = block_item
    scores = jnp.einsum('qgd,kd->qgk', queries, key_rows, precision=lax.Precision.HIGHEST) * DH ** (-0.5)
    scores = low_back(scores)
    scores = jnp.where(allowed[:, None, :], scores, NEGATIVE)
    row_max = lax.optimization_barrier(jnp.max(scores, axis=-1, keepdims=True))
    exp_scores = jnp.exp(scores - row_max)
    attn_probs = low(exp_scores / lax.optimization_barrier(jnp.sum(exp_scores, axis=-1, keepdims=True)))
    return jnp.einsum('qgk,kd->qgd', attn_probs, value_rows, precision=lax.Precision.HIGHEST)

def one_sequence(params, block_item):
    seq_input, segment, cos_table, sin_table = block_item
    attn_gain, query_proj, key_proj, value_proj, out_proj, mlp_gain, gate_proj, up_proj, down_proj = params
    length = seq_input.shape[0]
    groups = HQ // HK
    normed_attn = low(seq_input * inverse_rms(seq_input) * attn_gain)
    query_pre = low_back(precise(normed_attn, query_proj)).reshape(length, HQ, DH)
    key_pre = low_back(precise(normed_attn, key_proj)).reshape(length, HK, DH)
    value_rows = low(low_back(precise(normed_attn, value_proj))).reshape(length, HK, DH)
    query_rot = low(rotate(query_pre, cos_table[:, None, :], sin_table[:, None, :]))
    key_rot = low(rotate(key_pre, cos_table[:, None, :], sin_table[:, None, :]))
    token_index = jnp.arange(length)
    allowed = (segment[:, None] == segment[None, :]) & (token_index[:, None] >= token_index[None, :])
    grouped = query_rot.reshape(length, HK, groups, DH).transpose(1, 0, 2, 3)
    mixed_heads = lax.map(jax.checkpoint(partial(attend, allowed)), (grouped, key_rot.transpose(1, 0, 2), value_rows.transpose(1, 0, 2)))
    mixed_heads = low(low_back(mixed_heads.transpose(1, 0, 2, 3).reshape(length, HQ * DH)))
    residual = seq_input + low_back(precise(mixed_heads, out_proj))
    normed_mlp = low(residual * inverse_rms(residual) * mlp_gain)
    gate_pre = low_back(precise(normed_mlp, gate_proj))
    up_pre = low_back(precise(normed_mlp, up_proj))
    hidden = low(jax.nn.silu(gate_pre) * up_pre)
    return residual + low_back(precise(hidden, down_proj))

def reference(layer_input, segments, positions, attn_gain, query_proj, key_proj, value_proj, out_proj, mlp_gain, gate_proj, up_proj, down_proj, out_grad):
    cos_table, sin_table = rotary_tables(positions)
    params = tuple((matrix.astype(jnp.float32) for matrix in (attn_gain, query_proj, key_proj, value_proj, out_proj, mlp_gain, gate_proj, up_proj, down_proj)))
    inputs = layer_input.astype(jnp.float32)

    def forward(seq_inputs, weights_all):
        return lax.map(jax.checkpoint(partial(one_sequence, weights_all)), (seq_inputs, segments, cos_table, sin_table))
    result, pullback = jax.vjp(forward, inputs, params)
    input_grad, param_grads = pullback(out_grad.astype(jnp.float32))
    return (result.astype(jnp.bfloat16), input_grad.astype(jnp.bfloat16), param_grads[0], param_grads[1], param_grads[2], param_grads[3], param_grads[4], param_grads[5], param_grads[6], param_grads[7], param_grads[8])
```

```python
import functools

import jax
import jax.numpy as jnp
from jax import lax
from jax.experimental import pallas as pl
from jax.experimental.pallas import tpu as pltpu
from jax.sharding import Mesh, PartitionSpec as P

HQ = 16
HK = 8
DH = 96


EPS = 1e-05
THETA = 100000.0
NEGATIVE = -1e30


def rotary_tables(positions):
    half_dim = DH // 2
    freq_index = jnp.arange(half_dim, dtype=jnp.float32)
    inverse = THETA ** (-2.0 * freq_index / DH)
    angles = positions.astype(jnp.float32)[..., None] * inverse
    return (jnp.cos(angles), jnp.sin(angles))


def rotate(field_in, cos_table, sin_table):
    half_dim = field_in.shape[-1] // 2
    front_half = field_in[..., :half_dim]
    back_half = field_in[..., half_dim:]
    return jnp.concatenate(
        [
            front_half * cos_table - back_half * sin_table,
            back_half * cos_table + front_half * sin_table,
        ],
        axis=-1,
    )


def unrotate(field_in, cos_table, sin_table):
    half_dim = field_in.shape[-1] // 2
    front_half = field_in[..., :half_dim]
    back_half = field_in[..., half_dim:]
    return jnp.concatenate(
        [
            front_half * cos_table + back_half * sin_table,
            back_half * cos_table - front_half * sin_table,
        ],
        axis=-1,
    )


def inverse_rms(values):
    return lax.rsqrt(jnp.mean(values * values, axis=-1, keepdims=True) + EPS)


def contract(left, right, left_dim, right_dim):
    return lax.dot_general(
        left, right, (((left_dim,), (right_dim,)), ((), ())), preferred_element_type=jnp.float32
    )


def norm_back(upstream, inner, values, scale_rows):
    cubed = scale_rows * scale_rows * scale_rows
    return (
        upstream
        + scale_rows * inner
        - values * cubed * jnp.mean(inner * values, axis=-1, keepdims=True)
    )


def to_blocks(matrix, seq_count, local_kv, groups):
    span = matrix.shape[0] // seq_count
    shaped = matrix.reshape(seq_count, span, local_kv, groups, DH).transpose(0, 2, 1, 3, 4)
    return shaped.reshape(seq_count * local_kv, span * groups, DH)


def from_blocks(blocks, seq_count, local_kv, groups):
    span = blocks.shape[1] // groups
    shaped = blocks.reshape(seq_count, local_kv, span, groups, DH).transpose(0, 2, 1, 3, 4)
    return shaped.reshape(seq_count * span, local_kv * groups * DH)


def seq_items(matrix, local_kv):
    seq_count = matrix.shape[0]
    length = matrix.shape[1]
    return (
        matrix.reshape(seq_count, length, local_kv, DH)
        .transpose(0, 2, 1, 3)
        .reshape(seq_count * local_kv, length, DH)
    )


def from_items(items, seq_count, local_kv):
    length = items.shape[1]
    return (
        items.reshape(seq_count, local_kv, length, DH)
        .transpose(0, 2, 1, 3)
        .reshape(seq_count, length, local_kv * DH)
    )


MESH_ID = pl.DeviceIdType.MESH
BF16 = jnp.bfloat16
F32 = jnp.float32
GROUP = ("fy", "pr", "ctx")
VMEM_LIMIT = 60 * 1024 * 1024
LANES = 128


def remote(src, dst, send_sem, recv_sem, device):
    return pltpu.make_async_remote_copy(
        src_ref=src,
        dst_ref=dst,
        send_sem=send_sem,
        recv_sem=recv_sem,
        device_id=device,
        device_id_type=MESH_ID,
    )


def greet(devices_and_conditions, count):
    barrier = pltpu.get_barrier_semaphore()
    for device, condition in devices_and_conditions:
        if condition is None:
            pl.semaphore_signal(barrier, inc=1, device_id=device, device_id_type=MESH_ID)
        else:

            @pl.when(condition)
            def _(device=device):
                pl.semaphore_signal(barrier, inc=1, device_id=device, device_id_type=MESH_ID)

    pl.semaphore_wait(barrier, count)


def dot(left, right, left_dim=1, right_dim=0):
    return lax.dot_general(
        left, right, (((left_dim,), (right_dim,)), ((), ())), preferred_element_type=F32
    )


def pair_kernel(nz, ng, *refs):
    raws = refs[:ng]
    small, rows_in, grad_in = refs[ng : ng + 3]
    pieces = refs[ng + 3 : 2 * ng + 3]
    smalls, rows_out, grad_out = refs[2 * ng + 3 : 2 * ng + 6]
    loc, cs, cr, zs, zr, ts, tr = refs[2 * ng + 6 :]
    y = lax.axis_index("fy")
    c = lax.axis_index("pr")
    z = lax.axis_index("ctx")
    other_y = {"fy": 1 - y}
    other_c = {"pr": 1 - c}
    greet(
        [(other_y, None), (other_c, None)] + [({"ctx": t}, z != t) for t in range(nz)], nz + 1
    )

    def small_to(t):
        return remote(small, smalls.at[y, c, z], zs.at[t], zr.at[z], {"ctx": t})

    def small_from(t):
        return remote(small, smalls.at[y, c, t], zs.at[t], zr.at[t], {"ctx": t})

    mine = pltpu.make_async_copy(small, smalls.at[y, c, z], loc.at[ng + 2])
    mine.start()
    for t in range(nz):

        @pl.when(z != t)
        def _(t=t):
            small_to(t).start()

    core = [remote(raws[g].at[1 - c], pieces[g].at[c], cs.at[g], cr.at[g], other_c) for g in range(ng)]
    local = [pltpu.make_async_copy(raws[g].at[c], pieces[g].at[c], loc.at[g]) for g in range(ng)]
    core.append(remote(rows_in, rows_out.at[c], cs.at[ng], cr.at[ng], other_c))
    core.append(remote(grad_in, grad_out.at[c], cs.at[ng + 1], cr.at[ng + 1], other_c))
    local.append(pltpu.make_async_copy(rows_in, rows_out.at[c], loc.at[ng]))
    local.append(pltpu.make_async_copy(grad_in, grad_out.at[c], loc.at[ng + 1]))
    for copy in core + local:
        copy.start()
    mine.wait()
    for t in range(nz):

        @pl.when(z != t)
        def _(t=t):
            small_from(t).wait_recv()

    line = remote(smalls.at[y, c], smalls.at[y, c], ts.at[0], tr.at[0], other_y)
    line.start()
    remote(smalls.at[1 - y, c], smalls.at[1 - y, c], ts.at[0], tr.at[0], other_y).wait_recv()
    plane = remote(smalls.at[:, c], smalls.at[:, c], ts.at[1], tr.at[1], other_c)
    plane.start()
    remote(smalls.at[:, 1 - c], smalls.at[:, 1 - c], ts.at[1], tr.at[1], other_c).wait_recv()
    for copy in core:
        copy.wait()
    for copy in local:
        copy.wait()
    line.wait_send()
    plane.wait_send()
    for t in range(nz):

        @pl.when(z != t)
        def _(t=t):
            small_to(t).wait_send()


def pair_swap(raws, small, rows, grads, ny, nz):
    ng = len(raws)
    dma = pltpu.SemaphoreType.DMA
    vmem = pl.BlockSpec(memory_space=pltpu.VMEM)
    shapes = [jax.ShapeDtypeStruct(raw.shape, raw.dtype) for raw in raws]
    shapes.append(jax.ShapeDtypeStruct((ny, 2, nz) + small.shape, small.dtype))
    shapes.append(jax.ShapeDtypeStruct((2,) + rows.shape, rows.dtype))
    shapes.append(jax.ShapeDtypeStruct((2,) + grads.shape, grads.dtype))
    results = pl.pallas_call(
        functools.partial(pair_kernel, nz, ng),
        out_shape=shapes,
        in_specs=[vmem] * (ng + 3),
        out_specs=[vmem] * (ng + 3),
        scratch_shapes=[
            dma((ng + 3,)),
            dma((ng + 2,)),
            dma((ng + 2,)),
            dma((nz,)),
            dma((nz,)),
            dma((2,)),
            dma((2,)),
        ],
        name="pair_swap",
        compiler_params=pltpu.CompilerParams(collective_id=0, has_side_effects=True),
    )(*raws, small, rows, grads)
    return results[:ng], results[ng], results[ng + 1], results[ng + 2]


class Gather:
    def __init__(self, nz, outs, us, ur, ds, dr, ys, yr, es, er):
        self.nz, self.outs = nz, outs
        self.sems = (us, ur, ds, dr, ys, yr, es, er)
        self.y = lax.axis_index("fy")
        self.z = lax.axis_index("ctx")
        self.odd = lax.rem(self.z, 2)
        self.pair = self.z + 1 - 2 * self.odd

    def up(self, g, s, slot):
        piece = self.outs[g].at[self.y, :, self.z - s]
        us, ur = self.sems[0], self.sems[1]
        return remote(piece, piece, us.at[g, slot], ur.at[g, slot], {"ctx": self.z + 1})

    def down(self, g, s, slot):
        piece = self.outs[g].at[self.y, :, self.z + s]
        ds, dr = self.sems[2], self.sems[3]
        return remote(piece, piece, ds.at[g, slot], dr.at[g, slot], {"ctx": self.z - 1})

    def across(self, g, slot, origin, half, row):
        piece = self.outs[g].at[row, 0, origin] if half else self.outs[g].at[row, :, origin]
        ys, yr = self.sems[4], self.sems[5]
        return remote(piece, piece, ys.at[g, slot], yr.at[g, slot], {"fy": 1 - self.y})

    def extra(self, g, origin):
        piece = self.outs[g].at[1 - self.y, 1, origin]
        es, er = self.sems[6], self.sems[7]
        return remote(piece, piece, es.at[g], er.at[g], {"ctx": self.pair})

    def own_z(self, g):
        @pl.when(self.z < self.nz - 1)
        def _():
            self.up(g, 0, 0).start()

        @pl.when(self.z > 0)
        def _():
            self.down(g, 0, 0).start()

    def own_y(self, g):
        self.across(g, 0, self.z, False, self.y).start()

    def each_across(self, g, s, row, act):
        z, nz = self.z, self.nz
        if s == 0:
            act(self.across(g, 0, z, False, row))
            return
        if s == 1:

            @pl.when(self.odd == 1)
            def _():
                act(self.across(g, 1, z - 1, True, row))

            @pl.when((self.odd == 0) & (z > 0))
            def _():
                act(self.across(g, 1, z - 1, False, row))

            @pl.when(self.odd == 0)
            def _():
                act(self.across(g, nz, z + 1, True, row))

            @pl.when((self.odd == 1) & (z < nz - 1))
            def _():
                act(self.across(g, nz, z + 1, False, row))

            return

        @pl.when(z >= s)
        def _():
            act(self.across(g, s, z - s, False, row))

        @pl.when(z + s < nz)
        def _():
            act(self.across(g, nz - 1 + s, z + s, False, row))

    def step(self, g, s):
        z, nz = self.z, self.nz

        @pl.when(z >= s)
        def _():
            self.up(g, s - 1 + 1, s - 1).wait_recv()

            @pl.when(z < nz - 1)
            def _():
                self.up(g, s, s).start()

        @pl.when(z + s < nz)
        def _():
            self.down(g, s, s - 1).wait_recv()

            @pl.when(z > 0)
            def _():
                self.down(g, s, s).start()

        self.each_across(g, s, self.y, lambda copy: copy.start())

    def spread(self, g):
        self.across(g, 0, self.z, False, 1 - self.y).wait_recv()
        self.extra(g, self.z).start()

    def finish(self, g):
        for s in range(1, self.nz):
            self.each_across(g, s, 1 - self.y, lambda copy: copy.wait_recv())
        self.extra(g, self.pair).wait_recv()

    def drain(self, g):
        z, nz = self.z, self.nz
        for s in range(nz):

            @pl.when((z >= s) & (z < nz - 1))
            def _(s=s):
                self.up(g, s, s).wait_send()

            @pl.when((z + s < nz) & (z > 0))
            def _(s=s):
                self.down(g, s, s).wait_send()

            self.each_across(g, s, self.y, lambda copy: copy.wait_send())
        self.extra(g, self.z).wait_send()


def forward_kernel(nz, items, scale, *refs):
    (normed, rows, cos, sin, q_seg, k_seg, spread_mat, gain) = refs[5:13]
    pieces = refs[:5]
    outs = refs[13:18]
    (q_out, k_out, v_out, mixed_out, mixed_low, lse_out, residual, normed_mlp) = refs[18:26]
    (acc, kvu, top, core_send, core_land, x_send, x_land, attended) = refs[26:34]
    loc, us, ur, ds, dr, ys, yr, es, er, ks, kr, cs, cr, xs, xr, ns, nr = refs[34:]
    y = lax.axis_index("fy")
    c = lax.axis_index("pr")
    z = lax.axis_index("ctx")
    x = lax.axis_index("tp")
    span = rows.shape[0]
    other_c = {"pr": 1 - c}
    other_x = {"tp": 1 - x}
    gather = Gather(nz, outs, us, ur, ds, dr, ys, yr, es, er)
    greet(
        [
            ({"fy": 1 - y}, None),
            (other_c, None),
            (other_x, None),
            ({"ctx": z + 1}, z < nz - 1),
            ({"ctx": z - 1}, z > 0),
        ],
        3 + (z < nz - 1).astype(jnp.int32) + (z > 0).astype(jnp.int32),
    )
    local = [pltpu.make_async_copy(pieces[g], outs[g].at[y, :, z], loc.at[g]) for g in range(5)]
    for copy in local:
        copy.start()
    early, late = (0, 1), (2, 3, 4)
    for g in early:
        local[g].wait()
        gather.own_z(g)
        gather.own_y(g)
    for g in late:
        local[g].wait()
    for s in range(1, nz):
        for g in early:
            gather.step(g, s)
        if s == 1:
            for g in early:
                gather.spread(g)
        if s == min(2, nz - 1):
            for g in late:
                gather.own_z(g)
    for g in late:
        gather.own_y(g)
    for g in early:
        gather.finish(g)

    chunk = nz * outs[0].shape[3]
    half = outs[0].shape[4] // 2
    for i in range(4):
        block = outs[0][i // 2, i % 2].reshape(chunk, 2 * half)
        wide = jnp.concatenate(
            [
                dot(block[:, :half], spread_mat[...]).astype(BF16),
                dot(block[:, half:], spread_mat[...]).astype(BF16),
            ],
            axis=1,
        )
        part = dot(normed[:, i * chunk : (i + 1) * chunk], wide)
        if i == 0:
            acc[...] = part
        else:
            acc[...] += part

    def rotated(b, lane):
        field = acc[pl.ds(b * span, span), pl.ds(lane * LANES, LANES)]
        turned = pltpu.roll(field, LANES // 2, 1)
        return (field * cos[pl.ds(b * span, span)] + turned * sin[pl.ds(b * span, span)]).astype(
            BF16
        )

    def keys_up(b, s):
        piece = kvu.at[z - s, b]
        return remote(piece, piece, ks.at[b, s], kr.at[b, s], {"ctx": z + 1})

    def keys_from(b, s):
        piece = kvu.at[z - s, b]
        return remote(piece, piece, ks.at[b, s - 1], kr.at[b, s - 1], {"ctx": z - 1})

    for b in range(2):
        fields = []
        for k in range(2):
            k_out[z, b * 2 + k] = rotated(b, 4 + k)
            fields.append(k_out[z, b * 2 + k])
        for k in range(2):
            v_out[z, b * 2 + k] = acc[
                pl.ds(b * span, span), pl.ds((6 + k) * LANES, LANES)
            ].astype(BF16)
            fields.append(v_out[z, b * 2 + k])
        kvu[z, b] = dot(jnp.concatenate(fields, axis=1), spread_mat[...], 1, 1).astype(BF16)

        @pl.when(z < nz - 1)
        def _(b=b):
            keys_up(b, 0).start()

    for b in range(2):
        for k in range(2):
            for j in range(2):
                q_out[b * 2 + k, pl.ds(j * span, span)] = rotated(b, 2 * k + j)

    def attend(block, first):
        def one(i, _):
            b = i // 2
            scores = dot(q_out[i], k_out[block, i], 1, 1) * scale
            allowed = q_seg[b] == k_seg[b, block]
            if first:
                row = lax.broadcasted_iota(jnp.int32, scores.shape, 0)
                column = lax.broadcasted_iota(jnp.int32, scores.shape, 1)
                allowed = allowed & (lax.rem(row, span) >= column)
            scores = jnp.where(allowed, scores, NEGATIVE)
            peak = jnp.max(scores, axis=1, keepdims=True)
            if first:
                probs = jnp.exp(scores - peak)
                total = jnp.sum(probs, axis=1, keepdims=True)
                mixed_out[i] = dot(probs.astype(BF16), v_out[block, i])
            else:
                old = top[i][:, :1]
                peak = jnp.maximum(old, peak)
                keep = jnp.exp(old - peak)
                probs = jnp.exp(scores - peak)
                total = keep * lse_out[i][:, :1] + jnp.sum(probs, axis=1, keepdims=True)
                mixed_out[i] = keep * mixed_out[i] + dot(probs.astype(BF16), v_out[block, i])
            top[i] = jnp.broadcast_to(peak, top.shape[1:])
            lse_out[i] = jnp.broadcast_to(total, lse_out.shape[1:])
            return 0

        lax.fori_loop(0, items, one, 0)

    attend(z, True)
    for g in late:
        gather.step(g, 1)
    for s in range(1, nz):

        @pl.when(z >= s)
        def _(s=s):
            for b in range(2):
                keys_from(b, s).wait_recv()

                @pl.when(z < nz - 1)
                def _(b=b):
                    keys_up(b, s).start()

                wide = dot(kvu[z - s, b], spread_mat[...]).astype(BF16)
                for k in range(2):
                    k_out[z - s, b * 2 + k] = wide[:, k * LANES : (k + 1) * LANES]
                    v_out[z - s, b * 2 + k] = wide[:, (2 + k) * LANES : (3 + k) * LANES]
            attend(z - s, False)

        if s == 1:
            for g in late:
                gather.spread(g)

    for i in range(items):
        total = lse_out[i]
        mixed_out[i] = mixed_out[i] / total
        lse_out[i] = top[i] + jnp.log(total)
    for b in range(2):
        heads = [
            mixed_out[b * 2 + k, pl.ds(j * span, span)].astype(BF16)
            for k in range(2)
            for j in range(2)
        ]
        mixed_low[pl.ds(b * span, span)] = dot(
            jnp.concatenate(heads, axis=1), spread_mat[...], 1, 1
        ).astype(BF16)
    for g in late:
        if nz > 2:
            gather.step(g, 2)

    def core(i):
        return remote(core_send.at[i], core_land.at[i], cs.at[i], cr.at[i], other_c)

    def sideways(i):
        return remote(x_send.at[i], x_land.at[i], xs.at[i], xr.at[i], other_x)

    def projected(who, i):
        weights = outs[1][i // 2, i % 2].reshape(chunk, half)
        return dot(mixed_low[pl.ds(pl.multiple_of(who * span, span), span)], weights, 1, 1)

    for i in range(4):
        core_send[i] = projected(1 - c, i).astype(BF16)
        core(i).start()
    for i in range(4):
        part = projected(c, i)
        core(i).wait_recv()
        x_send[i] = (part + core_land[i].astype(F32)).astype(BF16)
        sideways(i).start()
    for s in range(3, nz):
        for g in late:
            gather.step(g, s)
    squares = jnp.zeros((span, 1), F32)
    for i in range(4):
        sideways(i).wait_recv()
        column = pl.ds(i * chunk, chunk)
        total = rows[:, column].astype(F32) + (x_send[i].astype(F32) + x_land[i].astype(F32))
        residual[:, column] = total
        squares = squares + jnp.sum(total * total, axis=1, keepdims=True)
    factor = lax.rsqrt(squares / (4 * chunk) + EPS)
    normed_mlp[c] = (residual[...] * factor * gain[...]).astype(BF16)
    swap = remote(normed_mlp.at[c], normed_mlp.at[c], ns.at[0], nr.at[0], other_c)
    swap.start()
    remote(normed_mlp.at[1 - c], normed_mlp.at[1 - c], ns.at[0], nr.at[0], other_c).wait_recv()
    for g in late:
        gather.finish(g)
    for g in range(5):
        gather.drain(g)
    for b in range(2):
        for s in range(nz):

            @pl.when((z >= s) & (z < nz - 1))
            def _(b=b, s=s):
                keys_up(b, s).wait_send()

    for i in range(4):
        core(i).wait_send()
        sideways(i).wait_send()
    swap.wait_send()


def forward(pieces, normed, rows, cos, sin, q_seg, k_seg, spread_mat, gain, ny, nz):
    dma = pltpu.SemaphoreType.DMA
    vmem = pl.BlockSpec(memory_space=pltpu.VMEM)
    span, width = rows.shape
    items, q_rows = 4, 2 * span
    shape = jax.ShapeDtypeStruct
    chunk = width // 4
    out_shape = [shape((ny, 2, nz) + piece.shape[1:], BF16) for piece in pieces] + [
        shape((items, q_rows, LANES), BF16),
        shape((nz, items, span, LANES), BF16),
        shape((nz, items, span, LANES), BF16),
        shape((items, q_rows, LANES), F32),
        shape((2 * span, 4 * DH), BF16),
        shape((items, q_rows, LANES), F32),
        shape((span, width), F32),
        shape((2, span, width), BF16),
    ]
    return pl.pallas_call(
        functools.partial(forward_kernel, nz, items, DH ** (-0.5)),
        out_shape=out_shape,
        in_specs=[vmem] * 13,
        out_specs=[vmem] * len(out_shape),
        scratch_shapes=[
            pltpu.VMEM((2 * span, 8 * LANES), F32),
            pltpu.VMEM((nz, 2, span, 4 * DH), BF16),
            pltpu.VMEM((items, q_rows, LANES), F32),
        ]
        + [pltpu.VMEM((4, span, chunk), BF16)] * 4
        + [pltpu.VMEM((8, LANES), F32)]
        + [dma((5,))]
        + [dma((5, nz))] * 4
        + [dma((5, 2 * nz))] * 2
        + [dma((5,))] * 2
        + [dma((2, nz))] * 2
        + [dma((4,))] * 4
        + [dma((1,))] * 2,
        name="forward",
        compiler_params=pltpu.CompilerParams(
            collective_id=1, has_side_effects=True, vmem_limit_bytes=VMEM_LIMIT
        ),
    )(*pieces, normed, rows, cos, sin, q_seg, k_seg, spread_mat, gain)


def keys_down_kernel(nz, grads, out, sends, lands, ds, dr):
    z = lax.axis_index("ctx")
    greet(
        [({"ctx": z + 1}, z < nz - 1), ({"ctx": z - 1}, z > 0)],
        (z < nz - 1).astype(jnp.int32) + (z > 0).astype(jnp.int32),
    )

    def down(b, t):
        return remote(sends.at[t, b], lands.at[t, b], ds.at[b, t], dr.at[b, t], {"ctx": z - 1})

    for t in range(nz):
        for b in range(2):

            @pl.when(z >= t)
            def _(b=b, t=t):
                @pl.when(z < nz - 1)
                def _():
                    down(b, t).wait_recv()
                    sends[t, b] = (grads[t, b].astype(F32) + lands[t, b].astype(F32)).astype(BF16)

                @pl.when(z == nz - 1)
                def _():
                    sends[t, b] = grads[t, b]

                @pl.when(z > t)
                def _():
                    down(b, t).start()

                @pl.when(z == t)
                def _():
                    out[b] = sends[t, b]

    for t in range(nz):
        for b in range(2):

            @pl.when(z > t)
            def _(b=b, t=t):
                down(b, t).wait_send()


def keys_down(grads, nz):
    dma = pltpu.SemaphoreType.DMA
    vmem = pl.BlockSpec(memory_space=pltpu.VMEM)
    return pl.pallas_call(
        functools.partial(keys_down_kernel, nz),
        out_shape=jax.ShapeDtypeStruct(grads.shape[1:], BF16),
        in_specs=[vmem],
        out_specs=vmem,
        scratch_shapes=[
            pltpu.VMEM(grads.shape, BF16),
            pltpu.VMEM(grads.shape, BF16),
            dma((2, nz)),
            dma((2, nz)),
        ],
        name="keys_down",
        compiler_params=pltpu.CompilerParams(
            collective_id=2, has_side_effects=True, vmem_limit_bytes=VMEM_LIMIT
        ),
    )(grads)


CHUNKS = 4


def sum_kernel(part, out, core_send, core_land, x_send, x_land, cs, cr, xs, xr, fs, fr):
    c = lax.axis_index("pr")
    x = lax.axis_index("tp")
    other_c = {"pr": 1 - c}
    other_x = {"tp": 1 - x}
    greet([(other_c, None), (other_x, None)], 2)
    rows = part.shape[1] // CHUNKS

    def core(i):
        return remote(core_send.at[i], core_land.at[i], cs.at[i], cr.at[i], other_c)

    def across(i):
        return remote(x_send.at[i], x_land.at[i], xs.at[i], xr.at[i], other_x)

    def final(i):
        piece = out.at[c, pl.ds(i * rows, rows)]
        return remote(piece, piece, fs.at[i], fr.at[i], other_c)

    def final_from(i):
        piece = out.at[1 - c, pl.ds(i * rows, rows)]
        return remote(piece, piece, fs.at[i], fr.at[i], other_c)

    for i in range(CHUNKS):
        core_send[i] = part[1 - c, pl.ds(i * rows, rows)].astype(BF16)
        core(i).start()
    for i in range(CHUNKS):
        core(i).wait_recv()
        x_send[i] = (
            part[c, pl.ds(i * rows, rows)].astype(F32) + core_land[i].astype(F32)
        ).astype(BF16)
        across(i).start()
    for i in range(CHUNKS):
        across(i).wait_recv()
        out[c, pl.ds(i * rows, rows)] = x_send[i].astype(F32) + x_land[i].astype(F32)
        final(i).start()
    for i in range(CHUNKS):
        final_from(i).wait_recv()
    for i in range(CHUNKS):
        core(i).wait_send()
        across(i).wait_send()
        final(i).wait_send()


def sum_parts(part):
    dma = pltpu.SemaphoreType.DMA
    vmem = pl.BlockSpec(memory_space=pltpu.VMEM)
    rows, width = part.shape[1] // CHUNKS, part.shape[2]
    return pl.pallas_call(
        sum_kernel,
        out_shape=jax.ShapeDtypeStruct(part.shape, F32),
        in_specs=[vmem],
        out_specs=vmem,
        scratch_shapes=[pltpu.VMEM((CHUNKS, rows, width), BF16)] * 4 + [dma((CHUNKS,))] * 6,
        name="sum_parts",
        compiler_params=pltpu.CompilerParams(
            collective_id=3, has_side_effects=True, vmem_limit_bytes=VMEM_LIMIT
        ),
    )(part)


def inward(nz):
    order = []
    for k in range((nz + 1) // 2):
        order.append(nz - 1 - k)
        if k != nz - 1 - k:
            order.append(k)
    return order


def scatter_kernel(nz, ng, *refs):
    parts = refs[:ng]
    small = refs[ng]
    outs = refs[ng + 1 : 2 * ng + 1]
    smalls = refs[2 * ng + 1]
    scratch = refs[2 * ng + 2 :]
    owns, lands, ins, sends, totals = (scratch[i * ng : (i + 1) * ng] for i in range(5))
    loc, ys, yr, zs, zr, cs, cr, ws, wr, ts, tr = scratch[5 * ng :]
    y = lax.axis_index("fy")
    c = lax.axis_index("pr")
    z = lax.axis_index("ctx")
    other_y = {"fy": 1 - y}
    other_c = {"pr": 1 - c}
    greet(
        [(other_y, None), (other_c, None)] + [({"ctx": t}, z != t) for t in range(nz)], nz + 1
    )

    def across(g, t):
        return remote(parts[g].at[1 - y, :, t], lands[g].at[t], ys.at[g, t], yr.at[g, t], other_y)

    def own(g, t):
        return pltpu.make_async_copy(parts[g].at[y, :, t], owns[g].at[t], loc.at[g, t])

    def up(g, t):
        return remote(
            sends[g].at[t], ins[g].at[0, t], zs.at[0, g, t], zr.at[0, g, t], {"ctx": z + 1}
        )

    def down(g, t):
        return remote(
            sends[g].at[t], ins[g].at[1, t], zs.at[1, g, t], zr.at[1, g, t], {"ctx": z - 1}
        )

    def swap(g):
        return remote(totals[g].at[1 - c], outs[g].at[c], cs.at[g], cr.at[g], other_c)

    def keep(g):
        return pltpu.make_async_copy(totals[g].at[c], outs[g].at[c], loc.at[ng, g])

    def swap_from(g):
        return remote(totals[g].at[1 - c], outs[g].at[1 - c], cs.at[g], cr.at[g], other_c)

    def small_to(t):
        return remote(smalls.at[:, c, z], smalls.at[:, c, z], ws.at[t], wr.at[z], {"ctx": t})

    def small_from(t):
        return remote(smalls.at[:, c, t], smalls.at[:, c, t], ws.at[t], wr.at[t], {"ctx": t})

    def rows_of(g):
        block = owns[g].shape[2]
        return 32 if block % 32 == 0 else block

    def each_tile(g, body):
        rows = rows_of(g)
        per = owns[g].shape[2] // rows

        def step(i, _):
            body(i // per, pl.ds(pl.multiple_of((i % per) * rows, 8), rows))
            return 0

        lax.fori_loop(0, 2 * per, step, 0)

    order = inward(nz)
    mine = pltpu.make_async_copy(small, smalls.at[y, c, z], loc.at[ng + 1, 0])
    mine.start()
    line = remote(small, smalls.at[y, c, z], ts.at[0], tr.at[0], other_y)
    line.start()
    for t in order:
        for g in range(ng):
            across(g, t).start()
            own(g, t).start()
    mine.wait()
    remote(small, smalls.at[1 - y, c, z], ts.at[0], tr.at[0], other_y).wait_recv()
    for t in range(nz):

        @pl.when(z != t)
        def _(t=t):
            small_to(t).start()

    for t in order:
        for g in range(ng):
            side = (z > t).astype(jnp.int32)
            first = ((z == 0) & (z < t)) | ((z == nz - 1) & (z > t))

            @pl.when(first)
            def _(g=g, t=t, side=side):
                def clear(k, rows):
                    ins[g][side, t, k, rows] = jnp.zeros(
                        (rows_of(g), ins[g].shape[-1]), BF16
                    )

                each_tile(g, clear)

            own(g, t).wait()
            across(g, t).wait_recv()

            @pl.when((z < t) & (z > 0))
            def _(g=g, t=t):
                up(g, t).wait_recv()

            @pl.when((z > t) & (z < nz - 1))
            def _(g=g, t=t):
                down(g, t).wait_recv()

            @pl.when(z != t)
            def _(g=g, t=t, side=side):
                def add(k, rows):
                    sends[g][t, k, rows] = (
                        owns[g][t, k, rows].astype(F32)
                        + lands[g][t, k, rows].astype(F32)
                        + ins[g][side, t, k, rows].astype(F32)
                    ).astype(BF16)

                each_tile(g, add)

            @pl.when(z < t)
            def _(g=g, t=t):
                up(g, t).start()

            @pl.when(z > t)
            def _(g=g, t=t):
                down(g, t).start()

    for g in range(ng):

        @pl.when(z > 0)
        def _(g=g):
            up(g, z).wait_recv()

        @pl.when(z < nz - 1)
        def _(g=g):
            down(g, z).wait_recv()

        @pl.when(z == 0)
        def _(g=g):
            def clear(k, rows):
                ins[g][0, z, k, rows] = jnp.zeros((rows_of(g), ins[g].shape[-1]), BF16)

            each_tile(g, clear)

        @pl.when(z == nz - 1)
        def _(g=g):
            def clear(k, rows):
                ins[g][1, z, k, rows] = jnp.zeros((rows_of(g), ins[g].shape[-1]), BF16)

            each_tile(g, clear)

        def add(k, rows, g=g):
            totals[g][k, rows] = (
                owns[g][z, k, rows].astype(F32)
                + lands[g][z, k, rows].astype(F32)
                + ins[g][0, z, k, rows].astype(F32)
                + ins[g][1, z, k, rows].astype(F32)
            )

        each_tile(g, add)
        swap(g).start()
        keep(g).start()

    for t in range(nz):

        @pl.when(z != t)
        def _(t=t):
            small_from(t).wait_recv()

    plane = remote(smalls.at[:, c], smalls.at[:, c], ts.at[1], tr.at[1], other_c)
    plane.start()
    remote(smalls.at[:, 1 - c], smalls.at[:, 1 - c], ts.at[1], tr.at[1], other_c).wait_recv()
    for g in range(ng):
        swap_from(g).wait_recv()
        keep(g).wait()
        swap(g).wait_send()
    line.wait_send()
    plane.wait_send()
    for t in range(nz):

        @pl.when(z != t)
        def _(t=t):
            small_to(t).wait_send()

        for g in range(ng):
            across(g, t).wait_send()

            @pl.when(z < t)
            def _(g=g, t=t):
                up(g, t).wait_send()

            @pl.when(z > t)
            def _(g=g, t=t):
                down(g, t).wait_send()


def scatter_all(parts, small, ny, nz):
    ng = len(parts)
    dma = pltpu.SemaphoreType.DMA
    anywhere = pl.BlockSpec(memory_space=pl.ANY)
    shapes = [jax.ShapeDtypeStruct((2,) + part.shape[3:], F32) for part in parts]
    shapes.append(jax.ShapeDtypeStruct((ny, 2, nz) + small.shape, small.dtype))
    slots = [pltpu.VMEM((nz, 2) + part.shape[3:], BF16) for part in parts]
    results = pl.pallas_call(
        functools.partial(scatter_kernel, nz, ng),
        out_shape=shapes,
        in_specs=[anywhere] * (ng + 1),
        out_specs=[anywhere] * (ng + 1),
        scratch_shapes=slots * 2
        + [pltpu.VMEM((2, nz, 2) + part.shape[3:], BF16) for part in parts]
        + slots
        + [pltpu.VMEM((2,) + part.shape[3:], F32) for part in parts]
        + [
            dma((ng + 2, max(nz, ng))),
            dma((ng, nz)),
            dma((ng, nz)),
            dma((2, ng, nz)),
            dma((2, ng, nz)),
            dma((ng,)),
            dma((ng,)),
            dma((nz,)),
            dma((nz,)),
            dma((2,)),
            dma((2,)),
        ],
        name="scatter_all",
        compiler_params=pltpu.CompilerParams(
            collective_id=4, has_side_effects=True, vmem_limit_bytes=VMEM_LIMIT
        ),
    )(*parts, small)
    return results[:ng], results[ng]


def halves(matrix):
    half = matrix.shape[1] // 2
    return jnp.stack([matrix[:, :half], matrix[:, half:]])


def join(halved):
    return jnp.concatenate([halved[0], halved[1]], axis=1)


def on_device(
    ny,
    nz,
    layer_input,
    segments,
    positions,
    attn_gain,
    query_proj,
    key_proj,
    value_proj,
    out_proj,
    mlp_gain,
    gate_proj,
    up_proj,
    down_proj,
    out_grad,
):
    _, span, width = layer_input.shape
    block = query_proj.shape[0]
    groups = HQ // HK
    score_scale = DH ** (-0.5)
    y = lax.axis_index("fy")
    c = lax.axis_index("pr")
    z = lax.axis_index("ctx")
    rows_per = span // LANES
    small = jnp.concatenate(
        [
            jnp.pad(attn_gain.astype(F32), (0, LANES - block))[None],
            jnp.pad(mlp_gain.astype(F32), (0, LANES - block))[None],
            segments.astype(F32).reshape(rows_per, LANES),
            positions.astype(F32).reshape(rows_per, LANES),
            jnp.zeros((6 - 2 * rows_per, LANES), F32),
        ]
    )
    qkv_raw = jnp.concatenate([halves(query_proj), halves(key_proj), halves(value_proj)], axis=2)
    raws = (
        qkv_raw,
        halves(out_proj.T),
        halves(gate_proj),
        halves(up_proj),
        halves(down_proj.T),
    )
    layer_rows = layer_input.reshape(span, width)
    pieces, smalls, rows_both, grads_both = pair_swap(
        raws, small, layer_rows, out_grad.reshape(span, width), ny, nz
    )
    attn_gain_full = smalls[:, :, :, 0, :block].reshape(width)
    mlp_gain_full = smalls[:, :, :, 1, :block].reshape(width)
    mine = lax.dynamic_index_in_dim(smalls, y, 0, keepdims=False)
    segment_all = mine[:, :, 2 : 2 + rows_per].reshape(2, nz, 1, span).astype(jnp.int32)
    position_all = mine[:, :, 2 + rows_per : 2 + 2 * rows_per].reshape(2, nz, span)
    here = lax.dynamic_index_in_dim(position_all, z, 1, keepdims=False)
    segments_here = lax.dynamic_index_in_dim(segment_all, z, 1, keepdims=False)
    q_seg = jnp.tile(segments_here.reshape(2, span), (1, groups))[:, :, None]

    total_rows = 2 * span
    inputs = rows_both.reshape(total_rows, width).astype(F32)
    scale_attn = inverse_rms(inputs)
    normed_attn = (inputs * scale_attn * attn_gain_full).astype(BF16)
    cos_half, sin_half = rotary_tables(here.reshape(total_rows))
    blank = jnp.zeros((total_rows, LANES // 2 - DH // 2), F32)
    cos_wide = jnp.concatenate([cos_half, blank, cos_half, blank], axis=1)
    sin_wide = jnp.concatenate([-sin_half, blank, sin_half, blank], axis=1)
    lane_from = jnp.arange(4 * DH)
    lane_to = lane_from // DH * LANES + lane_from % DH
    lane_to = jnp.where(lane_from % DH < DH // 2, lane_to, lane_to + LANES // 2 - DH // 2)
    spread_mat = (lane_to[:, None] == jnp.arange(4 * LANES)[None]).astype(BF16)
    results = forward(
        pieces,
        normed_attn,
        layer_rows,
        cos_wide,
        sin_wide,
        q_seg,
        segment_all,
        spread_mat,
        mlp_gain_full.reshape(1, width),
        ny,
        nz,
    )
    qkv_full, out_full, gate_full, up_full, down_full = (
        piece.reshape(width, piece.shape[-1]) for piece in results[:5]
    )
    q_items, k_items, v_items, mixed_wide, mixed_rows, row_lse, residual_own, normed_mlp = results[5:]
    normed_mlp = normed_mlp.reshape(total_rows, width)
    gate_pre = jnp.dot(normed_mlp, gate_full, preferred_element_type=F32)
    up_pre = jnp.dot(normed_mlp, up_full, preferred_element_type=F32)
    activated = jax.nn.silu(gate_pre)
    hidden = (activated * up_pre).astype(BF16)

    def own_rows(both):
        return lax.dynamic_slice_in_dim(both.reshape(total_rows, width), c * span, span, 0)

    mlp_out = sum_parts(contract(hidden, down_full, 1, 1).reshape(2, span, width))
    layer_output = (residual_own + own_rows(mlp_out)).astype(BF16)

    upstream_low = grads_both.reshape(total_rows, width)
    hidden_grad = jnp.dot(upstream_low, down_full, preferred_element_type=F32)
    down_part = contract(upstream_low, hidden, 0, 0).astype(BF16)
    sigmoid_gate = jax.nn.sigmoid(gate_pre)
    gate_grad = (
        hidden_grad * up_pre * sigmoid_gate * (1.0 + gate_pre * (1.0 - sigmoid_gate))
    ).astype(BF16)
    up_grad = (hidden_grad * activated).astype(BF16)
    normed_mlp_grad = own_rows(
        sum_parts(
            (contract(gate_grad, gate_full, 1, 1) + contract(up_grad, up_full, 1, 1)).reshape(
                2, span, width
            )
        )
    )
    gate_part = contract(normed_mlp, gate_grad, 0, 0).astype(BF16)
    up_part = contract(normed_mlp, up_grad, 0, 0).astype(BF16)
    scale_mlp = inverse_rms(residual_own)
    mlp_gain_term = jnp.sum(normed_mlp_grad * residual_own * scale_mlp, axis=0)
    upstream = out_grad.reshape(span, width).astype(F32)
    residual_grad = norm_back(upstream, normed_mlp_grad * mlp_gain_full, residual_own, scale_mlp)
    residual_low = core_both(residual_grad.astype(BF16)).reshape(total_rows, width)
    out_part = contract(residual_low, mixed_rows, 0, 0).astype(BF16)
    mixed_grad = jnp.dot(residual_low, out_full, preferred_element_type=F32).astype(BF16)

    def to_items(rows):
        wide = jnp.dot(rows, spread_mat, preferred_element_type=F32).astype(BF16)
        return wide.reshape(2, span, 2, groups, LANES).transpose(0, 2, 3, 1, 4).reshape(
            4, groups * span, LANES
        )

    def narrow(wide):
        return contract(wide.astype(BF16), spread_mat, 1, 1)

    grad_items = to_items(mixed_grad)
    reached = (jnp.arange(nz) <= z)[:, None, None, None]
    k_all = jnp.where(reached, k_items, jnp.zeros_like(k_items)).transpose(1, 0, 2, 3).reshape(
        4, nz * span, LANES
    )
    v_all = jnp.where(reached, v_items, jnp.zeros_like(v_items)).transpose(1, 0, 2, 3).reshape(
        4, nz * span, LANES
    )
    query_index = jnp.tile(z * span + jnp.arange(span), groups)
    key_index = jnp.arange(nz * span)
    key_segments = jnp.repeat(segment_all.reshape(2, nz * span), 2, axis=0)
    query_segments = jnp.repeat(q_seg[:, :, 0], 2, axis=0)

    def backward_block(item):
        bq, bk, bv, ks, qs, blse, bg = item
        scores = jnp.einsum("qd,kd->qk", bq, bk, preferred_element_type=F32) * score_scale
        allowed = (qs[:, None] == ks[None, :]) & (query_index[:, None] >= key_index[None, :])
        probs = jnp.where(allowed, jnp.exp(scores - blse[:, :1]), 0.0)
        prob_grad = jnp.einsum("qd,kd->qk", bg, bv, preferred_element_type=F32)
        row_delta = jnp.sum(prob_grad * probs, axis=1, keepdims=True)
        score_grad = (probs * (prob_grad - row_delta)).astype(BF16)
        value_grad = jnp.einsum("qk,qd->kd", probs.astype(BF16), bg, preferred_element_type=F32)
        key_grad = jnp.einsum("qk,qd->kd", score_grad, bq, preferred_element_type=F32) * score_scale
        query_grad = jnp.dot(score_grad, bk, preferred_element_type=F32) * score_scale
        return (query_grad, key_grad, value_grad)

    query_grads, key_grads, value_grads = lax.map(
        backward_block, (q_items, k_all, v_all, key_segments, query_segments, row_lse, grad_items)
    )
    kv_wide = jnp.concatenate(
        [
            key_grads.reshape(2, 2, nz, span, LANES).transpose(2, 0, 3, 1, 4).reshape(nz * 2 * span, 2 * LANES),
            value_grads.reshape(2, 2, nz, span, LANES).transpose(2, 0, 3, 1, 4).reshape(nz * 2 * span, 2 * LANES),
        ],
        axis=1,
    )
    kv_back = keys_down(narrow(kv_wide).astype(BF16).reshape(nz, 2, span, 4 * DH), nz).reshape(
        total_rows, 4 * DH
    )
    kv_width = 2 * DH
    cos_t = cos_half[:, None, :]
    sin_t = sin_half[:, None, :]
    swapped = jnp.concatenate([query_grads[:, :, LANES // 2 :], query_grads[:, :, : LANES // 2]], axis=2)
    cos_i = jnp.repeat(jnp.tile(cos_wide.reshape(2, span, LANES), (1, groups, 1)), 2, axis=0)
    sin_i = jnp.repeat(jnp.tile(sin_wide.reshape(2, span, LANES), (1, groups, 1)), 2, axis=0)
    q_un = (query_grads * cos_i - swapped * sin_i).astype(BF16)
    q_un = q_un.reshape(2, 2, groups, span, LANES).transpose(0, 3, 1, 2, 4).reshape(total_rows, 4 * LANES)
    query_grad_rows = narrow(q_un).astype(BF16)
    key_grad_rows = (
        unrotate(kv_back[:, :kv_width].astype(F32).reshape(total_rows, 2, DH), cos_t, sin_t)
        .astype(BF16)
        .reshape(total_rows, -1)
    )
    qkv_grad_rows = jnp.concatenate([query_grad_rows, key_grad_rows, kv_back[:, kv_width:]], axis=1)
    qkv_part = contract(normed_attn, qkv_grad_rows, 0, 0).astype(BF16)
    normed_attn_grad = own_rows(
        sum_parts(contract(qkv_grad_rows, qkv_full, 1, 1).reshape(2, span, width))
    )
    inputs_own = layer_rows.astype(F32)
    scale_own = inverse_rms(inputs_own)
    attn_gain_term = jnp.sum(normed_attn_grad * inputs_own * scale_own, axis=0)
    input_grad = norm_back(
        residual_grad, normed_attn_grad * attn_gain_full, inputs_own, scale_own
    ).astype(BF16)

    parts = tuple(
        part.reshape(ny, 2, nz, block, part.shape[1])
        for part in (down_part, gate_part, up_part, out_part, qkv_part)
    )
    gains = jnp.stack([attn_gain_term, mlp_gain_term]).reshape(2 * width // LANES, LANES)
    reduced, gains_all = scatter_all(parts, gains, ny, nz)
    down_g, gate_g, up_g, out_g, qkv_g = reduced
    gain_sum = jnp.sum(gains_all, axis=(0, 1, 2)).reshape(2, width)
    place = ((y * 2 + c) * nz + z) * block
    gain_own = lax.dynamic_slice_in_dim(gain_sum, place, block, 1)
    q_width = 4 * DH
    return (
        layer_output.reshape(1, span, width),
        input_grad.reshape(1, span, width),
        gain_own[0],
        join(qkv_g[:, :, :q_width]),
        join(qkv_g[:, :, q_width : q_width + kv_width]),
        join(qkv_g[:, :, q_width + kv_width :]),
        join(out_g).T,
        gain_own[1],
        join(gate_g),
        join(up_g),
        join(down_g).T,
    )


def core_both(rows):
    def kernel(own, both, ss, rs, ls):
        c = lax.axis_index("pr")
        greet([({"pr": 1 - c}, None)], 1)
        local = pltpu.make_async_copy(own, both.at[c], ls.at[0])
        copy = remote(own, both.at[c], ss.at[0], rs.at[0], {"pr": 1 - c})
        local.start()
        copy.start()
        copy.wait()
        local.wait()

    dma = pltpu.SemaphoreType.DMA
    vmem = pl.BlockSpec(memory_space=pltpu.VMEM)
    return pl.pallas_call(
        kernel,
        out_shape=jax.ShapeDtypeStruct((2,) + rows.shape, rows.dtype),
        in_specs=[vmem],
        out_specs=vmem,
        scratch_shapes=[dma((1,)), dma((1,)), dma((1,))],
        name="core_both",
        compiler_params=pltpu.CompilerParams(collective_id=5, has_side_effects=True),
    )(rows)


def solution(mesh):
    sizes = mesh.shape
    ny, nz = sizes["fsdp"] // 2, sizes["ctx"]
    inner = Mesh(
        mesh.devices.reshape(ny, 2, nz, sizes["tp"]), ("fy", "pr", "ctx", "tp")
    )
    seqs = ("fy", "pr")
    rows = P(seqs, "ctx", None)
    marks = P(seqs, "ctx")
    gain = P(GROUP)
    tall = P(GROUP, "tp")
    wide = P("tp", GROUP)
    return jax.shard_map(
        functools.partial(on_device, ny, nz),
        mesh=inner,
        in_specs=(
            rows, marks, marks, gain, tall, tall, tall, wide, gain, tall, tall, wide, rows,
        ),
        out_specs=(rows, rows, gain, tall, tall, tall, wide, gain, tall, tall, wide),
        check_vma=False,
    )
```

```python
import functools

import jax
import jax.numpy as jnp
from jax import lax
from jax.experimental import pallas as pl
from jax.experimental.pallas import tpu as pltpu
from jax.sharding import Mesh, PartitionSpec as P

HQ = 16
HK = 8
DH = 96


EPS = 1e-05
THETA = 100000.0
NEGATIVE = -1e30


def rotary_tables(positions):
    half_dim = DH // 2
    freq_index = jnp.arange(half_dim, dtype=jnp.float32)
    inverse = THETA ** (-2.0 * freq_index / DH)
    angles = positions.astype(jnp.float32)[..., None] * inverse
    return (jnp.cos(angles), jnp.sin(angles))


def inverse_rms(values):
    return lax.rsqrt(jnp.mean(values * values, axis=-1, keepdims=True) + EPS)


def contract(left, right, left_dim, right_dim):
    return lax.dot_general(
        left, right, (((left_dim,), (right_dim,)), ((), ())), preferred_element_type=jnp.float32
    )


MESH_ID = pl.DeviceIdType.MESH
BF16 = jnp.bfloat16
F32 = jnp.float32
GROUP = ("fy", "pr", "ctx")
VMEM_LIMIT = 60 * 1024 * 1024
LANES = 128


def remote(src, dst, send_sem, recv_sem, device):
    return pltpu.make_async_remote_copy(
        src_ref=src,
        dst_ref=dst,
        send_sem=send_sem,
        recv_sem=recv_sem,
        device_id=device,
        device_id_type=MESH_ID,
    )


def greet(devices_and_conditions, count):
    barrier = pltpu.get_barrier_semaphore()
    for device, condition in devices_and_conditions:
        if condition is None:
            pl.semaphore_signal(barrier, inc=1, device_id=device, device_id_type=MESH_ID)
        else:

            @pl.when(condition)
            def _(device=device):
                pl.semaphore_signal(barrier, inc=1, device_id=device, device_id_type=MESH_ID)

    pl.semaphore_wait(barrier, count)


def dot(left, right, left_dim=1, right_dim=0):
    return lax.dot_general(
        left, right, (((left_dim,), (right_dim,)), ((), ())), preferred_element_type=F32
    )


def pair_kernel(nz, ng, *refs):
    raws = refs[:ng]
    small, rows_in, grad_in = refs[ng : ng + 3]
    pieces = refs[ng + 3 : 2 * ng + 3]
    smalls, rows_out, grad_out = refs[2 * ng + 3 : 2 * ng + 6]
    loc, cs, cr, zs, zr, ts, tr = refs[2 * ng + 6 :]
    y = lax.axis_index("fy")
    c = lax.axis_index("pr")
    z = lax.axis_index("ctx")
    other_y = {"fy": 1 - y}
    other_c = {"pr": 1 - c}
    greet(
        [(other_y, None), (other_c, None)] + [({"ctx": t}, z != t) for t in range(nz)], nz + 1
    )

    def small_to(t):
        return remote(small, smalls.at[y, c, z], zs.at[t], zr.at[z], {"ctx": t})

    def small_from(t):
        return remote(small, smalls.at[y, c, t], zs.at[t], zr.at[t], {"ctx": t})

    mine = pltpu.make_async_copy(small, smalls.at[y, c, z], loc.at[ng + 2])
    mine.start()
    for t in range(nz):

        @pl.when(z != t)
        def _(t=t):
            small_to(t).start()

    core = [remote(raws[g].at[1 - c], pieces[g].at[c], cs.at[g], cr.at[g], other_c) for g in range(ng)]
    local = [pltpu.make_async_copy(raws[g].at[c], pieces[g].at[c], loc.at[g]) for g in range(ng)]
    core.append(remote(rows_in, rows_out.at[c], cs.at[ng], cr.at[ng], other_c))
    core.append(remote(grad_in, grad_out.at[c], cs.at[ng + 1], cr.at[ng + 1], other_c))
    local.append(pltpu.make_async_copy(rows_in, rows_out.at[c], loc.at[ng]))
    local.append(pltpu.make_async_copy(grad_in, grad_out.at[c], loc.at[ng + 1]))
    for copy in core + local:
        copy.start()
    mine.wait()
    for t in range(nz):

        @pl.when(z != t)
        def _(t=t):
            small_from(t).wait_recv()

    line = remote(smalls.at[y, c], smalls.at[y, c], ts.at[0], tr.at[0], other_y)
    line.start()
    remote(smalls.at[1 - y, c], smalls.at[1 - y, c], ts.at[0], tr.at[0], other_y).wait_recv()
    plane = remote(smalls.at[:, c], smalls.at[:, c], ts.at[1], tr.at[1], other_c)
    plane.start()
    remote(smalls.at[:, 1 - c], smalls.at[:, 1 - c], ts.at[1], tr.at[1], other_c).wait_recv()
    for copy in core:
        copy.wait()
    for copy in local:
        copy.wait()
    line.wait_send()
    plane.wait_send()
    for t in range(nz):

        @pl.when(z != t)
        def _(t=t):
            small_to(t).wait_send()


def pair_swap(raws, small, rows, grads, ny, nz):
    ng = len(raws)
    dma = pltpu.SemaphoreType.DMA
    vmem = pl.BlockSpec(memory_space=pltpu.VMEM)
    shapes = [jax.ShapeDtypeStruct(raw.shape, raw.dtype) for raw in raws]
    shapes.append(jax.ShapeDtypeStruct((ny, 2, nz) + small.shape, small.dtype))
    shapes.append(jax.ShapeDtypeStruct((2,) + rows.shape, rows.dtype))
    shapes.append(jax.ShapeDtypeStruct((2,) + grads.shape, grads.dtype))
    results = pl.pallas_call(
        functools.partial(pair_kernel, nz, ng),
        out_shape=shapes,
        in_specs=[vmem] * (ng + 3),
        out_specs=[vmem] * (ng + 3),
        scratch_shapes=[
            dma((ng + 3,)),
            dma((ng + 2,)),
            dma((ng + 2,)),
            dma((nz,)),
            dma((nz,)),
            dma((2,)),
            dma((2,)),
        ],
        name="pair_swap",
        compiler_params=pltpu.CompilerParams(collective_id=0, has_side_effects=True),
    )(*raws, small, rows, grads)
    return results[:ng], results[ng], results[ng + 1], results[ng + 2]


class Gather:
    def __init__(self, nz, outs, us, ur, ds, dr, ys, yr, es, er):
        self.nz, self.outs = nz, outs
        self.sems = (us, ur, ds, dr, ys, yr, es, er)
        self.y = lax.axis_index("fy")
        self.z = lax.axis_index("ctx")
        self.odd = lax.rem(self.z, 2)
        self.pair = self.z + 1 - 2 * self.odd

    def up(self, g, s, slot):
        piece = self.outs[g].at[self.y, :, self.z - s]
        us, ur = self.sems[0], self.sems[1]
        return remote(piece, piece, us.at[g, slot], ur.at[g, slot], {"ctx": self.z + 1})

    def down(self, g, s, slot):
        piece = self.outs[g].at[self.y, :, self.z + s]
        ds, dr = self.sems[2], self.sems[3]
        return remote(piece, piece, ds.at[g, slot], dr.at[g, slot], {"ctx": self.z - 1})

    def across(self, g, slot, origin, half, row):
        piece = self.outs[g].at[row, 0, origin] if half else self.outs[g].at[row, :, origin]
        ys, yr = self.sems[4], self.sems[5]
        return remote(piece, piece, ys.at[g, slot], yr.at[g, slot], {"fy": 1 - self.y})

    def extra(self, g, origin):
        piece = self.outs[g].at[1 - self.y, 1, origin]
        es, er = self.sems[6], self.sems[7]
        return remote(piece, piece, es.at[g], er.at[g], {"ctx": self.pair})

    def own_z(self, g):
        @pl.when(self.z < self.nz - 1)
        def _():
            self.up(g, 0, 0).start()

        @pl.when(self.z > 0)
        def _():
            self.down(g, 0, 0).start()

    def own_y(self, g):
        self.across(g, 0, self.z, False, self.y).start()

    def each_across(self, g, s, row, act):
        z, nz = self.z, self.nz
        if s == 0:
            act(self.across(g, 0, z, False, row))
            return
        if s == 1:

            @pl.when(self.odd == 1)
            def _():
                act(self.across(g, 1, z - 1, True, row))

            @pl.when((self.odd == 0) & (z > 0))
            def _():
                act(self.across(g, 1, z - 1, False, row))

            @pl.when(self.odd == 0)
            def _():
                act(self.across(g, nz, z + 1, True, row))

            @pl.when((self.odd == 1) & (z < nz - 1))
            def _():
                act(self.across(g, nz, z + 1, False, row))

            return

        @pl.when(z >= s)
        def _():
            act(self.across(g, s, z - s, False, row))

        @pl.when(z + s < nz)
        def _():
            act(self.across(g, nz - 1 + s, z + s, False, row))

    def step(self, g, s):
        z, nz = self.z, self.nz

        @pl.when(z >= s)
        def _():
            self.up(g, s - 1 + 1, s - 1).wait_recv()

            @pl.when(z < nz - 1)
            def _():
                self.up(g, s, s).start()

        @pl.when(z + s < nz)
        def _():
            self.down(g, s, s - 1).wait_recv()

            @pl.when(z > 0)
            def _():
                self.down(g, s, s).start()

        self.each_across(g, s, self.y, lambda copy: copy.start())

    def spread(self, g):
        self.across(g, 0, self.z, False, 1 - self.y).wait_recv()
        self.extra(g, self.z).start()

    def finish(self, g):
        for s in range(1, self.nz):
            self.each_across(g, s, 1 - self.y, lambda copy: copy.wait_recv())
        self.extra(g, self.pair).wait_recv()

    def drain(self, g):
        z, nz = self.z, self.nz
        for s in range(nz):

            @pl.when((z >= s) & (z < nz - 1))
            def _(s=s):
                self.up(g, s, s).wait_send()

            @pl.when((z + s < nz) & (z > 0))
            def _(s=s):
                self.down(g, s, s).wait_send()

            self.each_across(g, s, self.y, lambda copy: copy.wait_send())
        self.extra(g, self.z).wait_send()


def forward_kernel(nz, items, scale, *refs):
    (normed, rows, cos, sin, q_seg, k_seg, spread_mat, gain) = refs[5:13]
    pieces = refs[:5]
    outs = refs[13:18]
    (q_out, k_out, v_out, mixed_out, mixed_low, lse_out, residual, normed_mlp) = refs[18:26]
    (acc, kvu, top, core_send, core_land, x_send, x_land, attended) = refs[26:34]
    loc, us, ur, ds, dr, ys, yr, es, er, ks, kr, cs, cr, xs, xr, ns, nr = refs[34:]
    y = lax.axis_index("fy")
    c = lax.axis_index("pr")
    z = lax.axis_index("ctx")
    x = lax.axis_index("tp")
    span = rows.shape[0]
    other_c = {"pr": 1 - c}
    other_x = {"tp": 1 - x}
    gather = Gather(nz, outs, us, ur, ds, dr, ys, yr, es, er)
    greet(
        [
            ({"fy": 1 - y}, None),
            (other_c, None),
            (other_x, None),
            ({"ctx": z + 1}, z < nz - 1),
            ({"ctx": z - 1}, z > 0),
        ],
        3 + (z < nz - 1).astype(jnp.int32) + (z > 0).astype(jnp.int32),
    )
    local = [pltpu.make_async_copy(pieces[g], outs[g].at[y, :, z], loc.at[g]) for g in range(5)]
    for copy in local:
        copy.start()
    early, late = (0, 1), (2, 3, 4)
    for g in early:
        local[g].wait()
        gather.own_z(g)
        gather.own_y(g)
    for g in late:
        local[g].wait()
    for s in range(1, nz):
        for g in early:
            gather.step(g, s)
        if s == 1:
            for g in early:
                gather.spread(g)
        if s == min(2, nz - 1):
            for g in late:
                gather.own_z(g)
    for g in late:
        gather.own_y(g)
    for g in early:
        gather.finish(g)

    chunk = nz * outs[0].shape[3]
    half = outs[0].shape[4] // 2
    for i in range(4):
        block = outs[0][i // 2, i % 2].reshape(chunk, 2 * half)
        wide = jnp.concatenate(
            [
                dot(block[:, :half], spread_mat[...]).astype(BF16),
                dot(block[:, half:], spread_mat[...]).astype(BF16),
            ],
            axis=1,
        )
        part = dot(normed[:, i * chunk : (i + 1) * chunk], wide)
        if i == 0:
            acc[...] = part
        else:
            acc[...] += part

    def rotated(b, lane):
        field = acc[pl.ds(b * span, span), pl.ds(lane * LANES, LANES)]
        turned = pltpu.roll(field, LANES // 2, 1)
        return (field * cos[pl.ds(b * span, span)] + turned * sin[pl.ds(b * span, span)]).astype(
            BF16
        )

    def keys_up(b, s):
        piece = kvu.at[z - s, b]
        return remote(piece, piece, ks.at[b, s], kr.at[b, s], {"ctx": z + 1})

    def keys_from(b, s):
        piece = kvu.at[z - s, b]
        return remote(piece, piece, ks.at[b, s - 1], kr.at[b, s - 1], {"ctx": z - 1})

    for b in range(2):
        fields = []
        for k in range(2):
            k_out[z, b * 2 + k] = rotated(b, 4 + k)
            fields.append(k_out[z, b * 2 + k])
        for k in range(2):
            v_out[z, b * 2 + k] = acc[
                pl.ds(b * span, span), pl.ds((6 + k) * LANES, LANES)
            ].astype(BF16)
            fields.append(v_out[z, b * 2 + k])
        kvu[z, b] = dot(jnp.concatenate(fields, axis=1), spread_mat[...], 1, 1).astype(BF16)

        @pl.when(z < nz - 1)
        def _(b=b):
            keys_up(b, 0).start()

    for b in range(2):
        for k in range(2):
            for j in range(2):
                q_out[b * 2 + k, pl.ds(j * span, span)] = rotated(b, 2 * k + j)

    def attend(block, first):
        def one(i, _):
            b = i // 2
            scores = dot(q_out[i], k_out[block, i], 1, 1) * scale
            allowed = q_seg[b] == k_seg[b, block]
            if first:
                row = lax.broadcasted_iota(jnp.int32, scores.shape, 0)
                column = lax.broadcasted_iota(jnp.int32, scores.shape, 1)
                allowed = allowed & (lax.rem(row, span) >= column)
            scores = jnp.where(allowed, scores, NEGATIVE)
            peak = jnp.max(scores, axis=1, keepdims=True)
            if first:
                probs = jnp.exp(scores - peak)
                total = jnp.sum(probs, axis=1, keepdims=True)
                mixed_out[i] = dot(probs.astype(BF16), v_out[block, i])
            else:
                old = top[i][:, :1]
                peak = jnp.maximum(old, peak)
                keep = jnp.exp(old - peak)
                probs = jnp.exp(scores - peak)
                total = keep * lse_out[i][:, :1] + jnp.sum(probs, axis=1, keepdims=True)
                mixed_out[i] = keep * mixed_out[i] + dot(probs.astype(BF16), v_out[block, i])
            top[i] = jnp.broadcast_to(peak, top.shape[1:])
            lse_out[i] = jnp.broadcast_to(total, lse_out.shape[1:])
            return 0

        lax.fori_loop(0, items, one, 0)

    attend(z, True)
    for g in late:
        gather.step(g, 1)
    for s in range(1, nz):

        @pl.when(z >= s)
        def _(s=s):
            for b in range(2):
                keys_from(b, s).wait_recv()

                @pl.when(z < nz - 1)
                def _(b=b):
                    keys_up(b, s).start()

                wide = dot(kvu[z - s, b], spread_mat[...]).astype(BF16)
                for k in range(2):
                    k_out[z - s, b * 2 + k] = wide[:, k * LANES : (k + 1) * LANES]
                    v_out[z - s, b * 2 + k] = wide[:, (2 + k) * LANES : (3 + k) * LANES]
            attend(z - s, False)

        if s == 1:
            for g in late:
                gather.spread(g)

    for i in range(items):
        total = lse_out[i]
        mixed_out[i] = mixed_out[i] / total
        lse_out[i] = top[i] + jnp.log(total)
    for b in range(2):
        heads = [
            mixed_out[b * 2 + k, pl.ds(j * span, span)].astype(BF16)
            for k in range(2)
            for j in range(2)
        ]
        mixed_low[pl.ds(b * span, span)] = dot(
            jnp.concatenate(heads, axis=1), spread_mat[...], 1, 1
        ).astype(BF16)
    for g in late:
        if nz > 2:
            gather.step(g, 2)

    def core(i):
        return remote(core_send.at[i], core_land.at[i], cs.at[i], cr.at[i], other_c)

    def sideways(i):
        return remote(x_send.at[i], x_land.at[i], xs.at[i], xr.at[i], other_x)

    def projected(who, i):
        weights = outs[1][i // 2, i % 2].reshape(chunk, half)
        return dot(mixed_low[pl.ds(pl.multiple_of(who * span, span), span)], weights, 1, 1)

    for i in range(4):
        core_send[i] = projected(1 - c, i).astype(BF16)
        core(i).start()
    for i in range(4):
        part = projected(c, i)
        core(i).wait_recv()
        x_send[i] = (part + core_land[i].astype(F32)).astype(BF16)
        sideways(i).start()
    for s in range(3, nz):
        for g in late:
            gather.step(g, s)
    squares = jnp.zeros((span, 1), F32)
    for i in range(4):
        sideways(i).wait_recv()
        column = pl.ds(i * chunk, chunk)
        total = rows[:, column].astype(F32) + (x_send[i].astype(F32) + x_land[i].astype(F32))
        residual[:, column] = total
        squares = squares + jnp.sum(total * total, axis=1, keepdims=True)
    factor = lax.rsqrt(squares / (4 * chunk) + EPS)
    normed_mlp[c] = (residual[...] * factor * gain[...]).astype(BF16)
    swap = remote(normed_mlp.at[c], normed_mlp.at[c], ns.at[0], nr.at[0], other_c)
    swap.start()
    remote(normed_mlp.at[1 - c], normed_mlp.at[1 - c], ns.at[0], nr.at[0], other_c).wait_recv()
    for g in late:
        gather.finish(g)
    for g in range(5):
        gather.drain(g)
    for b in range(2):
        for s in range(nz):

            @pl.when((z >= s) & (z < nz - 1))
            def _(b=b, s=s):
                keys_up(b, s).wait_send()

    for i in range(4):
        core(i).wait_send()
        sideways(i).wait_send()
    swap.wait_send()


def forward(pieces, normed, rows, cos, sin, q_seg, k_seg, spread_mat, gain, ny, nz):
    dma = pltpu.SemaphoreType.DMA
    vmem = pl.BlockSpec(memory_space=pltpu.VMEM)
    span, width = rows.shape
    items, q_rows = 4, 2 * span
    shape = jax.ShapeDtypeStruct
    chunk = width // 4
    out_shape = [shape((ny, 2, nz) + piece.shape[1:], BF16) for piece in pieces] + [
        shape((items, q_rows, LANES), BF16),
        shape((nz, items, span, LANES), BF16),
        shape((nz, items, span, LANES), BF16),
        shape((items, q_rows, LANES), F32),
        shape((2 * span, 4 * DH), BF16),
        shape((items, q_rows, LANES), F32),
        shape((span, width), F32),
        shape((2, span, width), BF16),
    ]
    return pl.pallas_call(
        functools.partial(forward_kernel, nz, items, DH ** (-0.5)),
        out_shape=out_shape,
        in_specs=[vmem] * 13,
        out_specs=[vmem] * len(out_shape),
        scratch_shapes=[
            pltpu.VMEM((2 * span, 8 * LANES), F32),
            pltpu.VMEM((nz, 2, span, 4 * DH), BF16),
            pltpu.VMEM((items, q_rows, LANES), F32),
        ]
        + [pltpu.VMEM((4, span, chunk), BF16)] * 4
        + [pltpu.VMEM((8, LANES), F32)]
        + [dma((5,))]
        + [dma((5, nz))] * 4
        + [dma((5, 2 * nz))] * 2
        + [dma((5,))] * 2
        + [dma((2, nz))] * 2
        + [dma((4,))] * 4
        + [dma((1,))] * 2,
        name="forward",
        compiler_params=pltpu.CompilerParams(
            collective_id=1, has_side_effects=True, vmem_limit_bytes=VMEM_LIMIT
        ),
    )(*pieces, normed, rows, cos, sin, q_seg, k_seg, spread_mat, gain)


def inward(nz):
    order = []
    for k in range((nz + 1) // 2):
        order.append(nz - 1 - k)
        if k != nz - 1 - k:
            order.append(k)
    return order


OWN = 3


class Scatter:
    def __init__(self, nz, sources, owns, lands, ins, overs, mids, extras, totals, outs, sems):
        self.nz, self.sources, self.owns, self.lands = nz, sources, owns, lands
        self.ins, self.overs, self.mids, self.extras = ins, overs, mids, extras
        self.totals, self.outs, self.sems = totals, outs, sems
        self.y = lax.axis_index("fy")
        self.c = lax.axis_index("pr")
        self.z = lax.axis_index("ctx")
        self.pair = self.z + 1 - 2 * lax.rem(self.z, 2)
        self.order = inward(nz)

    def own_copy(self, g, place):
        t = self.order[place] if place < self.nz else self.z
        return pltpu.make_async_copy(
            self.sources[g].at[self.y, :, t],
            self.owns[g].at[place % 2],
            self.sems[0].at[g, 3 + place % 2],
        )

    def own(self, g, place, k, rows):
        if self.owns[g] is None:
            t = self.order[place] if place < self.nz else self.z
            return self.sources[g][self.y, k, t, rows].astype(F32)
        return self.owns[g][place % 2, k, rows].astype(F32)

    def fetch(self, g, place):
        if self.owns[g] is not None and place <= self.nz:
            self.own_copy(g, place).start()

    def fetched(self, g, place):
        if self.owns[g] is not None:
            self.own_copy(g, place).wait()

    def middle(self, g):
        return pltpu.make_async_copy(
            self.sources[g].at[1 - self.y, 1, self.z], self.mids[g], self.sems[0].at[g, 1]
        )

    def across(self, g, t, part):
        ys, yr = self.sems[1], self.sems[2]
        src, dst = self.sources[g], self.lands[g]
        if part == "both":
            src, dst = src.at[1 - self.y, :, t], dst.at[t]
        else:
            src, dst = src.at[1 - self.y, 0, t], dst.at[t, 0]
        return remote(src, dst, ys.at[g, t], yr.at[g, t], {"fy": 1 - self.y})

    def relayed(self, g):
        ys, yr = self.sems[1], self.sems[2]
        return remote(
            self.mids[g],
            self.lands[g].at[self.z, 1],
            ys.at[g, self.nz],
            yr.at[g, self.nz],
            {"fy": 1 - self.y},
        )

    def extra(self, g):
        es, er = self.sems[3], self.sems[4]
        src = self.sources[g].at[1 - self.y, 1, self.pair]
        return remote(src, self.extras[g], es.at[g], er.at[g], {"ctx": self.pair})

    def up(self, g, t):
        zs, zr = self.sems[5], self.sems[6]
        return remote(
            self.lands[g].at[t], self.ins[g].at[t], zs.at[g, 0, t], zr.at[g, 0, t], {"ctx": self.z + 1}
        )

    def down(self, g, t):
        zs, zr = self.sems[5], self.sems[6]
        return remote(
            self.lands[g].at[t], self.ins[g].at[t], zs.at[g, 1, t], zr.at[g, 1, t], {"ctx": self.z - 1}
        )

    def down_home(self, g, t):
        zs, zr = self.sems[5], self.sems[6]
        return remote(
            self.lands[g].at[t], self.overs[g], zs.at[g, 1, t], zr.at[g, 1, t], {"ctx": self.z - 1}
        )

    def swap(self, g, slot):
        cs, cr = self.sems[7], self.sems[8]
        return remote(
            self.totals[g].at[1 - self.c], self.outs[g].at[slot], cs.at[g], cr.at[g], {"pr": 1 - self.c}
        )

    def keep(self, g):
        return pltpu.make_async_copy(
            self.totals[g].at[self.c], self.outs[g].at[self.c], self.sems[0].at[g, 2]
        )

    def each_tile(self, g, body):
        block = self.lands[g].shape[2]
        rows = 32 if block % 32 == 0 else block
        per = block // rows

        def step(i, _):
            body(i // per, pl.ds(pl.multiple_of(lax.rem(i, per) * rows, 8), rows))
            return 0

        lax.fori_loop(0, 2 * per, step, 0)

    def start(self, g):
        self.middle(g).start()
        self.extra(g).start()
        self.fetch(g, 0)
        self.fetch(g, 1)
        self.lands[g][self.pair, 1] = jnp.zeros(self.lands[g].shape[2:], BF16)
        for t in self.order:

            @pl.when((self.z != t) & (self.pair != t))
            def _(t=t):
                self.across(g, t, "both").start()

            @pl.when(self.pair == t)
            def _(t=t):
                self.across(g, t, "half").start()

        self.across(g, self.z, "half").start()

    def relay(self, g):
        self.middle(g).wait()
        self.extra(g).wait_recv()
        self.mids[g][...] = (
            self.mids[g][...].astype(F32) + self.extras[g][...].astype(F32)
        ).astype(BF16)
        self.relayed(g).start()

    def step(self, g, place):
        z, nz, t = self.z, self.nz, self.order[place]
        land, into = self.lands[g], self.ins[g]
        self.fetched(g, place)

        @pl.when(z != t)
        def _():
            @pl.when(self.pair != t)
            def _():
                self.across(g, t, "both").wait_recv()

            @pl.when(self.pair == t)
            def _():
                self.across(g, t, "half").wait_recv()

            inner = ((z < t) & (z > 0)) | ((z > t) & (z < nz - 1))

            @pl.when(inner)
            def _():
                @pl.when(z < t)
                def _():
                    self.up(g, t).wait_recv()

                @pl.when(z > t)
                def _():
                    self.down(g, t).wait_recv()

                def add(k, rows):
                    land[t, k, rows] = (
                        self.own(g, place, k, rows)
                        + land[t, k, rows].astype(F32)
                        + into[t, k, rows].astype(F32)
                    ).astype(BF16)

                self.each_tile(g, add)

            @pl.when(jnp.logical_not(inner))
            def _():
                def add(k, rows):
                    land[t, k, rows] = (
                        self.own(g, place, k, rows) + land[t, k, rows].astype(F32)
                    ).astype(BF16)

                self.each_tile(g, add)

            @pl.when(z < t)
            def _():
                self.up(g, t).start()

            @pl.when(z > t + 1)
            def _():
                self.down(g, t).start()

            @pl.when(z == t + 1)
            def _():
                self.down_home(g, t).start()

        self.fetch(g, place + 2)

    def last(self, g):
        z, nz = self.z, self.nz
        land, into, over = self.lands[g], self.ins[g], self.overs[g]
        self.fetched(g, nz)
        total = self.totals[g]
        self.across(g, z, "half").wait_recv()
        self.relayed(g).wait_recv()

        def base(k, rows):
            total[k, rows] = self.own(g, nz, k, rows) + land[z, k, rows].astype(F32)

        self.each_tile(g, base)

        @pl.when(z > 0)
        def _():
            self.up(g, z).wait_recv()

            def add(k, rows):
                total[k, rows] += into[z, k, rows].astype(F32)

            self.each_tile(g, add)

        @pl.when(z < nz - 1)
        def _():
            self.down_home(g, z).wait_recv()

            def add(k, rows):
                total[k, rows] += over[k, rows].astype(F32)

            self.each_tile(g, add)

        self.swap(g, self.c).start()
        self.keep(g).start()

    def finish(self, g):
        self.swap(g, 1 - self.c).wait_recv()
        self.swap(g, self.c).wait_send()
        self.keep(g).wait()
        self.extra(g).wait_send()
        self.relayed(g).wait_send()
        self.across(g, self.z, "half").wait_send()
        for t in self.order:

            @pl.when((self.z != t) & (self.pair != t))
            def _(t=t):
                self.across(g, t, "both").wait_send()

            @pl.when(self.pair == t)
            def _(t=t):
                self.across(g, t, "half").wait_send()

            @pl.when(self.z < t)
            def _(t=t):
                self.up(g, t).wait_send()

            @pl.when(self.z > t)
            def _(t=t):
                self.down(g, t).wait_send()


class TokenSum:
    def __init__(self, part, bufs, sems, n):
        self.part, self.n = part, n
        self.core_send, self.core_land, self.x_send, self.x_land = bufs
        self.cs, self.cr, self.xs, self.xr = sems
        self.c = lax.axis_index("pr")
        self.x = lax.axis_index("tp")

    def core(self, i):
        return remote(
            self.core_send.at[i],
            self.core_land.at[self.n % 2, i],
            self.cs.at[self.n, i],
            self.cr.at[self.n, i],
            {"pr": 1 - self.c},
        )

    def sideways(self, i):
        return remote(
            self.x_send.at[i],
            self.x_land.at[self.n % 2, i],
            self.xs.at[self.n, i],
            self.xr.at[self.n, i],
            {"tp": 1 - self.x},
        )

    def start(self):
        for i in range(4):
            self.core_send[i] = self.part(1 - self.c, i).astype(BF16)
            self.core(i).start()
        for i in range(4):
            mine = self.part(self.c, i).astype(F32)
            self.core(i).wait_recv()
            self.x_send[i] = (mine + self.core_land[self.n % 2, i].astype(F32)).astype(BF16)
            self.sideways(i).start()

    def arrived(self, i):
        self.sideways(i).wait_recv()

    def total(self, i):
        return self.x_send[i].astype(F32) + self.x_land[self.n % 2, i].astype(F32)

    def drain(self):
        for i in range(4):
            self.core(i).wait_send()
            self.sideways(i).wait_send()


def backward_kernel(nz, scale, *refs):
    sources = refs[:3]
    (
        dx_part, out_part, residual, rows, upstream, mlp_gain, attn_gain, cos, sin, q_seg, k_seg,
        spread_mat, q_items, k_items, v_items, mixed_wide, mixed_low, lse, w_qkv, w_out, normed,
    ) = refs[3:24]
    layer_out, input_grad = refs[24:26]
    outs = refs[26:31]
    gains = refs[31]
    scratch = refs[32:]
    owns = (*scratch[:OWN], None, None)
    lands, ins, overs, mids, extras, totals = (
        scratch[OWN + 5 * i : OWN + 5 * i + 5] for i in range(6)
    )
    (
        o_part, qkv_part, core_send, core_land, x_send, x_land, back_rows, low_rows, grad_items,
        delta, dq, kv_send, kv_land, qkv_rows, gain_rows, keys, values,
    ) = scratch[OWN + 30 : OWN + 47]
    (
        loc, ys, yr, es, er, zs, zr, ss, sr, cs, cr, xs, xr, ns, nr, ks, kr, gs, gr, ts, tr, bs,
    ) = scratch[OWN + 47 :]
    y = lax.axis_index("fy")
    c = lax.axis_index("pr")
    z = lax.axis_index("ctx")
    span, width = rows.shape
    chunk = width // 4
    half = 4 * DH
    sources = (*sources, o_part, qkv_part)
    scatter = Scatter(
        nz, sources, owns, lands, ins, overs, mids, extras, totals, outs,
        (loc, ys, yr, es, er, zs, zr, ss, sr),
    )
    greet(
        [
            ({"fy": 1 - y}, None),
            ({"pr": 1 - c}, None),
            ({"tp": 1 - lax.axis_index("tp")}, None),
        ]
        + [({"ctx": t}, z != t) for t in range(nz)],
        2 + nz,
    )
    bufs = (core_send, core_land, x_send, x_land)
    sems = (cs, cr, xs, xr)
    late = (0, 1, 2)

    def columns(i):
        return pl.ds(i * chunk, chunk)

    first = TokenSum(lambda who, i: dx_part[who, :, columns(i)], bufs, sems, 0)
    first.start()
    for g in late:
        scatter.start(g)

    squares = jnp.zeros((span, 1), F32)
    inner_sum = jnp.zeros((span, 1), F32)
    for i in range(4):
        first.arrived(i)
        grad = first.total(i)
        back_rows[:, columns(i)] = grad
        value = residual[:, columns(i)]
        squares = squares + jnp.sum(value * value, axis=1, keepdims=True)
        inner_sum = inner_sum + jnp.sum(grad * mlp_gain[:, columns(i)] * value, axis=1, keepdims=True)
    factor = lax.rsqrt(squares / width + EPS)
    slope = factor * factor * factor * (inner_sum / width)
    for i in range(4):
        grad = back_rows[:, columns(i)]
        value = residual[:, columns(i)]
        gain_rows[1:2, columns(i)] = jnp.sum(grad * value * factor, axis=0, keepdims=True)
        back = (
            upstream[:, columns(i)].astype(F32)
            + factor * (grad * mlp_gain[:, columns(i)])
            - value * slope
        )
        back_rows[:, columns(i)] = back
        low_rows[c, :, columns(i)] = back.astype(BF16)
    first.drain()
    swap = remote(low_rows.at[c], low_rows.at[c], ns.at[0], nr.at[0], {"pr": 1 - c})
    swap.start()
    for g in late:
        scatter.relay(g)
    remote(low_rows.at[1 - c], low_rows.at[1 - c], ns.at[0], nr.at[0], {"pr": 1 - c}).wait_recv()
    second = TokenSum(lambda who, i: out_part[who, :, columns(i)], bufs, sems, 1)
    second.start()

    for b in range(2):
        grads = jnp.zeros((span, half), F32)
        for i in range(4):
            weights = w_out[i // 2, i % 2].reshape(chunk, half)
            grads = grads + dot(low_rows[b, :, columns(i)], weights)
        wide = dot(grads.astype(BF16), spread_mat[...]).astype(BF16)
        for k in range(2):
            for j in range(2):
                head = 2 * k + j
                grad_items[b * 2 + k, pl.ds(j * span, span)] = wide[
                    :, head * LANES : (head + 1) * LANES
                ]
    for i in range(4):
        part = dot(low_rows[0, :, columns(i)], mixed_low[:span], 0, 0) + dot(
            low_rows[1, :, columns(i)], mixed_low[span:], 0, 0
        )
        o_part[i // 2, i % 2] = part.astype(BF16).reshape(o_part.shape[2:])
    for g in late:
        scatter.step(g, 0)
    scatter.start(3)

    for i in range(4):
        delta[i] = jnp.broadcast_to(
            jnp.sum(grad_items[i].astype(F32) * mixed_wide[i], axis=1, keepdims=True),
            delta.shape[1:],
        )

    slots = kv_send.shape[0]

    def keys_down(b, s):
        t = z - s
        return remote(
            kv_send.at[s % slots, b], kv_land.at[t, b], ks.at[b, t], kr.at[b, t], {"ctx": z - 1}
        )

    def keys_from(b, s):
        t = z - s
        return remote(
            kv_send.at[s % slots, b], kv_land.at[t, b], ks.at[b, t], kr.at[b, t], {"ctx": z - 1}
        )

    def load(s):
        return (
            pltpu.make_async_copy(k_items.at[z - s], keys.at[s % 2], bs.at[0, s % 2]),
            pltpu.make_async_copy(v_items.at[z - s], values.at[s % 2], bs.at[1, s % 2]),
        )

    def back_block(s, diagonal):
        block, slot = z - s, s % 2
        for copy in load(s):
            copy.wait()

        def one(b, _):
            key_grads, value_grads = [], []
            for k in range(2):
                item = b * 2 + k
                scores = dot(q_items[item], keys[slot, item], 1, 1) * scale
                allowed = q_seg[b] == k_seg[b, block]
                if diagonal:
                    row = lax.broadcasted_iota(jnp.int32, scores.shape, 0)
                    column = lax.broadcasted_iota(jnp.int32, scores.shape, 1)
                    allowed = allowed & (lax.rem(row, span) >= column)
                probs = jnp.where(allowed, jnp.exp(scores - lse[item][:, :1]), 0.0)
                prob_grad = dot(grad_items[item], values[slot, item], 1, 1)
                score_grad = (probs * (prob_grad - delta[item][:, :1])).astype(BF16)
                value_grads.append(dot(probs.astype(BF16), grad_items[item], 0, 0))
                key_grads.append(dot(score_grad, q_items[item], 0, 0) * scale)
                dq[item] += dot(score_grad, keys[slot, item]) * scale
            wide = jnp.concatenate(key_grads + value_grads, axis=1).astype(BF16)
            kv_send[s % slots, b] = dot(wide, spread_mat[...], 1, 1).astype(BF16)
            return 0

        lax.fori_loop(0, 2, one, 0)

    dq[...] = jnp.zeros_like(dq)
    for s in range(nz - 1, -1, -1):

        @pl.when(z == s)
        def _(s=s):
            for copy in load(s):
                copy.start()

    for s in range(nz - 1, 0, -1):

        @pl.when(z >= s)
        def _(s=s):
            for copy in load(s - 1):
                copy.start()
            if s + slots < nz:

                @pl.when(z >= s + slots)
                def _():
                    for b in range(2):
                        keys_down(b, s + slots).wait_send()

            back_block(s, False)
            for b in range(2):

                @pl.when(z < nz - 1)
                def _(b=b):
                    keys_from(b, s).wait_recv()
                    kv_send[s % slots, b] = (
                        kv_send[s % slots, b].astype(F32) + kv_land[z - s, b].astype(F32)
                    ).astype(BF16)

                keys_down(b, s).start()

        for g in late:
            scatter.step(g, nz - s)
    if slots < nz:

        @pl.when(z >= slots)
        def _():
            for b in range(2):
                keys_down(b, slots).wait_send()

    back_block(0, True)
    for i in range(4):
        second.arrived(i)
        layer_out[:, columns(i)] = (residual[:, columns(i)] + second.total(i)).astype(BF16)
    second.drain()

    def unrotated(field, b):
        turned = pltpu.roll(field, LANES // 2, 1)
        here = pl.ds(b * span, span)
        return (field * cos[here] - turned * sin[here]).astype(BF16)

    for b in range(2):
        heads = [
            unrotated(dq[b * 2 + k, pl.ds(j * span, span)], b) for k in range(2) for j in range(2)
        ]
        qkv_rows[b, :, :half] = dot(
            jnp.concatenate(heads, axis=1), spread_mat[...], 1, 1
        ).astype(BF16)
    for b in range(2):

        @pl.when(z < nz - 1)
        def _(b=b):
            keys_from(b, 0).wait_recv()
            kv_send[0, b] = (
                kv_send[0, b].astype(F32) + kv_land[z, b].astype(F32)
            ).astype(BF16)

        wide = dot(kv_send[0, b], spread_mat[...])
        fields = [unrotated(wide[:, k * LANES : (k + 1) * LANES], b) for k in range(2)]
        fields += [wide[:, (2 + k) * LANES : (3 + k) * LANES].astype(BF16) for k in range(2)]
        qkv_rows[b, :, half:] = dot(
            jnp.concatenate(fields, axis=1), spread_mat[...], 1, 1
        ).astype(BF16)
    for i in range(4):
        part = dot(normed[:span, columns(i)], qkv_rows[0], 0, 0) + dot(
            normed[span:, columns(i)], qkv_rows[1], 0, 0
        )
        qkv_part[i // 2, i % 2] = part.astype(BF16).reshape(qkv_part.shape[2:])
    scatter.start(4)

    def back_in(who, i):
        weights = w_qkv[i // 2, i % 2].reshape(chunk, 2 * half)
        return dot(qkv_rows[who], weights, 1, 1)

    third = TokenSum(back_in, bufs, sems, 2)
    third.start()
    scatter.relay(3)
    scatter.relay(4)
    for g in late:
        scatter.last(g)
    squares = jnp.zeros((span, 1), F32)
    inner_sum = jnp.zeros((span, 1), F32)
    for i in range(4):
        third.arrived(i)
        grad = third.total(i)
        value = rows[:, columns(i)].astype(F32)
        squares = squares + jnp.sum(value * value, axis=1, keepdims=True)
        inner_sum = inner_sum + jnp.sum(grad * attn_gain[:, columns(i)] * value, axis=1, keepdims=True)
    factor = lax.rsqrt(squares / width + EPS)
    slope = factor * factor * factor * (inner_sum / width)
    for i in range(4):
        value = rows[:, columns(i)].astype(F32)
        gain_rows[0:1, columns(i)] = jnp.sum(third.total(i) * value * factor, axis=0, keepdims=True)
        input_grad[:, columns(i)] = (
            back_rows[:, columns(i)]
            + factor * (third.total(i) * attn_gain[:, columns(i)])
            - value * slope
        ).astype(BF16)
    third.drain()

    mine = pltpu.make_async_copy(gain_rows, gains.at[y, c, z], ts.at[2])
    mine.start()
    mine.wait()
    core_gain = remote(gains.at[y, c, z], gains.at[y, c, z], ts.at[1], tr.at[1], {"pr": 1 - c})
    core_gain.start()
    remote(
        gains.at[y, 1 - c, z], gains.at[y, 1 - c, z], ts.at[1], tr.at[1], {"pr": 1 - c}
    ).wait_recv()

    def gain_to(t):
        return remote(gains.at[y, :, z], gains.at[y, :, z], gs.at[t], gr.at[z], {"ctx": t})

    def gain_from(t):
        return remote(gains.at[y, :, t], gains.at[y, :, t], gs.at[t], gr.at[t], {"ctx": t})

    for t in range(nz):

        @pl.when(z != t)
        def _(t=t):
            gain_to(t).start()

    for place in range(nz):
        scatter.step(3, place)
        scatter.step(4, place)
    for t in range(nz):

        @pl.when(z != t)
        def _(t=t):
            gain_from(t).wait_recv()

    gain_line = remote(gains.at[y], gains.at[y], ts.at[0], tr.at[0], {"fy": 1 - y})
    gain_line.start()
    scatter.last(3)
    scatter.last(4)
    remote(gains.at[1 - y], gains.at[1 - y], ts.at[0], tr.at[0], {"fy": 1 - y}).wait_recv()
    for g in range(5):
        scatter.finish(g)
    core_gain.wait_send()
    gain_line.wait_send()
    swap.wait_send()
    for t in range(nz):

        @pl.when(z != t)
        def _(t=t):
            gain_to(t).wait_send()

    for s in range(1, slots):

        @pl.when(z >= s)
        def _(s=s):
            for b in range(2):
                keys_down(b, s).wait_send()


def backward(parts, operands, ny, nz):
    dma = pltpu.SemaphoreType.DMA
    anywhere = pl.BlockSpec(memory_space=pl.ANY)
    vmem = pl.BlockSpec(memory_space=pltpu.VMEM)
    residual = operands[2]
    span, width = residual.shape
    chunk = width // 4
    block = parts[0].shape[3]
    half = 4 * DH
    wide = [part.shape[4] for part in parts] + [half, 2 * half]
    shape = jax.ShapeDtypeStruct
    out_shape = (
        [shape((span, width), BF16)] * 2
        + [shape((2, block, w), F32) for w in wide]
        + [shape((ny, 2, nz, 2, width), F32)]
    )

    def bufs(lead, dtype=BF16):
        return [pltpu.VMEM(lead + (block, w), dtype) for w in wide]

    return pl.pallas_call(
        functools.partial(backward_kernel, nz, DH ** (-0.5)),
        out_shape=out_shape,
        in_specs=[anywhere] * 3 + [vmem] * 13 + [anywhere] * 2 + [vmem] * 6,
        out_specs=[vmem] * 2 + [anywhere] * 6,
        scratch_shapes=bufs((2, 2))[:OWN]
        + bufs((nz, 2))
        + bufs((nz, 2))
        + bufs((2,))
        + bufs(())
        + bufs(())
        + bufs((2,), F32)
        + [
            pltpu.VMEM((ny, 2, nz, block, half), BF16),
            pltpu.VMEM((ny, 2, nz, block, 2 * half), BF16),
            pltpu.VMEM((4, span, chunk), BF16),
            pltpu.VMEM((2, 4, span, chunk), BF16),
            pltpu.VMEM((4, span, chunk), BF16),
            pltpu.VMEM((2, 4, span, chunk), BF16),
            pltpu.VMEM((span, width), F32),
            pltpu.VMEM((2, span, width), BF16),
            pltpu.VMEM((4, 2 * span, LANES), BF16),
            pltpu.VMEM((4, 2 * span, LANES), F32),
            pltpu.VMEM((4, 2 * span, LANES), F32),
            pltpu.VMEM((min(nz, 4), 2, span, half), BF16),
            pltpu.VMEM((nz, 2, span, half), BF16),
            pltpu.VMEM((2, span, 2 * half), BF16),
            pltpu.VMEM((2, width), F32),
            pltpu.VMEM((2, 4, span, LANES), BF16),
            pltpu.VMEM((2, 4, span, LANES), BF16),
        ]
        + [dma((5, 5))]
        + [dma((5, nz + 1))] * 2
        + [dma((5,))] * 2
        + [dma((5, 2, nz))] * 2
        + [dma((5,))] * 2
        + [dma((3, 4))] * 4
        + [dma((1,))] * 2
        + [dma((2, nz))] * 2
        + [dma((nz,))] * 2
        + [dma((3,)), dma((2,)), dma((2, 2))],
        name="backward",
        compiler_params=pltpu.CompilerParams(
            collective_id=2, has_side_effects=True, vmem_limit_bytes=VMEM_LIMIT
        ),
    )(*parts, *operands)


def halves(matrix):
    half = matrix.shape[1] // 2
    return jnp.stack([matrix[:, :half], matrix[:, half:]])


def join(halved):
    return jnp.concatenate([halved[0], halved[1]], axis=1)


def on_device(
    ny,
    nz,
    layer_input,
    segments,
    positions,
    attn_gain,
    query_proj,
    key_proj,
    value_proj,
    out_proj,
    mlp_gain,
    gate_proj,
    up_proj,
    down_proj,
    out_grad,
):
    _, span, width = layer_input.shape
    block = query_proj.shape[0]
    groups = HQ // HK
    y = lax.axis_index("fy")
    c = lax.axis_index("pr")
    z = lax.axis_index("ctx")
    rows_per = span // LANES
    small = jnp.concatenate(
        [
            jnp.pad(attn_gain.astype(F32), (0, LANES - block))[None],
            jnp.pad(mlp_gain.astype(F32), (0, LANES - block))[None],
            segments.astype(F32).reshape(rows_per, LANES),
            positions.astype(F32).reshape(rows_per, LANES),
            jnp.zeros((6 - 2 * rows_per, LANES), F32),
        ]
    )
    qkv_raw = jnp.concatenate([halves(query_proj), halves(key_proj), halves(value_proj)], axis=2)
    raws = (
        qkv_raw,
        halves(out_proj.T),
        halves(gate_proj),
        halves(up_proj),
        halves(down_proj.T),
    )
    layer_rows = layer_input.reshape(span, width)
    pieces, smalls, rows_both, grads_both = pair_swap(
        raws, small, layer_rows, out_grad.reshape(span, width), ny, nz
    )
    attn_gain_full = smalls[:, :, :, 0, :block].reshape(width)
    mlp_gain_full = smalls[:, :, :, 1, :block].reshape(width)
    mine = lax.dynamic_index_in_dim(smalls, y, 0, keepdims=False)
    segment_all = mine[:, :, 2 : 2 + rows_per].reshape(2, nz, 1, span).astype(jnp.int32)
    position_all = mine[:, :, 2 + rows_per : 2 + 2 * rows_per].reshape(2, nz, span)
    here = lax.dynamic_index_in_dim(position_all, z, 1, keepdims=False)
    segments_here = lax.dynamic_index_in_dim(segment_all, z, 1, keepdims=False)
    q_seg = jnp.tile(segments_here.reshape(2, span), (1, groups))[:, :, None]

    total_rows = 2 * span
    inputs = rows_both.reshape(total_rows, width).astype(F32)
    scale_attn = inverse_rms(inputs)
    normed_attn = (inputs * scale_attn * attn_gain_full).astype(BF16)
    cos_half, sin_half = rotary_tables(here.reshape(total_rows))
    blank = jnp.zeros((total_rows, LANES // 2 - DH // 2), F32)
    cos_wide = jnp.concatenate([cos_half, blank, cos_half, blank], axis=1)
    sin_wide = jnp.concatenate([-sin_half, blank, sin_half, blank], axis=1)
    lane_from = jnp.arange(4 * DH)
    lane_to = lane_from // DH * LANES + lane_from % DH
    lane_to = jnp.where(lane_from % DH < DH // 2, lane_to, lane_to + LANES // 2 - DH // 2)
    spread_mat = (lane_to[:, None] == jnp.arange(4 * LANES)[None]).astype(BF16)
    results = forward(
        pieces,
        normed_attn,
        layer_rows,
        cos_wide,
        sin_wide,
        q_seg,
        segment_all,
        spread_mat,
        mlp_gain_full.reshape(1, width),
        ny,
        nz,
    )
    gate_full, up_full, down_full = (
        piece.reshape(width, piece.shape[-1]) for piece in results[2:5]
    )
    q_items, k_items, v_items, mixed_wide, mixed_low, row_lse, residual_own, normed_mlp = results[5:]
    normed_mlp = normed_mlp.reshape(total_rows, width)
    gate_pre = jnp.dot(normed_mlp, gate_full, preferred_element_type=F32)
    up_pre = jnp.dot(normed_mlp, up_full, preferred_element_type=F32)
    activated = jax.nn.silu(gate_pre)
    hidden = (activated * up_pre).astype(BF16)

    out_part = contract(hidden, down_full, 1, 1).astype(BF16).reshape(2, span, width)
    upstream_low = grads_both.reshape(total_rows, width)
    hidden_grad = jnp.dot(upstream_low, down_full, preferred_element_type=F32)
    sigmoid_gate = jax.nn.sigmoid(gate_pre)
    gate_grad = (
        hidden_grad * up_pre * sigmoid_gate * (1.0 + gate_pre * (1.0 - sigmoid_gate))
    ).astype(BF16)
    up_grad = (hidden_grad * activated).astype(BF16)
    dx_part = (
        (contract(gate_grad, gate_full, 1, 1) + contract(up_grad, up_full, 1, 1))
        .astype(BF16)
        .reshape(2, span, width)
    )
    parts = [
        part.astype(BF16).reshape(ny, 2, nz, block, part.shape[1])
        for part in (
            contract(upstream_low, hidden, 0, 0),
            contract(normed_mlp, gate_grad, 0, 0),
            contract(normed_mlp, up_grad, 0, 0),
        )
    ]
    operands = (
        dx_part,
        out_part,
        residual_own,
        layer_rows,
        out_grad.reshape(span, width),
        mlp_gain_full.reshape(1, width),
        attn_gain_full.reshape(1, width),
        cos_wide,
        sin_wide,
        q_seg,
        segment_all,
        spread_mat,
        q_items,
        k_items,
        v_items,
        mixed_wide,
        mixed_low,
        row_lse,
        results[0],
        results[1],
        normed_attn,
    )
    layer_output, input_grad, down_g, gate_g, up_g, out_g, qkv_g, gains_all = backward(
        parts, operands, ny, nz
    )
    gain_sum = jnp.sum(gains_all, axis=(0, 1, 2))
    place = ((y * 2 + c) * nz + z) * block
    gain_own = lax.dynamic_slice_in_dim(gain_sum, place, block, 1)
    q_width, kv_width = 4 * DH, 2 * DH
    return (
        layer_output.reshape(1, span, width),
        input_grad.reshape(1, span, width),
        gain_own[0],
        join(qkv_g[:, :, :q_width]),
        join(qkv_g[:, :, q_width : q_width + kv_width]),
        join(qkv_g[:, :, q_width + kv_width :]),
        join(out_g).T,
        gain_own[1],
        join(gate_g),
        join(up_g),
        join(down_g).T,
    )


def solution(mesh):
    sizes = mesh.shape
    ny, nz = sizes["fsdp"] // 2, sizes["ctx"]
    inner = Mesh(
        mesh.devices.reshape(ny, 2, nz, sizes["tp"]), ("fy", "pr", "ctx", "tp")
    )
    seqs = ("fy", "pr")
    rows = P(seqs, "ctx", None)
    marks = P(seqs, "ctx")
    gain = P(GROUP)
    tall = P(GROUP, "tp")
    wide = P("tp", GROUP)
    return jax.shard_map(
        functools.partial(on_device, ny, nz),
        mesh=inner,
        in_specs=(
            rows, marks, marks, gain, tall, tall, tall, wide, gain, tall, tall, wide, rows,
        ),
        out_specs=(rows, rows, gain, tall, tall, tall, wide, gain, tall, tall, wide),
        check_vma=False,
    )
```

```python
import functools

import jax
import jax.numpy as jnp
from jax import lax
from jax.experimental import pallas as pl
from jax.experimental.pallas import tpu as pltpu
from jax.sharding import Mesh, PartitionSpec as P

HQ = 16
HK = 8
DH = 96


EPS = 1e-05
THETA = 100000.0
NEGATIVE = -1e30


def rotary_tables(positions):
    half_dim = DH // 2
    freq_index = jnp.arange(half_dim, dtype=jnp.float32)
    inverse = THETA ** (-2.0 * freq_index / DH)
    angles = positions.astype(jnp.float32)[..., None] * inverse
    return (jnp.cos(angles), jnp.sin(angles))


def inverse_rms(values):
    return lax.rsqrt(jnp.mean(values * values, axis=-1, keepdims=True) + EPS)


def contract(left, right, left_dim, right_dim):
    return lax.dot_general(
        left, right, (((left_dim,), (right_dim,)), ((), ())), preferred_element_type=jnp.float32
    )


MESH_ID = pl.DeviceIdType.MESH
BF16 = jnp.bfloat16
F32 = jnp.float32
GROUP = ("fy", "pr", "ctx")
VMEM_LIMIT = 60 * 1024 * 1024
LANES = 128


def remote(src, dst, send_sem, recv_sem, device):
    return pltpu.make_async_remote_copy(
        src_ref=src,
        dst_ref=dst,
        send_sem=send_sem,
        recv_sem=recv_sem,
        device_id=device,
        device_id_type=MESH_ID,
    )


def greet(devices_and_conditions, count):
    barrier = pltpu.get_barrier_semaphore()
    for device, condition in devices_and_conditions:
        if condition is None:
            pl.semaphore_signal(barrier, inc=1, device_id=device, device_id_type=MESH_ID)
        else:

            @pl.when(condition)
            def _(device=device):
                pl.semaphore_signal(barrier, inc=1, device_id=device, device_id_type=MESH_ID)

    pl.semaphore_wait(barrier, count)


def dot(left, right, left_dim=1, right_dim=0):
    return lax.dot_general(
        left, right, (((left_dim,), (right_dim,)), ((), ())), preferred_element_type=F32
    )


def pair_kernel(nz, ng, *refs):
    raws = refs[:ng]
    small, rows_in, grad_in = refs[ng : ng + 3]
    pieces = refs[ng + 3 : 2 * ng + 3]
    smalls, rows_out, grad_out = refs[2 * ng + 3 : 2 * ng + 6]
    loc, cs, cr, zs, zr, ts, tr = refs[2 * ng + 6 :]
    y = lax.axis_index("fy")
    c = lax.axis_index("pr")
    z = lax.axis_index("ctx")
    other_y = {"fy": 1 - y}
    other_c = {"pr": 1 - c}
    greet(
        [(other_y, None), (other_c, None)] + [({"ctx": t}, z != t) for t in range(nz)], nz + 1
    )

    def small_to(t):
        return remote(small, smalls.at[y, c, z], zs.at[t], zr.at[z], {"ctx": t})

    def small_from(t):
        return remote(small, smalls.at[y, c, t], zs.at[t], zr.at[t], {"ctx": t})

    mine = pltpu.make_async_copy(small, smalls.at[y, c, z], loc.at[ng + 2])
    mine.start()
    for t in range(nz):

        @pl.when(z != t)
        def _(t=t):
            small_to(t).start()

    core = [remote(raws[g].at[1 - c], pieces[g].at[c], cs.at[g], cr.at[g], other_c) for g in range(ng)]
    local = [pltpu.make_async_copy(raws[g].at[c], pieces[g].at[c], loc.at[g]) for g in range(ng)]
    core.append(remote(rows_in, rows_out.at[c], cs.at[ng], cr.at[ng], other_c))
    core.append(remote(grad_in, grad_out.at[c], cs.at[ng + 1], cr.at[ng + 1], other_c))
    local.append(pltpu.make_async_copy(rows_in, rows_out.at[c], loc.at[ng]))
    local.append(pltpu.make_async_copy(grad_in, grad_out.at[c], loc.at[ng + 1]))
    for copy in core + local:
        copy.start()
    mine.wait()
    for t in range(nz):

        @pl.when(z != t)
        def _(t=t):
            small_from(t).wait_recv()

    line = remote(smalls.at[y, c], smalls.at[y, c], ts.at[0], tr.at[0], other_y)
    line.start()
    remote(smalls.at[1 - y, c], smalls.at[1 - y, c], ts.at[0], tr.at[0], other_y).wait_recv()
    plane = remote(smalls.at[:, c], smalls.at[:, c], ts.at[1], tr.at[1], other_c)
    plane.start()
    remote(smalls.at[:, 1 - c], smalls.at[:, 1 - c], ts.at[1], tr.at[1], other_c).wait_recv()
    for copy in core:
        copy.wait()
    for copy in local:
        copy.wait()
    line.wait_send()
    plane.wait_send()
    for t in range(nz):

        @pl.when(z != t)
        def _(t=t):
            small_to(t).wait_send()


def pair_swap(raws, small, rows, grads, ny, nz):
    ng = len(raws)
    dma = pltpu.SemaphoreType.DMA
    vmem = pl.BlockSpec(memory_space=pltpu.VMEM)
    shapes = [jax.ShapeDtypeStruct(raw.shape, raw.dtype) for raw in raws]
    shapes.append(jax.ShapeDtypeStruct((ny, 2, nz) + small.shape, small.dtype))
    shapes.append(jax.ShapeDtypeStruct((2,) + rows.shape, rows.dtype))
    shapes.append(jax.ShapeDtypeStruct((2,) + grads.shape, grads.dtype))
    results = pl.pallas_call(
        functools.partial(pair_kernel, nz, ng),
        out_shape=shapes,
        in_specs=[vmem] * (ng + 3),
        out_specs=[vmem] * (ng + 3),
        scratch_shapes=[
            dma((ng + 3,)),
            dma((ng + 2,)),
            dma((ng + 2,)),
            dma((nz,)),
            dma((nz,)),
            dma((2,)),
            dma((2,)),
        ],
        name="pair_swap",
        compiler_params=pltpu.CompilerParams(collective_id=0, has_side_effects=True),
    )(*raws, small, rows, grads)
    return results[:ng], results[ng], results[ng + 1], results[ng + 2]


def low_bit(number):
    return (number & -number).bit_length() - 1


class Line:
    def __init__(self, nz):
        self.nz, self.levels = nz, nz.bit_length() - 1
        self.z = lax.axis_index("ctx")
        self.bits = [lax.rem(self.z // (1 << level), 2) for level in range(self.levels)]

    def at(self, offset):
        place = self.z
        for level in range(self.levels):
            if offset >> level & 1:
                place = place + (1 << level) - (2 << level) * self.bits[level]
        return place

    def partner(self, level):
        return self.at(1 << level)


class Gather:
    def __init__(self, line, outs, zs, zr, ys, yr, es, er):
        self.line, self.outs = line, outs
        self.zs, self.zr, self.ys, self.yr, self.es, self.er = zs, zr, ys, yr, es, er
        self.y = lax.axis_index("fy")
        offsets = range(1, line.nz)
        self.arrivals = sorted(offsets, key=lambda offset: (-low_bit(offset), offset))

    def hop(self, g, offset, level):
        piece = self.outs[g].at[self.y, :, self.line.at(offset)]
        slot = offset + (1 << level)
        return remote(
            piece, piece, self.zs.at[g, slot], self.zr.at[g, slot], {"ctx": self.line.partner(level)}
        )

    def hop_from(self, g, offset):
        piece = self.outs[g].at[self.y, :, self.line.at(offset)]
        partner = self.line.partner(low_bit(offset))
        return remote(piece, piece, self.zs.at[g, offset], self.zr.at[g, offset], {"ctx": partner})

    def across(self, g, offset, row):
        place = self.line.at(offset)
        piece = self.outs[g].at[row, 0, place] if offset == 1 else self.outs[g].at[row, :, place]
        return remote(
            piece, piece, self.ys.at[g, offset], self.yr.at[g, offset], {"fy": 1 - self.y}
        )

    def extra(self, g, offset):
        piece = self.outs[g].at[1 - self.y, 1, self.line.at(offset)]
        return remote(piece, piece, self.es.at[g], self.er.at[g], {"ctx": self.line.partner(0)})

    def hops(self, offset):
        last = low_bit(offset) if offset else self.line.levels
        return reversed(range(last))

    def own_z(self, g):
        for level in self.hops(0):
            self.hop(g, 0, level).start()

    def own_y(self, g):
        self.across(g, 0, self.y).start()

    def step(self, g, offset):
        self.hop_from(g, offset).wait_recv()
        for level in self.hops(offset):
            self.hop(g, offset, level).start()
        self.across(g, offset, self.y).start()

    def spread(self, g):
        self.across(g, 0, 1 - self.y).wait_recv()
        self.extra(g, 0).start()

    def finish(self, g):
        for offset in self.arrivals:
            self.across(g, offset, 1 - self.y).wait_recv()
        self.extra(g, 1).wait_recv()

    def drain(self, g):
        for offset in (0, *self.arrivals):
            for level in self.hops(offset):
                self.hop(g, offset, level).wait_send()
            self.across(g, offset, self.y).wait_send()
        self.extra(g, 0).wait_send()


def forward_kernel(nz, items, scale, *refs):
    (normed, rows, cos, sin, q_seg, k_seg, spread_mat, gain) = refs[5:13]
    pieces = refs[:5]
    outs = refs[13:18]
    (q_out, k_out, v_out, mixed_out, mixed_low, lse_out, residual, normed_mlp) = refs[18:26]
    (acc, kvu, top, core_send, core_land, x_send, x_land) = refs[26:33]
    loc, zs, zr, ys, yr, es, er, ks, kr, cs, cr, xs, xr, ns, nr = refs[33:]
    y = lax.axis_index("fy")
    c = lax.axis_index("pr")
    z = lax.axis_index("ctx")
    x = lax.axis_index("tp")
    span = rows.shape[0]
    other_c = {"pr": 1 - c}
    other_x = {"tp": 1 - x}
    line = Line(nz)
    gather = Gather(line, outs, zs, zr, ys, yr, es, er)
    greet(
        [({"fy": 1 - y}, None), (other_c, None), (other_x, None)]
        + [({"ctx": line.partner(level)}, None) for level in range(line.levels)],
        3 + line.levels,
    )
    local = [pltpu.make_async_copy(pieces[g], outs[g].at[y, :, z], loc.at[g]) for g in range(5)]
    for copy in local:
        copy.start()
    early, late = (0, 1), (2, 3, 4)
    for g in early:
        local[g].wait()
        gather.own_z(g)
        gather.own_y(g)
    for g in late:
        local[g].wait()
    gather.own_y(2)
    for offset in gather.arrivals:
        for g in early:
            gather.step(g, offset)
        if offset == gather.arrivals[0]:
            for g in early:
                gather.spread(g)
    for g in late:
        gather.own_z(g)
    for g in late[1:]:
        gather.own_y(g)
    for g in early:
        gather.finish(g)

    chunk = nz * outs[0].shape[3]
    half = outs[0].shape[4] // 2
    for i in range(4):
        block = outs[0][i // 2, i % 2].reshape(chunk, 2 * half)
        wide = jnp.concatenate(
            [
                dot(block[:, :half], spread_mat[...]).astype(BF16),
                dot(block[:, half:], spread_mat[...]).astype(BF16),
            ],
            axis=1,
        )
        part = dot(normed[:, i * chunk : (i + 1) * chunk], wide)
        if i == 0:
            acc[...] = part
        else:
            acc[...] += part

    def rotated(b, lane):
        field = acc[pl.ds(b * span, span), pl.ds(lane * LANES, LANES)]
        turned = pltpu.roll(field, LANES // 2, 1)
        return (field * cos[pl.ds(b * span, span)] + turned * sin[pl.ds(b * span, span)]).astype(
            BF16
        )

    def keys_hop(b, offset, level):
        piece = kvu.at[line.at(offset), b]
        slot = offset + (1 << level)
        return remote(
            piece, piece, ks.at[b, slot], kr.at[b, slot], {"ctx": line.partner(level)}
        )

    def keys_from(b, offset):
        piece = kvu.at[line.at(offset), b]
        partner = line.partner(low_bit(offset))
        return remote(piece, piece, ks.at[b, offset], kr.at[b, offset], {"ctx": partner})

    def each_hop(offset, act):
        for level in gather.hops(offset):

            @pl.when(line.at(offset) <= line.partner(level))
            def _(level=level):
                act(level)

    for b in range(2):
        fields = []
        for k in range(2):
            k_out[z, b * 2 + k] = rotated(b, 4 + k)
            fields.append(k_out[z, b * 2 + k])
        for k in range(2):
            v_out[z, b * 2 + k] = acc[
                pl.ds(b * span, span), pl.ds((6 + k) * LANES, LANES)
            ].astype(BF16)
            fields.append(v_out[z, b * 2 + k])
        kvu[z, b] = dot(jnp.concatenate(fields, axis=1), spread_mat[...], 1, 1).astype(BF16)
        each_hop(0, lambda level, b=b: keys_hop(b, 0, level).start())

    for b in range(2):
        for k in range(2):
            for j in range(2):
                q_out[b * 2 + k, pl.ds(j * span, span)] = rotated(b, 2 * k + j)

    def attend(block, first):
        def one(i, _):
            b = i // 2
            scores = dot(q_out[i], k_out[block, i], 1, 1) * scale
            allowed = q_seg[b] == k_seg[b, block]
            if first:
                row = lax.broadcasted_iota(jnp.int32, scores.shape, 0)
                column = lax.broadcasted_iota(jnp.int32, scores.shape, 1)
                allowed = allowed & (lax.rem(row, span) >= column)
            scores = jnp.where(allowed, scores, NEGATIVE)
            peak = jnp.max(scores, axis=1, keepdims=True)
            if first:
                probs = jnp.exp(scores - peak)
                total = jnp.sum(probs, axis=1, keepdims=True)
                mixed_out[i] = dot(probs.astype(BF16), v_out[block, i])
            else:
                old = top[i][:, :1]
                peak = jnp.maximum(old, peak)
                keep = jnp.exp(old - peak)
                probs = jnp.exp(scores - peak)
                total = keep * lse_out[i][:, :1] + jnp.sum(probs, axis=1, keepdims=True)
                mixed_out[i] = keep * mixed_out[i] + dot(probs.astype(BF16), v_out[block, i])
            top[i] = jnp.broadcast_to(peak, top.shape[1:])
            lse_out[i] = jnp.broadcast_to(total, lse_out.shape[1:])
            return 0

        lax.fori_loop(0, items, one, 0)

    attend(z, True)
    for place, offset in enumerate(gather.arrivals):
        from_there = line.at(offset)

        @pl.when(from_there <= z)
        def _(offset=offset, from_there=from_there):
            for b in range(2):
                keys_from(b, offset).wait_recv()
                each_hop(offset, lambda level, b=b: keys_hop(b, offset, level).start())
                wide = dot(kvu[from_there, b], spread_mat[...]).astype(BF16)
                for k in range(2):
                    k_out[from_there, b * 2 + k] = wide[:, k * LANES : (k + 1) * LANES]
                    v_out[from_there, b * 2 + k] = wide[:, (2 + k) * LANES : (3 + k) * LANES]
            attend(from_there, False)

        if place == 0:
            for g in late:
                gather.step(g, offset)

    for i in range(items):
        total = lse_out[i]
        mixed_out[i] = mixed_out[i] / total
        lse_out[i] = top[i] + jnp.log(total)
    for b in range(2):
        heads = [
            mixed_out[b * 2 + k, pl.ds(j * span, span)].astype(BF16)
            for k in range(2)
            for j in range(2)
        ]
        mixed_low[pl.ds(b * span, span)] = dot(
            jnp.concatenate(heads, axis=1), spread_mat[...], 1, 1
        ).astype(BF16)
    for g in late:
        gather.spread(g)

    def core(i):
        return remote(core_send.at[i], core_land.at[i], cs.at[i], cr.at[i], other_c)

    def sideways(i):
        return remote(x_send.at[i], x_land.at[i], xs.at[i], xr.at[i], other_x)

    def projected(who, i):
        weights = outs[1][i // 2, i % 2].reshape(chunk, half)
        return dot(mixed_low[pl.ds(pl.multiple_of(who * span, span), span)], weights, 1, 1)

    for i in range(4):
        core_send[i] = projected(1 - c, i).astype(BF16)
        core(i).start()
    for i in range(4):
        part = projected(c, i)
        core(i).wait_recv()
        x_send[i] = (part + core_land[i].astype(F32)).astype(BF16)
        sideways(i).start()
    for offset in gather.arrivals[1:]:
        for g in late:
            gather.step(g, offset)
    squares = jnp.zeros((span, 1), F32)
    for i in range(4):
        sideways(i).wait_recv()
        column = pl.ds(i * chunk, chunk)
        total = rows[:, column].astype(F32) + (x_send[i].astype(F32) + x_land[i].astype(F32))
        residual[:, column] = total
        squares = squares + jnp.sum(total * total, axis=1, keepdims=True)
    factor = lax.rsqrt(squares / (4 * chunk) + EPS)
    normed_mlp[c] = (residual[...] * factor * gain[...]).astype(BF16)
    swap = remote(normed_mlp.at[c], normed_mlp.at[c], ns.at[0], nr.at[0], other_c)
    swap.start()
    remote(normed_mlp.at[1 - c], normed_mlp.at[1 - c], ns.at[0], nr.at[0], other_c).wait_recv()
    for g in late:
        gather.finish(g)
    for g in range(5):
        gather.drain(g)
    for b in range(2):
        each_hop(0, lambda level, b=b: keys_hop(b, 0, level).wait_send())
        for offset in gather.arrivals:

            @pl.when(line.at(offset) <= z)
            def _(b=b, offset=offset):
                each_hop(offset, lambda level: keys_hop(b, offset, level).wait_send())

    for i in range(4):
        core(i).wait_send()
        sideways(i).wait_send()
    swap.wait_send()


def forward(pieces, normed, rows, cos, sin, q_seg, k_seg, spread_mat, gain, ny, nz):
    dma = pltpu.SemaphoreType.DMA
    vmem = pl.BlockSpec(memory_space=pltpu.VMEM)
    span, width = rows.shape
    items, q_rows = 4, 2 * span
    shape = jax.ShapeDtypeStruct
    chunk = width // 4
    out_shape = [shape((ny, 2, nz) + piece.shape[1:], BF16) for piece in pieces] + [
        shape((items, q_rows, LANES), BF16),
        shape((nz, items, span, LANES), BF16),
        shape((nz, items, span, LANES), BF16),
        shape((items, q_rows, LANES), F32),
        shape((2 * span, 4 * DH), BF16),
        shape((items, q_rows, LANES), F32),
        shape((span, width), F32),
        shape((2, span, width), BF16),
    ]
    return pl.pallas_call(
        functools.partial(forward_kernel, nz, items, DH ** (-0.5)),
        out_shape=out_shape,
        in_specs=[vmem] * 13,
        out_specs=[vmem] * len(out_shape),
        scratch_shapes=[
            pltpu.VMEM((2 * span, 8 * LANES), F32),
            pltpu.VMEM((nz, 2, span, 4 * DH), BF16),
            pltpu.VMEM((items, q_rows, LANES), F32),
        ]
        + [pltpu.VMEM((4, span, chunk), BF16)] * 4
        + [dma((5,))]
        + [dma((5, nz))] * 4
        + [dma((5,))] * 2
        + [dma((2, nz))] * 2
        + [dma((4,))] * 4
        + [dma((1,))] * 2,
        name="forward",
        compiler_params=pltpu.CompilerParams(
            collective_id=1, has_side_effects=True, vmem_limit_bytes=VMEM_LIMIT
        ),
    )(*pieces, normed, rows, cos, sin, q_seg, k_seg, spread_mat, gain)


OWN = 3


class Scatter:
    def __init__(self, line, sources, owns, lands, ins, mids, extras, totals, outs, sems):
        self.line, self.sources, self.owns, self.lands = line, sources, owns, lands
        self.ins, self.mids, self.extras = ins, mids, extras
        self.totals, self.outs, self.sems = totals, outs, sems
        self.y = lax.axis_index("fy")
        self.c = lax.axis_index("pr")
        nz = line.nz
        self.order = sorted(range(1, nz), key=lambda offset: (low_bit(offset), -offset)) + [0]

    def own_copy(self, g, place):
        return pltpu.make_async_copy(
            self.sources[g].at[self.y, :, self.line.at(self.order[place])],
            self.owns[g].at[place % 2],
            self.sems[0].at[g, 3 + place % 2],
        )

    def own(self, g, place, k, rows):
        if self.owns[g] is None:
            place_at = self.line.at(self.order[place])
            return self.sources[g][self.y, k, place_at, rows].astype(F32)
        return self.owns[g][place % 2, k, rows].astype(F32)

    def fetch(self, g, place):
        if self.owns[g] is not None and place < self.line.nz:
            self.own_copy(g, place).start()

    def fetched(self, g, place):
        if self.owns[g] is not None:
            self.own_copy(g, place).wait()

    def middle(self, g):
        return pltpu.make_async_copy(
            self.sources[g].at[1 - self.y, 1, self.line.z], self.mids[g], self.sems[0].at[g, 1]
        )

    def across(self, g, offset):
        ys, yr = self.sems[1], self.sems[2]
        src, dst, place = self.sources[g], self.lands[g], self.line.at(offset)
        if offset > 1:
            src, dst = src.at[1 - self.y, :, place], dst.at[offset]
        else:
            src, dst = src.at[1 - self.y, 0, place], dst.at[offset, 0]
        return remote(src, dst, ys.at[g, offset], yr.at[g, offset], {"fy": 1 - self.y})

    def relayed(self, g):
        ys, yr = self.sems[1], self.sems[2]
        slot = self.line.nz
        return remote(
            self.mids[g], self.lands[g].at[0, 1], ys.at[g, slot], yr.at[g, slot], {"fy": 1 - self.y}
        )

    def extra(self, g):
        es, er = self.sems[3], self.sems[4]
        src = self.sources[g].at[1 - self.y, 1, self.line.at(1)]
        return remote(src, self.extras[g], es.at[g], er.at[g], {"ctx": self.line.partner(0)})

    def hop(self, g, offset):
        zs, zr = self.sems[5], self.sems[6]
        return remote(
            self.lands[g].at[offset],
            self.ins[g].at[offset - 1],
            zs.at[g, offset],
            zr.at[g, offset],
            {"ctx": self.line.partner(low_bit(offset))},
        )

    def swap(self, g, slot):
        cs, cr = self.sems[7], self.sems[8]
        return remote(
            self.totals[g].at[1 - self.c], self.outs[g].at[slot], cs.at[g], cr.at[g], {"pr": 1 - self.c}
        )

    def keep(self, g):
        return pltpu.make_async_copy(
            self.totals[g].at[self.c], self.outs[g].at[self.c], self.sems[0].at[g, 2]
        )

    def each_tile(self, g, body):
        block = self.lands[g].shape[2]
        rows = 32 if block % 32 == 0 else block
        per = block // rows

        def step(i, _):
            body(i // per, pl.ds(pl.multiple_of(lax.rem(i, per) * rows, 8), rows))
            return 0

        lax.fori_loop(0, 2 * per, step, 0)

    def start(self, g):
        self.middle(g).start()
        self.extra(g).start()
        self.fetch(g, 0)
        self.fetch(g, 1)
        self.lands[g][1, 1] = jnp.zeros(self.lands[g].shape[2:], BF16)
        for offset in self.order:
            self.across(g, offset).start()

    def relay(self, g):
        self.middle(g).wait()
        self.extra(g).wait_recv()
        self.mids[g][...] = (
            self.mids[g][...].astype(F32) + self.extras[g][...].astype(F32)
        ).astype(BF16)
        self.relayed(g).start()

    def step(self, g, place):
        offset = self.order[place]
        land, into = self.lands[g], self.ins[g]
        self.fetched(g, place)
        self.across(g, offset).wait_recv()
        arrived = [offset ^ (1 << level) for level in range(low_bit(offset))]
        for other in arrived:
            self.hop(g, other).wait_recv()

        def add(k, rows):
            total = self.own(g, place, k, rows) + land[offset, k, rows].astype(F32)
            for other in arrived:
                total = total + into[other - 1, k, rows].astype(F32)
            land[offset, k, rows] = total.astype(BF16)

        self.each_tile(g, add)
        self.hop(g, offset).start()
        self.fetch(g, place + 2)

    def last(self, g):
        place = self.line.nz - 1
        land, into = self.lands[g], self.ins[g]
        total = self.totals[g]
        self.fetched(g, place)
        self.across(g, 0).wait_recv()
        self.relayed(g).wait_recv()
        arrived = [1 << level for level in range(self.line.levels)]
        for other in arrived:
            self.hop(g, other).wait_recv()

        def add(k, rows):
            value = self.own(g, place, k, rows) + land[0, k, rows].astype(F32)
            for other in arrived:
                value = value + into[other - 1, k, rows].astype(F32)
            total[k, rows] = value

        self.each_tile(g, add)
        self.swap(g, self.c).start()
        self.keep(g).start()

    def finish(self, g):
        self.swap(g, 1 - self.c).wait_recv()
        self.swap(g, self.c).wait_send()
        self.keep(g).wait()
        self.extra(g).wait_send()
        self.relayed(g).wait_send()
        for offset in self.order:
            self.across(g, offset).wait_send()
            if offset:
                self.hop(g, offset).wait_send()


class TokenSum:
    def __init__(self, part, bufs, sems, n):
        self.part, self.n = part, n
        self.core_send, self.core_land, self.x_send, self.x_land = bufs
        self.cs, self.cr, self.xs, self.xr = sems
        self.c = lax.axis_index("pr")
        self.x = lax.axis_index("tp")

    def core(self, i):
        return remote(
            self.core_send.at[i],
            self.core_land.at[self.n % 2, i],
            self.cs.at[self.n, i],
            self.cr.at[self.n, i],
            {"pr": 1 - self.c},
        )

    def sideways(self, i):
        return remote(
            self.x_send.at[i],
            self.x_land.at[self.n % 2, i],
            self.xs.at[self.n, i],
            self.xr.at[self.n, i],
            {"tp": 1 - self.x},
        )

    def start(self):
        for i in range(4):
            self.core_send[i] = self.part(1 - self.c, i).astype(BF16)
            self.core(i).start()
        for i in range(4):
            mine = self.part(self.c, i).astype(F32)
            self.core(i).wait_recv()
            self.x_send[i] = (mine + self.core_land[self.n % 2, i].astype(F32)).astype(BF16)
            self.sideways(i).start()

    def arrived(self, i):
        self.sideways(i).wait_recv()

    def total(self, i):
        return self.x_send[i].astype(F32) + self.x_land[self.n % 2, i].astype(F32)

    def drain(self):
        for i in range(4):
            self.core(i).wait_send()
            self.sideways(i).wait_send()


def backward_kernel(nz, scale, *refs):
    sources = refs[:3]
    (
        dx_part, out_part, residual, rows, upstream, mlp_gain, attn_gain, cos, sin, q_seg, k_seg,
        spread_mat, q_items, k_items, v_items, mixed_wide, mixed_low, lse, w_qkv, w_out, normed,
    ) = refs[3:24]
    layer_out, input_grad = refs[24:26]
    outs = refs[26:31]
    gains = refs[31]
    scratch = refs[32:]
    owns = (*scratch[:OWN], None, None)
    lands, ins, mids, extras, totals = (
        scratch[OWN + 5 * i : OWN + 5 * i + 5] for i in range(5)
    )
    (
        o_part, qkv_part, core_send, core_land, x_send, x_land, back_rows, low_rows, grad_items,
        delta, dq, kv_send, kv_land, qkv_rows, gain_rows, keys, values,
    ) = scratch[OWN + 25 : OWN + 42]
    (
        loc, ys, yr, es, er, zs, zr, ss, sr, cs, cr, xs, xr, ns, nr, ks, kr, gs, gr, ts, tr, bs,
    ) = scratch[OWN + 42 :]
    y = lax.axis_index("fy")
    c = lax.axis_index("pr")
    z = lax.axis_index("ctx")
    span, width = rows.shape
    chunk = width // 4
    half = 4 * DH
    sources = (*sources, o_part, qkv_part)
    line = Line(nz)
    scatter = Scatter(
        line, sources, owns, lands, ins, mids, extras, totals, outs,
        (loc, ys, yr, es, er, zs, zr, ss, sr),
    )
    greet(
        [
            ({"fy": 1 - y}, None),
            ({"pr": 1 - c}, None),
            ({"tp": 1 - lax.axis_index("tp")}, None),
        ]
        + [({"ctx": t}, z != t) for t in range(nz)],
        2 + nz,
    )
    bufs = (core_send, core_land, x_send, x_land)
    sems = (cs, cr, xs, xr)
    late = (0, 1, 2)

    def columns(i):
        return pl.ds(i * chunk, chunk)

    scatter.start(0)
    first = TokenSum(lambda who, i: dx_part[who, :, columns(i)], bufs, sems, 0)
    first.start()
    scatter.start(2)
    scatter.step(0, 0)
    scatter.step(0, 1)
    scatter.start(1)

    squares = jnp.zeros((span, 1), F32)
    inner_sum = jnp.zeros((span, 1), F32)
    for i in range(4):
        first.arrived(i)
        grad = first.total(i)
        back_rows[:, columns(i)] = grad
        value = residual[:, columns(i)]
        squares = squares + jnp.sum(value * value, axis=1, keepdims=True)
        inner_sum = inner_sum + jnp.sum(grad * mlp_gain[:, columns(i)] * value, axis=1, keepdims=True)
    factor = lax.rsqrt(squares / width + EPS)
    slope = factor * factor * factor * (inner_sum / width)
    for i in range(4):
        grad = back_rows[:, columns(i)]
        value = residual[:, columns(i)]
        gain_rows[1:2, columns(i)] = jnp.sum(grad * value * factor, axis=0, keepdims=True)
        back = (
            upstream[:, columns(i)].astype(F32)
            + factor * (grad * mlp_gain[:, columns(i)])
            - value * slope
        )
        back_rows[:, columns(i)] = back
        low_rows[c, :, columns(i)] = back.astype(BF16)
    first.drain()
    swap = remote(low_rows.at[c], low_rows.at[c], ns.at[0], nr.at[0], {"pr": 1 - c})
    swap.start()
    remote(low_rows.at[1 - c], low_rows.at[1 - c], ns.at[0], nr.at[0], {"pr": 1 - c}).wait_recv()
    for b in range(2):
        grads = jnp.zeros((span, half), F32)
        for i in range(4):
            weights = w_out[i // 2, i % 2].reshape(chunk, half)
            grads = grads + dot(low_rows[b, :, columns(i)], weights)
        wide = dot(grads.astype(BF16), spread_mat[...]).astype(BF16)
        for k in range(2):
            for j in range(2):
                head = 2 * k + j
                grad_items[b * 2 + k, pl.ds(j * span, span)] = wide[
                    :, head * LANES : (head + 1) * LANES
                ]
    for i in range(4):
        part = dot(low_rows[0, :, columns(i)], mixed_low[:span], 0, 0) + dot(
            low_rows[1, :, columns(i)], mixed_low[span:], 0, 0
        )
        o_part[i // 2, i % 2] = part.astype(BF16).reshape(o_part.shape[2:])
    scatter.start(3)
    scatter.step(2, 0)

    for i in range(4):
        delta[i] = jnp.broadcast_to(
            jnp.sum(grad_items[i].astype(F32) * mixed_wide[i], axis=1, keepdims=True),
            delta.shape[1:],
        )

    slots = kv_send.shape[0]
    order = scatter.order

    def keys_hop(b, place):
        offset = order[place]
        return remote(
            kv_send.at[place % slots, b],
            kv_land.at[offset, b],
            ks.at[b, offset],
            kr.at[b, offset],
            {"ctx": line.partner(low_bit(offset))},
        )

    def keys_add(b, place, offset):
        remote(
            kv_send.at[place % slots, b],
            kv_land.at[offset, b],
            ks.at[b, offset],
            kr.at[b, offset],
            {"ctx": line.partner(low_bit(offset))},
        ).wait_recv()
        kv_send[place % slots, b] = (
            kv_send[place % slots, b].astype(F32) + kv_land[offset, b].astype(F32)
        ).astype(BF16)

    def load(place):
        block = line.at(order[place])
        return (
            pltpu.make_async_copy(k_items.at[block], keys.at[place % 2], bs.at[0, place % 2]),
            pltpu.make_async_copy(v_items.at[block], values.at[place % 2], bs.at[1, place % 2]),
        )

    def load_start(place):
        @pl.when(line.at(order[place]) <= z)
        def _():
            for copy in load(place):
                copy.start()

    def back_block(place, diagonal):
        block, slot = line.at(order[place]), place % 2
        for copy in load(place):
            copy.wait()

        def one(b, _):
            key_grads, value_grads = [], []
            for k in range(2):
                item = b * 2 + k
                scores = dot(q_items[item], keys[slot, item], 1, 1) * scale
                allowed = q_seg[b] == k_seg[b, block]
                if diagonal:
                    row = lax.broadcasted_iota(jnp.int32, scores.shape, 0)
                    column = lax.broadcasted_iota(jnp.int32, scores.shape, 1)
                    allowed = allowed & (lax.rem(row, span) >= column)
                probs = jnp.where(allowed, jnp.exp(scores - lse[item][:, :1]), 0.0)
                prob_grad = dot(grad_items[item], values[slot, item], 1, 1)
                score_grad = (probs * (prob_grad - delta[item][:, :1])).astype(BF16)
                value_grads.append(dot(probs.astype(BF16), grad_items[item], 0, 0))
                key_grads.append(dot(score_grad, q_items[item], 0, 0) * scale)
                dq[item] += dot(score_grad, keys[slot, item]) * scale
            wide = jnp.concatenate(key_grads + value_grads, axis=1).astype(BF16)
            kv_send[place % slots, b] = dot(wide, spread_mat[...], 1, 1).astype(BF16)
            return 0

        lax.fori_loop(0, 2, one, 0)

    def keys_pass(place):
        offset = order[place]

        @pl.when(line.at(offset) <= z)
        def _():
            for b in range(2):
                for level in range(low_bit(offset)):
                    keys_add(b, place, offset ^ (1 << level))
                keys_hop(b, place).start()

    def keys_sent(place):
        @pl.when(line.at(order[place]) <= z)
        def _():
            for b in range(2):
                keys_hop(b, place).wait_send()

    dq[...] = jnp.zeros_like(dq)
    final = nz - 1
    load_start(0)
    for place in range(final):
        load_start(place + 1)
        if place >= slots:
            keys_sent(place - slots)

        @pl.when(line.at(order[place]) <= z)
        def _(place=place):
            back_block(place, False)

        if low_bit(order[place]) == 0 or slots < nz:
            keys_pass(place)
    scatter.step(0, 2)
    scatter.relay(2)
    if final >= slots:
        keys_sent(final - slots)
    back_block(final, True)
    scatter.relay(0)
    scatter.step(2, 1)
    if slots == nz:
        for place in range(final):
            if low_bit(order[place]) > 0:
                keys_pass(place)
    second = TokenSum(lambda who, i: out_part[who, :, columns(i)], bufs, sems, 1)
    second.start()
    scatter.step(1, 0)
    scatter.step(3, 0)
    scatter.step(2, 2)
    for i in range(4):
        second.arrived(i)
        layer_out[:, columns(i)] = (residual[:, columns(i)] + second.total(i)).astype(BF16)
    second.drain()
    for level in range(line.levels):

        @pl.when(line.bits[level] == 0)
        def _(level=level):
            for b in range(2):
                keys_add(b, final, 1 << level)

    def unrotated(field, b):
        turned = pltpu.roll(field, LANES // 2, 1)
        here = pl.ds(b * span, span)
        return (field * cos[here] - turned * sin[here]).astype(BF16)

    for b in range(2):
        heads = [
            unrotated(dq[b * 2 + k, pl.ds(j * span, span)], b) for k in range(2) for j in range(2)
        ]
        qkv_rows[b, :, :half] = dot(
            jnp.concatenate(heads, axis=1), spread_mat[...], 1, 1
        ).astype(BF16)
    for b in range(2):
        wide = dot(kv_send[final % slots, b], spread_mat[...])
        fields = [unrotated(wide[:, k * LANES : (k + 1) * LANES], b) for k in range(2)]
        fields += [wide[:, (2 + k) * LANES : (3 + k) * LANES].astype(BF16) for k in range(2)]
        qkv_rows[b, :, half:] = dot(
            jnp.concatenate(fields, axis=1), spread_mat[...], 1, 1
        ).astype(BF16)
    for i in range(4):
        part = dot(normed[:span, columns(i)], qkv_rows[0], 0, 0) + dot(
            normed[span:, columns(i)], qkv_rows[1], 0, 0
        )
        qkv_part[i // 2, i % 2] = part.astype(BF16).reshape(qkv_part.shape[2:])
    scatter.last(0)
    scatter.start(4)

    def back_in(who, i):
        weights = w_qkv[i // 2, i % 2].reshape(chunk, 2 * half)
        return dot(qkv_rows[who], weights, 1, 1)

    third = TokenSum(back_in, bufs, sems, 2)
    scatter.step(1, 1)
    scatter.relay(1)
    scatter.step(3, 1)
    scatter.step(1, 2)
    scatter.step(4, 0)
    scatter.step(3, 2)
    scatter.step(4, 1)
    for g in range(5):
        for place in range(3, final):
            scatter.step(g, place)
    scatter.last(2)
    third.start()
    scatter.relay(3)
    scatter.last(1)
    scatter.last(3)
    scatter.relay(4)
    squares = jnp.zeros((span, 1), F32)
    inner_sum = jnp.zeros((span, 1), F32)
    for i in range(4):
        third.arrived(i)
        grad = third.total(i)
        value = rows[:, columns(i)].astype(F32)
        squares = squares + jnp.sum(value * value, axis=1, keepdims=True)
        inner_sum = inner_sum + jnp.sum(grad * attn_gain[:, columns(i)] * value, axis=1, keepdims=True)
    factor = lax.rsqrt(squares / width + EPS)
    slope = factor * factor * factor * (inner_sum / width)
    for i in range(4):
        value = rows[:, columns(i)].astype(F32)
        gain_rows[0:1, columns(i)] = jnp.sum(third.total(i) * value * factor, axis=0, keepdims=True)
        input_grad[:, columns(i)] = (
            back_rows[:, columns(i)]
            + factor * (third.total(i) * attn_gain[:, columns(i)])
            - value * slope
        ).astype(BF16)
    third.drain()

    mine = pltpu.make_async_copy(gain_rows, gains.at[y, c, z], ts.at[2])
    mine.start()
    mine.wait()
    core_gain = remote(gains.at[y, c, z], gains.at[y, c, z], ts.at[1], tr.at[1], {"pr": 1 - c})
    core_gain.start()
    remote(
        gains.at[y, 1 - c, z], gains.at[y, 1 - c, z], ts.at[1], tr.at[1], {"pr": 1 - c}
    ).wait_recv()

    def gain_to(t):
        return remote(gains.at[y, :, z], gains.at[y, :, z], gs.at[t], gr.at[z], {"ctx": t})

    def gain_from(t):
        return remote(gains.at[y, :, t], gains.at[y, :, t], gs.at[t], gr.at[t], {"ctx": t})

    for t in range(nz):

        @pl.when(z != t)
        def _(t=t):
            gain_to(t).start()

    scatter.step(4, 2)
    for t in range(nz):

        @pl.when(z != t)
        def _(t=t):
            gain_from(t).wait_recv()

    gain_line = remote(gains.at[y], gains.at[y], ts.at[0], tr.at[0], {"fy": 1 - y})
    gain_line.start()
    scatter.last(4)
    remote(gains.at[1 - y], gains.at[1 - y], ts.at[0], tr.at[0], {"fy": 1 - y}).wait_recv()
    for g in range(5):
        scatter.finish(g)
    core_gain.wait_send()
    gain_line.wait_send()
    swap.wait_send()
    for t in range(nz):

        @pl.when(z != t)
        def _(t=t):
            gain_to(t).wait_send()

    for place in range(max(0, nz - slots), final):
        keys_sent(place)


def backward(parts, operands, ny, nz):
    dma = pltpu.SemaphoreType.DMA
    anywhere = pl.BlockSpec(memory_space=pl.ANY)
    vmem = pl.BlockSpec(memory_space=pltpu.VMEM)
    residual = operands[2]
    span, width = residual.shape
    chunk = width // 4
    block = parts[0].shape[3]
    half = 4 * DH
    wide = [part.shape[4] for part in parts] + [half, 2 * half]
    shape = jax.ShapeDtypeStruct
    out_shape = (
        [shape((span, width), BF16)] * 2
        + [shape((2, block, w), F32) for w in wide]
        + [shape((ny, 2, nz, 2, width), F32)]
    )

    def bufs(lead, dtype=BF16):
        return [pltpu.VMEM(lead + (block, w), dtype) for w in wide]

    return pl.pallas_call(
        functools.partial(backward_kernel, nz, DH ** (-0.5)),
        out_shape=out_shape,
        in_specs=[anywhere] * 3 + [vmem] * 13 + [anywhere] * 2 + [vmem] * 6,
        out_specs=[vmem] * 2 + [anywhere] * 6,
        scratch_shapes=bufs((2, 2))[:OWN]
        + bufs((nz, 2))
        + bufs((nz - 1, 2))
        + bufs(())
        + bufs(())
        + bufs((2,), F32)
        + [
            pltpu.VMEM((ny, 2, nz, block, half), BF16),
            pltpu.VMEM((ny, 2, nz, block, 2 * half), BF16),
            pltpu.VMEM((4, span, chunk), BF16),
            pltpu.VMEM((2, 4, span, chunk), BF16),
            pltpu.VMEM((4, span, chunk), BF16),
            pltpu.VMEM((2, 4, span, chunk), BF16),
            pltpu.VMEM((span, width), F32),
            pltpu.VMEM((2, span, width), BF16),
            pltpu.VMEM((4, 2 * span, LANES), BF16),
            pltpu.VMEM((4, 2 * span, LANES), F32),
            pltpu.VMEM((4, 2 * span, LANES), F32),
            pltpu.VMEM((min(nz, 4), 2, span, half), BF16),
            pltpu.VMEM((nz, 2, span, half), BF16),
            pltpu.VMEM((2, span, 2 * half), BF16),
            pltpu.VMEM((2, width), F32),
            pltpu.VMEM((2, 4, span, LANES), BF16),
            pltpu.VMEM((2, 4, span, LANES), BF16),
        ]
        + [dma((5, 5))]
        + [dma((5, nz + 1))] * 2
        + [dma((5,))] * 2
        + [dma((5, nz))] * 2
        + [dma((5,))] * 2
        + [dma((3, 4))] * 4
        + [dma((1,))] * 2
        + [dma((2, nz))] * 2
        + [dma((nz,))] * 2
        + [dma((3,)), dma((2,)), dma((2, 2))],
        name="backward",
        compiler_params=pltpu.CompilerParams(
            collective_id=2, has_side_effects=True, vmem_limit_bytes=VMEM_LIMIT
        ),
    )(*parts, *operands)


def halves(matrix):
    half = matrix.shape[1] // 2
    return jnp.stack([matrix[:, :half], matrix[:, half:]])


def join(halved):
    return jnp.concatenate([halved[0], halved[1]], axis=1)


def on_device(
    ny,
    nz,
    layer_input,
    segments,
    positions,
    attn_gain,
    query_proj,
    key_proj,
    value_proj,
    out_proj,
    mlp_gain,
    gate_proj,
    up_proj,
    down_proj,
    out_grad,
):
    _, span, width = layer_input.shape
    block = query_proj.shape[0]
    groups = HQ // HK
    y = lax.axis_index("fy")
    c = lax.axis_index("pr")
    z = lax.axis_index("ctx")
    rows_per = span // LANES
    small = jnp.concatenate(
        [
            jnp.pad(attn_gain.astype(F32), (0, LANES - block))[None],
            jnp.pad(mlp_gain.astype(F32), (0, LANES - block))[None],
            segments.astype(F32).reshape(rows_per, LANES),
            positions.astype(F32).reshape(rows_per, LANES),
            jnp.zeros((6 - 2 * rows_per, LANES), F32),
        ]
    )
    qkv_raw = jnp.concatenate([halves(query_proj), halves(key_proj), halves(value_proj)], axis=2)
    raws = (
        qkv_raw,
        halves(out_proj.T),
        halves(gate_proj),
        halves(up_proj),
        halves(down_proj.T),
    )
    layer_rows = layer_input.reshape(span, width)
    pieces, smalls, rows_both, grads_both = pair_swap(
        raws, small, layer_rows, out_grad.reshape(span, width), ny, nz
    )
    attn_gain_full = smalls[:, :, :, 0, :block].reshape(width)
    mlp_gain_full = smalls[:, :, :, 1, :block].reshape(width)
    mine = lax.dynamic_index_in_dim(smalls, y, 0, keepdims=False)
    segment_all = mine[:, :, 2 : 2 + rows_per].reshape(2, nz, 1, span).astype(jnp.int32)
    position_all = mine[:, :, 2 + rows_per : 2 + 2 * rows_per].reshape(2, nz, span)
    here = lax.dynamic_index_in_dim(position_all, z, 1, keepdims=False)
    segments_here = lax.dynamic_index_in_dim(segment_all, z, 1, keepdims=False)
    q_seg = jnp.tile(segments_here.reshape(2, span), (1, groups))[:, :, None]

    total_rows = 2 * span
    inputs = rows_both.reshape(total_rows, width).astype(F32)
    scale_attn = inverse_rms(inputs)
    normed_attn = (inputs * scale_attn * attn_gain_full).astype(BF16)
    cos_half, sin_half = rotary_tables(here.reshape(total_rows))
    blank = jnp.zeros((total_rows, LANES // 2 - DH // 2), F32)
    cos_wide = jnp.concatenate([cos_half, blank, cos_half, blank], axis=1)
    sin_wide = jnp.concatenate([-sin_half, blank, sin_half, blank], axis=1)
    lane_from = jnp.arange(4 * DH)
    lane_to = lane_from // DH * LANES + lane_from % DH
    lane_to = jnp.where(lane_from % DH < DH // 2, lane_to, lane_to + LANES // 2 - DH // 2)
    spread_mat = (lane_to[:, None] == jnp.arange(4 * LANES)[None]).astype(BF16)
    results = forward(
        pieces,
        normed_attn,
        layer_rows,
        cos_wide,
        sin_wide,
        q_seg,
        segment_all,
        spread_mat,
        mlp_gain_full.reshape(1, width),
        ny,
        nz,
    )
    gate_full, up_full, down_full = (
        piece.reshape(width, piece.shape[-1]) for piece in results[2:5]
    )
    q_items, k_items, v_items, mixed_wide, mixed_low, row_lse, residual_own, normed_mlp = results[5:]
    normed_mlp = normed_mlp.reshape(total_rows, width)
    gate_pre = jnp.dot(normed_mlp, gate_full, preferred_element_type=F32)
    up_pre = jnp.dot(normed_mlp, up_full, preferred_element_type=F32)
    activated = jax.nn.silu(gate_pre)
    hidden = (activated * up_pre).astype(BF16)

    out_part = contract(hidden, down_full, 1, 1).astype(BF16).reshape(2, span, width)
    upstream_low = grads_both.reshape(total_rows, width)
    hidden_grad = jnp.dot(upstream_low, down_full, preferred_element_type=F32)
    sigmoid_gate = jax.nn.sigmoid(gate_pre)
    gate_grad = (
        hidden_grad * up_pre * sigmoid_gate * (1.0 + gate_pre * (1.0 - sigmoid_gate))
    ).astype(BF16)
    up_grad = (hidden_grad * activated).astype(BF16)
    dx_part = (
        (contract(gate_grad, gate_full, 1, 1) + contract(up_grad, up_full, 1, 1))
        .astype(BF16)
        .reshape(2, span, width)
    )
    parts = [
        part.astype(BF16).reshape(ny, 2, nz, block, part.shape[1])
        for part in (
            contract(upstream_low, hidden, 0, 0),
            contract(normed_mlp, gate_grad, 0, 0),
            contract(normed_mlp, up_grad, 0, 0),
        )
    ]
    operands = (
        dx_part,
        out_part,
        residual_own,
        layer_rows,
        out_grad.reshape(span, width),
        mlp_gain_full.reshape(1, width),
        attn_gain_full.reshape(1, width),
        cos_wide,
        sin_wide,
        q_seg,
        segment_all,
        spread_mat,
        q_items,
        k_items,
        v_items,
        mixed_wide,
        mixed_low,
        row_lse,
        results[0],
        results[1],
        normed_attn,
    )
    layer_output, input_grad, down_g, gate_g, up_g, out_g, qkv_g, gains_all = backward(
        parts, operands, ny, nz
    )
    gain_sum = jnp.sum(gains_all, axis=(0, 1, 2))
    place = ((y * 2 + c) * nz + z) * block
    gain_own = lax.dynamic_slice_in_dim(gain_sum, place, block, 1)
    q_width, kv_width = 4 * DH, 2 * DH
    return (
        layer_output.reshape(1, span, width),
        input_grad.reshape(1, span, width),
        gain_own[0],
        join(qkv_g[:, :, :q_width]),
        join(qkv_g[:, :, q_width : q_width + kv_width]),
        join(qkv_g[:, :, q_width + kv_width :]),
        join(out_g).T,
        gain_own[1],
        join(gate_g),
        join(up_g),
        join(down_g).T,
    )


def solution(mesh):
    sizes = mesh.shape
    ny, nz = sizes["fsdp"] // 2, sizes["ctx"]
    inner = Mesh(
        mesh.devices.reshape(ny, 2, nz, sizes["tp"]), ("fy", "pr", "ctx", "tp")
    )
    seqs = ("fy", "pr")
    rows = P(seqs, "ctx", None)
    marks = P(seqs, "ctx")
    gain = P(GROUP)
    tall = P(GROUP, "tp")
    wide = P("tp", GROUP)
    return jax.shard_map(
        functools.partial(on_device, ny, nz),
        mesh=inner,
        in_specs=(
            rows, marks, marks, gain, tall, tall, tall, wide, gain, tall, tall, wide, rows,
        ),
        out_specs=(rows, rows, gain, tall, tall, tall, wide, gain, tall, tall, wide),
        check_vma=False,
    )
```

```python
import functools

import jax
import jax.numpy as jnp
from jax import lax
from jax.experimental import pallas as pl
from jax.experimental.pallas import tpu as pltpu
from jax.sharding import Mesh, PartitionSpec as P

HQ = 16
HK = 8
DH = 96


EPS = 1e-05
THETA = 100000.0
NEGATIVE = -1e30


def contract(left, right, left_dim, right_dim):
    return lax.dot_general(
        left, right, (((left_dim,), (right_dim,)), ((), ())), preferred_element_type=jnp.float32
    )


MESH_ID = pl.DeviceIdType.MESH
BF16 = jnp.bfloat16
F32 = jnp.float32
GROUP = ("fy", "pr", "ctx")
VMEM_LIMIT = 62 * 1024 * 1024
LANES = 128


def remote(src, dst, send_sem, recv_sem, device):
    return pltpu.make_async_remote_copy(
        src_ref=src,
        dst_ref=dst,
        send_sem=send_sem,
        recv_sem=recv_sem,
        device_id=device,
        device_id_type=MESH_ID,
    )


def greet(devices_and_conditions, count):
    barrier = pltpu.get_barrier_semaphore()
    for device, condition in devices_and_conditions:
        if condition is None:
            pl.semaphore_signal(barrier, inc=1, device_id=device, device_id_type=MESH_ID)
        else:

            @pl.when(condition)
            def _(device=device):
                pl.semaphore_signal(barrier, inc=1, device_id=device, device_id_type=MESH_ID)

    pl.semaphore_wait(barrier, count)


def dot(left, right, left_dim=1, right_dim=0):
    return lax.dot_general(
        left, right, (((left_dim,), (right_dim,)), ((), ())), preferred_element_type=F32
    )


def low_bit(number):
    return (number & -number).bit_length() - 1


class Line:
    def __init__(self, nz):
        self.nz, self.levels = nz, nz.bit_length() - 1
        self.z = lax.axis_index("ctx")
        self.bits = [lax.rem(self.z // (1 << level), 2) for level in range(self.levels)]

    def at(self, offset):
        place = self.z
        for level in range(self.levels):
            if offset >> level & 1:
                place = place + (1 << level) - (2 << level) * self.bits[level]
        return place

    def partner(self, level):
        return self.at(1 << level)


class Gather:
    def __init__(self, line, outs, zs, zr, ys, yr):
        self.line, self.outs = line, outs
        self.zs, self.zr, self.ys, self.yr = zs, zr, ys, yr
        self.y = lax.axis_index("fy")
        offsets = range(1, line.nz)
        self.arrivals = sorted(offsets, key=lambda offset: (-low_bit(offset), offset))

    def hop(self, g, offset, level):
        piece = self.outs[g].at[self.y, :, self.line.at(offset)]
        slot = offset + (1 << level)
        return remote(
            piece, piece, self.zs.at[g, slot], self.zr.at[g, slot], {"ctx": self.line.partner(level)}
        )

    def hop_from(self, g, offset):
        piece = self.outs[g].at[self.y, :, self.line.at(offset)]
        partner = self.line.partner(low_bit(offset))
        return remote(piece, piece, self.zs.at[g, offset], self.zr.at[g, offset], {"ctx": partner})

    def across(self, g, offset, row):
        piece = self.outs[g].at[row, :, self.line.at(offset)]
        return remote(
            piece, piece, self.ys.at[g, offset], self.yr.at[g, offset], {"fy": 1 - self.y}
        )

    def hops(self, offset):
        last = low_bit(offset) if offset else self.line.levels
        return reversed(range(last))

    def own_z(self, g):
        for level in self.hops(0):
            self.hop(g, 0, level).start()

    def own_y(self, g):
        self.across(g, 0, self.y).start()

    def step(self, g, offset):
        self.hop_from(g, offset).wait_recv()
        for level in self.hops(offset):
            self.hop(g, offset, level).start()
        self.across(g, offset, self.y).start()

    def finish(self, g):
        for offset in (0, *self.arrivals):
            self.across(g, offset, 1 - self.y).wait_recv()

    def drain(self, g):
        for offset in (0, *self.arrivals):
            for level in self.hops(offset):
                self.hop(g, offset, level).wait_send()
            self.across(g, offset, self.y).wait_send()


class TokenSum:
    def __init__(self, part, bufs, sems, n):
        self.part, self.n = part, n
        self.core_send, self.core_land, self.x_send, self.x_land = bufs
        self.cs, self.cr, self.xs, self.xr = sems
        self.c = lax.axis_index("pr")
        self.x = lax.axis_index("tp")

    def core(self, i):
        return remote(
            self.core_send.at[i],
            self.core_land.at[self.n % 2, i],
            self.cs.at[self.n, i],
            self.cr.at[self.n, i],
            {"pr": 1 - self.c},
        )

    def sideways(self, i):
        return remote(
            self.x_send.at[i],
            self.x_land.at[self.n % 2, i],
            self.xs.at[self.n, i],
            self.xr.at[self.n, i],
            {"tp": 1 - self.x},
        )

    def start(self):
        def give(i, _):
            self.core_send[i] = self.part(1 - self.c, i).astype(BF16)
            self.core(i).start()
            return 0

        def add(i, _):
            mine = self.part(self.c, i).astype(F32)
            self.core(i).wait_recv()
            self.x_send[i] = (mine + self.core_land[self.n % 2, i].astype(F32)).astype(BF16)
            self.sideways(i).start()
            return 0

        lax.fori_loop(0, 4, give, 0)
        lax.fori_loop(0, 4, add, 0)

    def arrived(self, i):
        self.sideways(i).wait_recv()

    def total(self, i):
        return self.x_send[i].astype(F32) + self.x_land[self.n % 2, i].astype(F32)

    def drain(self):
        for i in range(4):
            self.core(i).wait_send()
            self.sideways(i).wait_send()


def weight_grad(into, left, right, stage, sems):
    _, span, width = left.shape
    chunk = width // 4

    def stored_part(i):
        slot = lax.rem(i, 2)
        return pltpu.make_async_copy(stage.at[slot], into.at[i // 2, slot], sems.at[slot])

    def one(i, _):
        here = pl.ds(pl.multiple_of(i * chunk, LANES), chunk)
        part = dot(left[0, :, here], right[:span], 0, 0) + dot(left[1, :, here], right[span:], 0, 0)

        @pl.when(i > 1)
        def _():
            stored_part(i - 2).wait()

        stage[lax.rem(i, 2)] = part.astype(BF16).reshape(stage.shape[1:])
        stored_part(i).start()
        return 0

    lax.fori_loop(0, 4, one, 0)
    for i in (2, 3):
        stored_part(i).wait()


def forward_kernel(nz, items, scale, *refs):
    weights = refs[:6]
    rows, upstream, small, info, freq, spread_mat = refs[6:12]
    stored = refs[12:26]
    down_grad = refs[26]
    cos, sin, q_seg, k_seg, gains = refs[27:32]
    made = refs[32:46]
    (
        w_qkv, w_out, q_out, kvu, mixed_out, mixed_low, lse_out, residual, normed, dx_part, out_part,
        normed_mlp, gate_grad, up_grad,
    ) = made
    (
        w_gate, w_up, w_down, acc, keys, values, top, core_send, core_land, x_send, x_land, smalls, info_both,
        rows_both, gate_pre, up_pre, upstream_both, hidden, stage,
    ) = refs[46:65]
    (
        loc, ps, pr, ws, wr, ts, tr, zs, zr, ys, yr, ks, kr, cs, cr, xs, xr, ns, nr, hs, gs,
    ) = refs[65:]

    def store(n):
        return pltpu.make_async_copy(made[n], stored[n], hs.at[n])

    outs = (w_qkv, w_out, w_gate, w_up, w_down)
    y = lax.axis_index("fy")
    c = lax.axis_index("pr")
    z = lax.axis_index("ctx")
    x = lax.axis_index("tp")
    span, width = rows.shape
    other_y, other_c, other_x = {"fy": 1 - y}, {"pr": 1 - c}, {"tp": 1 - x}
    line = Line(nz)
    gather = Gather(line, outs, zs, zr, ys, yr)
    chunk = width // 4
    half = w_out.shape[4]
    block = w_out.shape[3]
    late = (2, 3, 4)

    def columns(i):
        return pl.ds(pl.multiple_of(i * chunk, LANES), chunk)

    greet(
        [(other_y, None), (other_c, None), (other_x, None)]
        + [({"ctx": line.at(offset)}, None) for offset in range(1, nz)],
        2 + nz,
    )

    places = [(0, 0, half), (0, half, half), (1, 0, half)]
    places += [(g, 0, outs[g].shape[4]) for g in late]

    def half_of(n, which):
        size = places[n][2]
        return weights[n].at[:, pl.ds(pl.multiple_of(which * size, LANES), size)]

    def piece_of(n):
        g, first, size = places[n]
        return outs[g].at[y, c, z, :, pl.ds(first, size)]

    def other_piece(n):
        g, first, size = places[n]
        return outs[g].at[y, 1 - c, z, :, pl.ds(first, size)]

    moved = [(rows, rows_both), (upstream, upstream_both), (info, info_both)]
    local = [pltpu.make_async_copy(half_of(n, c), piece_of(n), loc.at[n]) for n in range(6)]
    local += [
        pltpu.make_async_copy(src, dst.at[c], loc.at[6 + n]) for n, (src, dst) in enumerate(moved)
    ]
    sent = [
        remote(half_of(n, 1 - c), piece_of(n), ps.at[n], pr.at[n], other_c) for n in range(6)
    ]
    sent += [
        remote(src, dst.at[c], ps.at[6 + n], pr.at[6 + n], other_c)
        for n, (src, dst) in enumerate(moved)
    ]
    landed = [
        remote(half_of(n, 1 - c), other_piece(n), ps.at[n], pr.at[n], other_c) for n in range(6)
    ]
    landed += [
        remote(src, dst.at[1 - c], ps.at[6 + n], pr.at[6 + n], other_c)
        for n, (src, dst) in enumerate(moved)
    ]

    def small_to(offset):
        return remote(
            small, smalls.at[y, c, z], ws.at[offset], wr.at[offset], {"ctx": line.at(offset)}
        )

    def small_from(offset):
        return remote(
            small, smalls.at[y, c, line.at(offset)], ws.at[offset], wr.at[offset],
            {"ctx": line.at(offset)},
        )

    small_here = pltpu.make_async_copy(small, smalls.at[y, c, z], loc.at[9])
    small_here.start()
    for n in range(3):
        local[n].start()
        sent[n].start()
    for offset in range(1, nz):
        small_to(offset).start()
    for n in (6, 8, 3, 4, 5, 7):
        local[n].start()
        sent[n].start()
    for n in range(2):
        local[n].wait()
        landed[n].wait_recv()
    gather.own_z(0)
    small_here.wait()
    for offset in range(1, nz):
        small_from(offset).wait_recv()
    small_line = remote(smalls.at[y, c], smalls.at[y, c], ts.at[0], tr.at[0], other_y)
    small_line.start()
    small_plane = remote(smalls.at[:, c], smalls.at[:, c], ts.at[1], tr.at[1], other_c)
    gather.own_y(0)
    for n in (5, 4, 2, 3):
        local[n].wait()
        landed[n].wait_recv()

    def prepare():
        remote(smalls.at[1 - y, c], smalls.at[1 - y, c], ts.at[0], tr.at[0], other_y).wait_recv()
        small_plane.start()
        for n in (6, 7, 8):
            local[n].wait()
            landed[n].wait_recv()
        factors = []
        for b in range(2):
            value = rows_both[b].astype(F32)
            factors.append(lax.rsqrt(jnp.sum(value * value, axis=1, keepdims=True) / width + EPS))
            angles = info_both[b, :, 0:1] * freq[...]
            lane = lax.broadcasted_iota(jnp.int32, (span, LANES), 1)
            used = lax.rem(lane, LANES // 2) < DH // 2
            here = pl.ds(b * span, span)
            cos[here] = jnp.where(used, jnp.cos(angles), 0.0)
            turn = jnp.where(used, jnp.sin(angles), 0.0)
            sin[here] = jnp.where(lane < LANES // 2, -turn, turn)
            for j in range(2):
                q_seg[b, pl.ds(j * span, span)] = info_both[b, :, 1:2]
        remote(smalls.at[:, 1 - c], smalls.at[:, 1 - c], ts.at[1], tr.at[1], other_c).wait_recv()
        per = span // LANES
        for b in range(2):
            for j in range(nz):
                for part in range(per):
                    k_seg[b, j, :, pl.ds(part * LANES, LANES)] = smalls[
                        y, b, j, pl.ds(2 + part, 1)
                    ]
        for which in range(2):
            gain_row = jnp.zeros((1, width), F32)
            blank = jnp.zeros((1, width - LANES), F32)
            for n in range(4 * nz):
                own = smalls[n // (2 * nz), n // nz % 2, n % nz, pl.ds(which, 1)]
                wide = jnp.concatenate([own, blank], axis=1)
                gain_row = gain_row + (pltpu.roll(wide, n * block, 1) if n else wide)
            gains[which] = gain_row
        for b in range(2):
            normed[b] = (rows_both[b].astype(F32) * factors[b] * gains[0]).astype(BF16)
        store(8).start()

    def head_fields():
        acc[...] = jnp.zeros_like(acc)

        def one(i, _):
            part = w_qkv[i // 2, lax.rem(i, 2)].reshape(chunk, 2 * half)
            wide = jnp.concatenate(
                [
                    dot(part[:, :half], spread_mat[...]).astype(BF16),
                    dot(part[:, half:], spread_mat[...]).astype(BF16),
                ],
                axis=1,
            )
            for b in range(2):
                acc[pl.ds(b * span, span)] += dot(normed[b, :, columns(i)], wide)
            return 0

        lax.fori_loop(0, 4, one, 0)

    def rotated(b, lane):
        here = pl.ds(b * span, span)
        field = acc[here, pl.ds(lane * LANES, LANES)]
        turned = pltpu.roll(field, LANES // 2, 1)
        return (field * cos[here] + turned * sin[here]).astype(BF16)

    def keys_hop(b, offset, level):
        piece = kvu.at[line.at(offset), b]
        slot = offset + (1 << level)
        return remote(
            piece, piece, ks.at[b, slot], kr.at[b, slot], {"ctx": line.partner(level)}
        )

    def keys_from(b, offset):
        piece = kvu.at[line.at(offset), b]
        partner = line.partner(low_bit(offset))
        return remote(piece, piece, ks.at[b, offset], kr.at[b, offset], {"ctx": partner})

    def each_hop(offset, act):
        for level in gather.hops(offset):

            @pl.when(line.at(offset) <= line.partner(level))
            def _(level=level):
                act(level)

    def project_heads():
        head_fields()
        for b in range(2):
            fields = []
            for k in range(2):
                keys[b * 2 + k] = rotated(b, 4 + k)
                fields.append(keys[b * 2 + k])
            for k in range(2):
                values[b * 2 + k] = acc[
                    pl.ds(b * span, span), pl.ds((6 + k) * LANES, LANES)
                ].astype(BF16)
                fields.append(values[b * 2 + k])
            kvu[z, b] = dot(jnp.concatenate(fields, axis=1), spread_mat[...], 1, 1).astype(BF16)
            each_hop(0, lambda level, b=b: keys_hop(b, 0, level).start())

        for b in range(2):
            for k in range(2):
                for j in range(2):
                    q_out[b * 2 + k, pl.ds(j * span, span)] = rotated(b, 2 * k + j)

    def attend(there, first):
        def one(n, _):
            i = n // 2
            b = i // 2
            here = pl.ds(pl.multiple_of(lax.rem(n, 2) * span, span), span)
            scores = dot(q_out[i, here], keys[i], 1, 1) * scale
            allowed = q_seg[b, :span] == k_seg[b, there]
            if first:
                row = lax.broadcasted_iota(jnp.int32, scores.shape, 0)
                column = lax.broadcasted_iota(jnp.int32, scores.shape, 1)
                allowed = allowed & (row >= column)
            scores = jnp.where(allowed, scores, NEGATIVE)
            peak = jnp.max(scores, axis=1, keepdims=True)
            if first:
                probs = jnp.exp(scores - peak)
                total = jnp.sum(probs, axis=1, keepdims=True)
                mixed_out[i, here] = dot(probs.astype(BF16), values[i])
            else:
                old = top[i, here][:, :1]
                peak = jnp.maximum(old, peak)
                keep = jnp.exp(old - peak)
                probs = jnp.exp(scores - peak)
                total = keep * lse_out[i, here][:, :1] + jnp.sum(probs, axis=1, keepdims=True)
                mixed_out[i, here] = keep * mixed_out[i, here] + dot(
                    probs.astype(BF16), values[i]
                )
            top[i, here] = jnp.broadcast_to(peak, (span, LANES))
            lse_out[i, here] = jnp.broadcast_to(total, (span, LANES))
            return 0

        lax.fori_loop(0, 2 * items, one, 0)

    def attend_own():
        attend(z, True)

    def keys_in(offset):
        @pl.when(line.at(offset) <= z)
        def _():
            for b in range(2):
                keys_from(b, offset).wait_recv()
                each_hop(offset, lambda level, b=b: keys_hop(b, offset, level).start())

    def attend_at(offset):
        there = line.at(offset)

        @pl.when(there <= z)
        def _():
            for b in range(2):
                wide = dot(kvu[there, b], spread_mat[...]).astype(BF16)
                for k in range(2):
                    keys[b * 2 + k] = wide[:, k * LANES : (k + 1) * LANES]
                    values[b * 2 + k] = wide[:, (2 + k) * LANES : (3 + k) * LANES]
            attend(there, False)

    def close():
        def divide(i, _):
            total = lse_out[i]
            mixed_out[i] = mixed_out[i] / total
            lse_out[i] = top[i] + jnp.log(total)
            return 0

        lax.fori_loop(0, items, divide, 0)
        for b in range(2):
            heads = [
                mixed_out[b * 2 + k, pl.ds(j * span, span)].astype(BF16)
                for k in range(2)
                for j in range(2)
            ]
            mixed_low[pl.ds(b * span, span)] = dot(
                jnp.concatenate(heads, axis=1), spread_mat[...], 1, 1
            ).astype(BF16)
        for n in (2, 3, 4, 5, 6):
            store(n).start()

    def projected(who, i):
        part = w_out[i // 2, lax.rem(i, 2)].reshape(chunk, half)
        return dot(mixed_low[pl.ds(pl.multiple_of(who * span, span), span)], part, 1, 1)

    token_sum = TokenSum(
        projected, (core_send, core_land, x_send, x_land), (cs, cr, xs, xr), 0
    )
    swap = remote(normed_mlp.at[c], normed_mlp.at[c], ns.at[0], nr.at[0], other_c)

    def add_residual():
        def one(i, _):
            token_sum.arrived(i)
            residual[:, columns(i)] = rows[:, columns(i)].astype(F32) + token_sum.total(i)
            return 0

        lax.fori_loop(0, 4, one, 0)
        store(7).start()

    def norm():
        def one(i, squares):
            total = residual[:, columns(i)]
            return squares + jnp.sum(total * total, axis=1, keepdims=True)

        squares = lax.fori_loop(0, 4, one, jnp.zeros((span, 1), F32))
        factor = lax.rsqrt(squares / width + EPS)

        def two(i, _):
            here = columns(i)
            normed_mlp[c, :, here] = (residual[:, here] * factor * gains[1, :, here]).astype(BF16)
            return 0

        lax.fori_loop(0, 4, two, 0)
        swap.start()

    def swapped():
        remote(normed_mlp.at[1 - c], normed_mlp.at[1 - c], ns.at[0], nr.at[0], other_c).wait_recv()

    size = 256
    blocks = w_gate.shape[4] // size

    def column_block(ref, n):
        part = ref[:, :, :, :, pl.ds(pl.multiple_of(n * size, size), size)]
        return part.reshape(width, size)

    def project(into, ref):
        def one(n, _):
            cols = pl.ds(pl.multiple_of(n * size, size), size)
            part = column_block(ref, n)
            for b in range(2):
                into[pl.ds(b * span, span), cols] = dot(normed_mlp[b], part)
            return 0

        lax.fori_loop(0, blocks, one, 0)

    def hidden_block(n, _):
        cols = pl.ds(pl.multiple_of(n * size, size), size)
        for b in range(2):
            here = pl.ds(b * span, span)
            gate = gate_pre[here, cols]
            hidden[here, cols] = (gate * jax.nn.sigmoid(gate) * up_pre[here, cols]).astype(BF16)
        return 0

    def grads_block(n, _):
        cols = pl.ds(pl.multiple_of(n * size, size), size)
        part = column_block(w_down, n)
        for b in range(2):
            here = pl.ds(b * span, span)
            back = dot(upstream_both[b], part)
            gate, up = gate_pre[here, cols], up_pre[here, cols]
            open_part = jax.nn.sigmoid(gate)
            gate_grad[here, cols] = (
                back * up * open_part * (1.0 + gate * (1.0 - open_part))
            ).astype(BF16)
            up_grad[here, cols] = (back * (gate * open_part)).astype(BF16)
        return 0

    def back_block(i, _):
        cols = pl.ds(pl.multiple_of(i * chunk, LANES), chunk)
        gate_part = w_gate[i // 2, lax.rem(i, 2)].reshape(chunk, blocks * size)
        up_part = w_up[i // 2, lax.rem(i, 2)].reshape(chunk, blocks * size)
        down_part = w_down[i // 2, lax.rem(i, 2)].reshape(chunk, blocks * size)
        for b in range(2):
            here = pl.ds(b * span, span)
            dx_part[b, :, cols] = (
                dot(gate_grad[here], gate_part, 1, 1) + dot(up_grad[here], up_part, 1, 1)
            ).astype(BF16)
            out_part[b, :, cols] = dot(hidden[here], down_part, 1, 1).astype(BF16)
        return 0

    own_z, own_y, step = gather.own_z, gather.own_y, gather.step

    def finish(g):
        gather.finish(g)
        if g < 2:
            store(g).start()

    start_sum = token_sum.start

    def gate():
        project(gate_pre, w_gate)

    def up():
        project(up_pre, w_up)

    def hide():
        lax.fori_loop(0, blocks, hidden_block, 0)
        weight_grad(down_grad, upstream_both, hidden, stage, gs)

    def grads():
        lax.fori_loop(0, blocks, grads_block, 0)
        for n in (11, 12, 13):
            store(n).start()

    def back_rows():
        lax.fori_loop(0, 4, back_block, 0)
        store(9).start()
        store(10).start()

    arrivals = gather.arrivals
    if nz == 4:
        plan = [
            (own_y, 4), (own_y, 3), (step, 0, 2), (own_y, 1), (own_z, 1), (prepare,), (own_z, 2),
            (step, 0, 1), (step, 0, 3), (step, 1, 2), (step, 1, 1), (own_z, 3), (step, 2, 2),
            (step, 2, 1), (finish, 0), (project_heads,), (step, 3, 1), (step, 1, 3),
            (step, 2, 3), (attend_own,), (keys_in, 2), (own_y, 2), (finish, 1), (own_z, 4),
            (attend_at, 2), (keys_in, 1), (step, 3, 2), (attend_at, 1), (keys_in, 3),
            (attend_at, 3), (close,), (step, 4, 2), (start_sum,), (step, 4, 1), (step, 3, 3),
            (add_residual,), (finish, 2), (norm,), (step, 4, 3), (finish, 3), (swapped,),
            (gate,), (up,), (hide,), (finish, 4), (grads,), (back_rows,),
        ]
    else:
        plan = [(own_z, 1), (own_y, 1), (prepare,)]
        plan += [(step, g, offset) for offset in arrivals for g in (0, 1)]
        plan += [(run, g) for g in late for run in (own_z, own_y)]
        plan += [(finish, 0), (project_heads,), (attend_own,)]
        plan += [(run, offset) for offset in arrivals for run in (keys_in, attend_at)]
        plan += [(close,), (finish, 1), (start_sum,)]
        plan += [(step, g, offset) for offset in arrivals for g in late]
        plan += [(add_residual,), (norm,), (swapped,), (finish, 2), (gate,), (finish, 3), (up,)]
        plan += [(hide,), (finish, 4), (grads,), (back_rows,)]
    for run, *which in plan:
        run(*which)

    for g in range(5):
        gather.drain(g)
    for b in range(2):
        each_hop(0, lambda level, b=b: keys_hop(b, 0, level).wait_send())
        for offset in gather.arrivals:

            @pl.when(line.at(offset) <= z)
            def _(b=b, offset=offset):
                each_hop(offset, lambda level: keys_hop(b, offset, level).wait_send())

    for n in range(14):
        store(n).wait()
    token_sum.drain()
    swap.wait_send()
    for copy in sent:
        copy.wait_send()
    small_line.wait_send()
    small_plane.wait_send()
    for offset in range(1, nz):
        small_to(offset).wait_send()


def forward(weights, rows, upstream, small, info, freq, spread_mat, ny, nz):
    dma = pltpu.SemaphoreType.DMA
    vmem = pl.BlockSpec(memory_space=pltpu.VMEM)
    span, width = rows.shape
    block, half, wide = weights[0].shape[0], weights[0].shape[1] // 2, weights[3].shape[1] // 2
    items, q_rows, both = 4, 2 * span, 2 * span
    shape = jax.ShapeDtypeStruct
    chunk = width // 4
    anywhere = pl.BlockSpec(memory_space=pl.ANY)
    weight = (ny, 2, nz, block)
    made = [
        (weight + (2 * half,), BF16),
        (weight + (half,), BF16),
        ((items, q_rows, LANES), BF16),
        ((nz, 2, span, half), BF16),
        ((items, q_rows, LANES), F32),
        ((both, half), BF16),
        ((items, q_rows, LANES), F32),
        ((span, width), F32),
        ((2, span, width), BF16),
        ((2, span, width), BF16),
        ((2, span, width), BF16),
        ((2, span, width), BF16),
        ((both, wide), BF16),
        ((both, wide), BF16),
    ]
    out_shape = [shape(*each) for each in made] + [shape(weight + (wide,), BF16)]
    out_shape += [
        shape((both, LANES), F32),
        shape((both, LANES), F32),
        shape((2, q_rows, 1), F32),
        shape((2, nz, 1, span), F32),
        shape((2, 1, width), F32),
    ]
    return pl.pallas_call(
        functools.partial(forward_kernel, nz, items, DH ** (-0.5)),
        out_shape=out_shape,
        in_specs=[vmem] * 12,
        out_specs=[anywhere] * 15 + [vmem] * 5,
        scratch_shapes=[pltpu.VMEM(*each) for each in made]
        + [pltpu.VMEM(weight + (wide,), BF16)] * 3
        + [
            pltpu.VMEM((both, 8 * LANES), F32),
            pltpu.VMEM((items, span, LANES), BF16),
            pltpu.VMEM((items, span, LANES), BF16),
            pltpu.VMEM((items, q_rows, LANES), F32),
            pltpu.VMEM((4, span, chunk), BF16),
            pltpu.VMEM((1, 4, span, chunk), BF16),
            pltpu.VMEM((4, span, chunk), BF16),
            pltpu.VMEM((1, 4, span, chunk), BF16),
            pltpu.VMEM((ny, 2, nz) + small.shape, F32),
            pltpu.VMEM((2, span, LANES), F32),
            pltpu.VMEM((2, span, width), BF16),
            pltpu.VMEM((both, wide), F32),
            pltpu.VMEM((both, wide), F32),
            pltpu.VMEM((2, span, width), BF16),
            pltpu.VMEM((both, wide), BF16),
            pltpu.VMEM((2, nz, block, wide), BF16),
        ]
        + [dma((10,)), dma((9,)), dma((9,)), dma((nz,)), dma((nz,)), dma((2,)), dma((2,))]
        + [dma((5, nz))] * 4
        + [dma((2, nz))] * 2
        + [dma((1, 4))] * 4
        + [dma((1,))] * 2
        + [dma((14,)), dma((2,))],
        name="forward",
        compiler_params=pltpu.CompilerParams(
            collective_id=1, has_side_effects=True, vmem_limit_bytes=VMEM_LIMIT
        ),
    )(*weights, rows, upstream, small, info, freq, spread_mat)


RELAYED = (0,)
LATER = (19, 21, 20, 17, 14, 13, 11, 15, 1, 18, 16, 3)


class Scatter:
    def __init__(self, line, sources, owns, lands, ins, mids, extras, totals, outs, sems):
        self.line, self.sources, self.owns, self.lands = line, sources, owns, lands
        self.ins, self.mids, self.extras = ins, mids, extras
        self.totals, self.outs, self.sems = totals, outs, sems
        self.y = lax.axis_index("fy")
        self.c = lax.axis_index("pr")
        nz = line.nz
        self.order = sorted(range(1, nz), key=lambda offset: (low_bit(offset), -offset)) + [0]

    def own_copy(self, g, place):
        return pltpu.make_async_copy(
            self.sources[g].at[self.y, :, self.line.at(self.order[place])],
            self.owns[g].at[place % 2],
            self.sems[0].at[g, 3 + place % 2],
        )

    def own(self, g, place, k, rows):
        if self.owns[g] is None:
            place_at = self.line.at(self.order[place])
            return self.sources[g][self.y, k, place_at, rows].astype(F32)
        return self.owns[g][place % 2, k, rows].astype(F32)

    def fetch(self, g, place):
        if self.owns[g] is not None and place < self.line.nz:
            self.own_copy(g, place).start()

    def fetched(self, g, place):
        if self.owns[g] is not None:
            self.own_copy(g, place).wait()

    def middle(self, g):
        return pltpu.make_async_copy(
            self.sources[g].at[1 - self.y, 1, self.line.z], self.mids[g], self.sems[0].at[g, 1]
        )

    def across(self, g, offset):
        ys, yr = self.sems[1], self.sems[2]
        src, dst, place = self.sources[g], self.lands[g], self.line.at(offset)
        if offset > 1 or g not in RELAYED:
            src, dst = src.at[1 - self.y, :, place], dst.at[offset]
        else:
            src, dst = src.at[1 - self.y, 0, place], dst.at[offset, 0]
        return remote(src, dst, ys.at[g, offset], yr.at[g, offset], {"fy": 1 - self.y})

    def relayed(self, g):
        ys, yr = self.sems[1], self.sems[2]
        slot = self.line.nz
        return remote(
            self.mids[g], self.lands[g].at[0, 1], ys.at[g, slot], yr.at[g, slot], {"fy": 1 - self.y}
        )

    def extra(self, g):
        es, er = self.sems[3], self.sems[4]
        src = self.sources[g].at[1 - self.y, 1, self.line.at(1)]
        return remote(src, self.extras[g], es.at[g], er.at[g], {"ctx": self.line.partner(0)})

    def hop(self, g, offset):
        zs, zr = self.sems[5], self.sems[6]
        return remote(
            self.lands[g].at[offset],
            self.ins[g].at[offset - 1],
            zs.at[g, offset],
            zr.at[g, offset],
            {"ctx": self.line.partner(low_bit(offset))},
        )

    def swap(self, g, slot):
        cs, cr = self.sems[7], self.sems[8]
        return remote(
            self.totals[g].at[1 - self.c], self.outs[g].at[slot], cs.at[g], cr.at[g], {"pr": 1 - self.c}
        )

    def keep(self, g):
        return pltpu.make_async_copy(
            self.totals[g].at[self.c], self.outs[g].at[self.c], self.sems[0].at[g, 2]
        )

    def each_tile(self, g, body):
        block = self.lands[g].shape[2]
        rows = 32 if block % 32 == 0 else block
        per = block // rows

        def step(i, _):
            body(i // per, pl.ds(pl.multiple_of(lax.rem(i, per) * rows, 8), rows))
            return 0

        lax.fori_loop(0, 2 * per, step, 0)

    def start(self, g):
        self.fetch(g, 0)
        self.fetch(g, 1)
        if g in RELAYED:
            self.middle(g).start()
            self.extra(g).start()
            self.lands[g][1, 1] = jnp.zeros(self.lands[g].shape[2:], BF16)
        for offset in self.order:
            self.across(g, offset).start()

    def relay(self, g):
        self.middle(g).wait()
        self.extra(g).wait_recv()
        self.mids[g][...] = (
            self.mids[g][...].astype(F32) + self.extras[g][...].astype(F32)
        ).astype(BF16)
        self.relayed(g).start()

    def step(self, g, place):
        offset = self.order[place]
        land, into = self.lands[g], self.ins[g]
        self.fetched(g, place)
        self.across(g, offset).wait_recv()
        arrived = [offset ^ (1 << level) for level in range(low_bit(offset))]
        for other in arrived:
            self.hop(g, other).wait_recv()

        def add(k, rows):
            total = self.own(g, place, k, rows) + land[offset, k, rows].astype(F32)
            for other in arrived:
                total = total + into[other - 1, k, rows].astype(F32)
            land[offset, k, rows] = total.astype(BF16)

        self.each_tile(g, add)
        self.hop(g, offset).start()
        self.fetch(g, place + 2)

    def last(self, g):
        place = self.line.nz - 1
        land, into = self.lands[g], self.ins[g]
        total = self.totals[g]
        self.fetched(g, place)
        self.across(g, 0).wait_recv()
        if g in RELAYED:
            self.relayed(g).wait_recv()
        arrived = [1 << level for level in range(self.line.levels)]
        for other in arrived:
            self.hop(g, other).wait_recv()

        def add(k, rows):
            value = self.own(g, place, k, rows) + land[0, k, rows].astype(F32)
            for other in arrived:
                value = value + into[other - 1, k, rows].astype(F32)
            total[k, rows] = value

        self.each_tile(g, add)
        self.swap(g, self.c).start()
        self.keep(g).start()

    def finish(self, g):
        self.swap(g, 1 - self.c).wait_recv()
        self.swap(g, self.c).wait_send()
        self.keep(g).wait()
        if g in RELAYED:
            self.extra(g).wait_send()
            self.relayed(g).wait_send()
        for offset in self.order:
            self.across(g, offset).wait_send()
            if offset:
                self.hop(g, offset).wait_send()


def backward_kernel(nz, scale, *refs):
    operands = list(refs[1:23])
    layer_out, input_grad = refs[23:25]
    outs = refs[25:30]
    gains = refs[30]
    sources = (refs[0], refs[31], refs[32])
    fetched, scratch = refs[33 : 33 + len(LATER)], refs[33 + len(LATER) : -3]
    stage, stage_sems = refs[-3], refs[-2]
    fetch = {}
    for n, which in enumerate(LATER):
        fetch[which] = pltpu.make_async_copy(operands[which], fetched[n], refs[-1].at[n])
        operands[which] = fetched[n]
    (
        dx_part, out_part, residual, rows, upstream, full_gains, cos, sin, q_seg, k_seg,
        spread_mat, q_items, kv_all, mixed_wide, mixed_low, lse, w_qkv, w_out, normed,
        normed_mlp, gate_grad, up_grad,
    ) = operands
    kept = 3
    owns = (*scratch[:kept], None, None)
    lands, ins, totals = (scratch[kept + 5 * i : kept + 5 * i + 5] for i in range(3))
    mids, extras = ({g: ref} for g, ref in zip(RELAYED * 2, scratch[kept + 15 : kept + 17]))
    (
        o_part, qkv_part, core_send, core_land, x_send, x_land, back_rows, low_rows, grad_items,
        delta, dq, kv_send, kv_land, qkv_rows, gain_rows, kv_here,
    ) = scratch[kept + 17 : kept + 33]
    (
        loc, ys, yr, es, er, zs, zr, ss, sr, cs, cr, xs, xr, ns, nr, ks, kr, gs, gr, ts, tr, bs,
    ) = scratch[kept + 33 :]
    y = lax.axis_index("fy")
    c = lax.axis_index("pr")
    z = lax.axis_index("ctx")
    span, width = rows.shape
    chunk = width // 4
    half = 4 * DH
    sources = (*sources, o_part, qkv_part)
    line = Line(nz)
    scatter = Scatter(
        line, sources, owns, lands, ins, mids, extras, totals, outs,
        (loc, ys, yr, es, er, zs, zr, ss, sr),
    )
    greet(
        [
            ({"fy": 1 - y}, None),
            ({"pr": 1 - c}, None),
            ({"tp": 1 - lax.axis_index("tp")}, None),
        ]
        + [({"ctx": t}, z != t) for t in range(nz)],
        2 + nz,
    )
    for which in LATER:
        fetch[which].start()
    bufs = (core_send, core_land, x_send, x_land)
    sems = (cs, cr, xs, xr)
    def columns(i):
        return pl.ds(pl.multiple_of(i * chunk, LANES), chunk)

    def back_in(who, i):
        weights = w_qkv[i // 2, lax.rem(i, 2)].reshape(chunk, 2 * half)
        return dot(qkv_rows[who], weights, 1, 1)

    first = TokenSum(lambda who, i: dx_part[who, :, columns(i)], bufs, sems, 0)
    second = TokenSum(lambda who, i: out_part[who, :, columns(i)], bufs, sems, 1)
    third = TokenSum(back_in, bufs, sems, 2)
    swap = remote(low_rows.at[c], low_rows.at[c], ns.at[0], nr.at[0], {"pr": 1 - c})

    def residual_back():
        def one(i, sums):
            here = columns(i)
            first.arrived(i)
            grad = first.total(i)
            back_rows[:, here] = grad
            value = residual[:, here]
            return (
                sums[0] + jnp.sum(value * value, axis=1, keepdims=True),
                sums[1] + jnp.sum(grad * full_gains[1, :, here] * value, axis=1, keepdims=True),
            )

        zero = jnp.zeros((span, 1), F32)
        squares, inner_sum = lax.fori_loop(0, 4, one, (zero, zero))
        factor = lax.rsqrt(squares / width + EPS)
        slope = factor * factor * factor * (inner_sum / width)

        def two(i, _):
            here = columns(i)
            grad = back_rows[:, here]
            value = residual[:, here]
            gain_rows[1:2, here] = jnp.sum(grad * value * factor, axis=0, keepdims=True)
            back = (
                upstream[:, here].astype(F32)
                + factor * (grad * full_gains[1, :, here])
                - value * slope
            )
            back_rows[:, here] = back
            low_rows[c, :, here] = back.astype(BF16)
            return 0

        lax.fori_loop(0, 4, two, 0)
        first.drain()
        swap.start()

    def low_rows_in():
        remote(low_rows.at[1 - c], low_rows.at[1 - c], ns.at[0], nr.at[0], {"pr": 1 - c}).wait_recv()

    def heads_back():
        fetch[17].wait()
        fetch[14].wait()
        for b in range(2):

            def add(i, total, b=b):
                weights = w_out[i // 2, lax.rem(i, 2)].reshape(chunk, half)
                return total + dot(low_rows[b, :, columns(i)], weights)

            grads = lax.fori_loop(0, 4, add, jnp.zeros((span, half), F32))
            wide = dot(grads.astype(BF16), spread_mat[...]).astype(BF16)
            for k in range(2):
                for j in range(2):
                    head = 2 * k + j
                    grad_items[b * 2 + k, pl.ds(j * span, span)] = wide[
                        :, head * LANES : (head + 1) * LANES
                    ]

        def one(i, _):
            part = dot(low_rows[0, :, columns(i)], mixed_low[:span], 0, 0) + dot(
                low_rows[1, :, columns(i)], mixed_low[span:], 0, 0
            )
            o_part[i // 2, lax.rem(i, 2)] = part.astype(BF16).reshape(o_part.shape[2:])
            return 0

        lax.fori_loop(0, 4, one, 0)

    def deltas():
        fetch[13].wait()
        for i in range(4):
            delta[i] = jnp.broadcast_to(
                jnp.sum(grad_items[i].astype(F32) * mixed_wide[i], axis=1, keepdims=True),
                delta.shape[1:],
            )
        dq[...] = jnp.zeros_like(dq)
        load_start(0)

    slots = kv_send.shape[0]
    order = scatter.order

    def keys_hop(b, place):
        offset = order[place]
        return remote(
            kv_send.at[place % slots, b],
            kv_land.at[offset, b],
            ks.at[b, offset],
            kr.at[b, offset],
            {"ctx": line.partner(low_bit(offset))},
        )

    def keys_add(b, place, offset):
        remote(
            kv_send.at[place % slots, b],
            kv_land.at[offset, b],
            ks.at[b, offset],
            kr.at[b, offset],
            {"ctx": line.partner(low_bit(offset))},
        ).wait_recv()
        kv_send[place % slots, b] = (
            kv_send[place % slots, b].astype(F32) + kv_land[offset, b].astype(F32)
        ).astype(BF16)

    def load(place):
        block = line.at(order[place])
        return pltpu.make_async_copy(kv_all.at[block], kv_here.at[place % 2], bs.at[place % 2])

    def load_start(place):
        @pl.when(line.at(order[place]) <= z)
        def _():
            load(place).start()

    def back_block(place, diagonal):
        block, slot = line.at(order[place]), place % 2
        load(place).wait()

        def one(b, _):
            key_grads, value_grads = [], []
            wide_kv = dot(kv_here[slot, b], spread_mat[...]).astype(BF16)
            for k in range(2):
                item = b * 2 + k
                keys = wide_kv[:, k * LANES : (k + 1) * LANES]
                values = wide_kv[:, (2 + k) * LANES : (3 + k) * LANES]
                scores = dot(q_items[item], keys, 1, 1) * scale
                allowed = q_seg[b] == k_seg[b, block]
                if diagonal:
                    row = lax.broadcasted_iota(jnp.int32, scores.shape, 0)
                    column = lax.broadcasted_iota(jnp.int32, scores.shape, 1)
                    allowed = allowed & (lax.rem(row, span) >= column)
                probs = jnp.where(allowed, jnp.exp(scores - lse[item][:, :1]), 0.0)
                prob_grad = dot(grad_items[item], values, 1, 1)
                score_grad = (probs * (prob_grad - delta[item][:, :1])).astype(BF16)
                value_grads.append(dot(probs.astype(BF16), grad_items[item], 0, 0))
                key_grads.append(dot(score_grad, q_items[item], 0, 0) * scale)
                dq[item] += dot(score_grad, keys) * scale
            wide = jnp.concatenate(key_grads + value_grads, axis=1).astype(BF16)
            kv_send[place % slots, b] = dot(wide, spread_mat[...], 1, 1).astype(BF16)
            return 0

        lax.fori_loop(0, 2, one, 0)

    def keys_pass(place):
        offset = order[place]

        @pl.when(line.at(offset) <= z)
        def _():
            for b in range(2):
                for level in range(low_bit(offset)):
                    keys_add(b, place, offset ^ (1 << level))
                keys_hop(b, place).start()

    def keys_sent(place):
        @pl.when(line.at(order[place]) <= z)
        def _():
            for b in range(2):
                keys_hop(b, place).wait_send()

    final = nz - 1

    def attend_back(place):
        if place == 0:
            fetch[11].wait()
            fetch[15].wait()
        if place < final:
            load_start(place + 1)
        if place >= slots:
            keys_sent(place - slots)
        if place == final:
            back_block(final, True)
            return

        @pl.when(line.at(order[place]) <= z)
        def _():
            back_block(place, False)

        if low_bit(order[place]) == 0 or slots < nz:
            keys_pass(place)

    def keys_final():
        for level in range(line.levels):

            @pl.when(line.bits[level] == 0)
            def _(level=level):
                for b in range(2):
                    keys_add(b, final, 1 << level)

    def layer_rows():
        def one(i, _):
            second.arrived(i)
            layer_out[:, columns(i)] = (residual[:, columns(i)] + second.total(i)).astype(BF16)
            return 0

        lax.fori_loop(0, 4, one, 0)
        second.drain()

    def unrotated(field, b):
        turned = pltpu.roll(field, LANES // 2, 1)
        here = pl.ds(b * span, span)
        return (field * cos[here] - turned * sin[here]).astype(BF16)

    def qkv_back():
        fetch[18].wait()
        for b in range(2):
            heads = [
                unrotated(dq[b * 2 + k, pl.ds(j * span, span)], b) for k in range(2) for j in range(2)
            ]
            qkv_rows[b, :, :half] = dot(
                jnp.concatenate(heads, axis=1), spread_mat[...], 1, 1
            ).astype(BF16)
        for b in range(2):
            wide = dot(kv_send[final % slots, b], spread_mat[...])
            fields = [unrotated(wide[:, k * LANES : (k + 1) * LANES], b) for k in range(2)]
            fields += [wide[:, (2 + k) * LANES : (3 + k) * LANES].astype(BF16) for k in range(2)]
            qkv_rows[b, :, half:] = dot(
                jnp.concatenate(fields, axis=1), spread_mat[...], 1, 1
            ).astype(BF16)

        def one(i, _):
            part = dot(normed[0, :, columns(i)], qkv_rows[0], 0, 0) + dot(
                normed[1, :, columns(i)], qkv_rows[1], 0, 0
            )
            qkv_part[i // 2, lax.rem(i, 2)] = part.astype(BF16).reshape(qkv_part.shape[2:])
            return 0

        lax.fori_loop(0, 4, one, 0)

    mine = pltpu.make_async_copy(gain_rows, gains.at[y, c, z], ts.at[2])
    core_gain = remote(gains.at[y, c, z], gains.at[y, c, z], ts.at[1], tr.at[1], {"pr": 1 - c})
    gain_line = remote(gains.at[y], gains.at[y], ts.at[0], tr.at[0], {"fy": 1 - y})

    def gain_to(t):
        return remote(gains.at[y, :, z], gains.at[y, :, z], gs.at[t], gr.at[z], {"ctx": t})

    def gain_from(t):
        return remote(gains.at[y, :, t], gains.at[y, :, t], gs.at[t], gr.at[t], {"ctx": t})

    def input_back():
        fetch[3].wait()
        def one(i, sums):
            here = columns(i)
            third.arrived(i)
            value = rows[:, here].astype(F32)
            weighed = third.total(i) * full_gains[0, :, here] * value
            return (
                sums[0] + jnp.sum(value * value, axis=1, keepdims=True),
                sums[1] + jnp.sum(weighed, axis=1, keepdims=True),
            )

        zero = jnp.zeros((span, 1), F32)
        squares, inner_sum = lax.fori_loop(0, 4, one, (zero, zero))
        factor = lax.rsqrt(squares / width + EPS)
        slope = factor * factor * factor * (inner_sum / width)

        def two(i, _):
            here = columns(i)
            value = rows[:, here].astype(F32)
            grad = third.total(i)
            gain_rows[0:1, here] = jnp.sum(grad * value * factor, axis=0, keepdims=True)
            input_grad[:, here] = (
                back_rows[:, here] + factor * (grad * full_gains[0, :, here]) - value * slope
            ).astype(BF16)
            return 0

        lax.fori_loop(0, 4, two, 0)
        third.drain()
        mine.start()
        mine.wait()
        core_gain.start()
        remote(
            gains.at[y, 1 - c, z], gains.at[y, 1 - c, z], ts.at[1], tr.at[1], {"pr": 1 - c}
        ).wait_recv()
        for t in range(nz):

            @pl.when(z != t)
            def _(t=t):
                gain_to(t).start()

    def gains_in():
        for t in range(nz):

            @pl.when(z != t)
            def _(t=t):
                gain_from(t).wait_recv()

        gain_line.start()

    start, relay, step, last = scatter.start, scatter.relay, scatter.step, scatter.last

    def grow(g):
        if g == 2:
            fetch[19].wait()
        which = 19 + g
        fetch[which].wait()
        weight_grad(sources[g], normed_mlp, operands[which], stage, stage_sems)

    def start_sum(n):
        if n:
            fetch[(None, 1, 16)[n]].wait()
        (first, second, third)[n].start()

    if nz == 4:
        plan = [
            (start, 0), (start_sum, 0), (grow, 2), (start, 2), (step, 0, 0), (grow, 1),
            (step, 0, 1), (residual_back,),
            (step, 0, 2), (low_rows_in,), (heads_back,), (start, 3), (start, 1), (deltas,),
            (step, 2, 0), (attend_back, 0), (start_sum, 1), (step, 2, 1), (attend_back, 1),
            (attend_back, 2), (step, 3, 0), (step, 3, 1), (keys_pass, 2), (step, 2, 2),
            (attend_back, 3), (keys_final,), (layer_rows,), (qkv_back,), (start, 4),
            (step, 1, 0), (step, 3, 2), (step, 1, 1), (relay, 0), (start_sum, 2), (step, 1, 2),
            (step, 4, 0), (step, 4, 1), (input_back,), (last, 2), (step, 4, 2), (last, 0),
            (last, 1), (last, 3), (gains_in,), (last, 4),
        ]
    else:
        plan = [(start, 0), (start_sum, 0), (grow, 2), (start, 2), (grow, 1), (start, 1)]
        plan += [(residual_back,)]
        plan += [(low_rows_in,), (heads_back,), (start, 3), (deltas,)]
        plan += [(attend_back, place) for place in range(nz)]
        plan += [(keys_pass, place) for place in range(nz // 2, nz - 1) if nz <= 4]
        plan += [(start_sum, 1), (keys_final,), (layer_rows,), (qkv_back,), (start, 4)]
        plan += [(relay, g) for g in RELAYED] + [(start_sum, 2)]
        plan += [(step, g, place) for g in range(4) for place in range(nz - 1)]
        plan += [(input_back,), (gains_in,)] + [(step, 4, place) for place in range(nz - 1)]
        plan += [(last, g) for g in range(5)]
    for run, *which in plan:
        run(*which)
    remote(gains.at[1 - y], gains.at[1 - y], ts.at[0], tr.at[0], {"fy": 1 - y}).wait_recv()
    for g in range(5):
        scatter.finish(g)
    core_gain.wait_send()
    gain_line.wait_send()
    swap.wait_send()
    for t in range(nz):

        @pl.when(z != t)
        def _(t=t):
            gain_to(t).wait_send()

    for place in range(max(0, nz - slots), final):
        keys_sent(place)


def backward(down_grad, operands, ny, nz):
    dma = pltpu.SemaphoreType.DMA
    anywhere = pl.BlockSpec(memory_space=pl.ANY)
    vmem = pl.BlockSpec(memory_space=pltpu.VMEM)
    residual = operands[2]
    span, width = residual.shape
    chunk = width // 4
    block = down_grad.shape[3]
    half = 4 * DH
    wide = [down_grad.shape[4]] * 3 + [half, 2 * half]
    shape = jax.ShapeDtypeStruct
    out_shape = (
        [shape((span, width), BF16)] * 2
        + [shape((2, block, w), F32) for w in wide]
        + [shape((ny, 2, nz, 2, width), F32)]
        + [shape(down_grad.shape, BF16)] * 2
    )

    def bufs(lead, dtype=BF16):
        return [pltpu.VMEM(lead + (block, w), dtype) for w in wide]

    return pl.pallas_call(
        functools.partial(backward_kernel, nz, DH ** (-0.5)),
        out_shape=out_shape,
        in_specs=[anywhere] + [anywhere if n in (12, *LATER) else vmem for n in range(22)],
        out_specs=[vmem] * 2 + [anywhere] * 8,
        scratch_shapes=[pltpu.VMEM(operands[n].shape, operands[n].dtype) for n in LATER]
        + bufs((2, 2))[:3]
        + bufs((nz, 2))
        + bufs((nz - 1, 2))
        + bufs((2,), F32)
        + [pltpu.VMEM((block, wide[g]), BF16) for g in RELAYED * 2]
        + [
            pltpu.VMEM((ny, 2, nz, block, half), BF16),
            pltpu.VMEM((ny, 2, nz, block, 2 * half), BF16),
            pltpu.VMEM((4, span, chunk), BF16),
            pltpu.VMEM((2, 4, span, chunk), BF16),
            pltpu.VMEM((4, span, chunk), BF16),
            pltpu.VMEM((2, 4, span, chunk), BF16),
            pltpu.VMEM((span, width), F32),
            pltpu.VMEM((2, span, width), BF16),
            pltpu.VMEM((4, 2 * span, LANES), BF16),
            pltpu.VMEM((4, 2 * span, LANES), F32),
            pltpu.VMEM((4, 2 * span, LANES), F32),
            pltpu.VMEM((min(nz, 4), 2, span, half), BF16),
            pltpu.VMEM((nz, 2, span, half), BF16),
            pltpu.VMEM((2, span, 2 * half), BF16),
            pltpu.VMEM((2, width), F32),
            pltpu.VMEM((2, 2, span, half), BF16),
        ]
        + [dma((5, 5))]
        + [dma((5, nz + 1))] * 2
        + [dma((5,))] * 2
        + [dma((5, nz))] * 2
        + [dma((5,))] * 2
        + [dma((3, 4))] * 4
        + [dma((1,))] * 2
        + [dma((2, nz))] * 2
        + [dma((nz,))] * 2
        + [dma((3,)), dma((2,)), dma((2,))]
        + [pltpu.VMEM((2,) + down_grad.shape[2:], BF16), dma((2,)), dma((len(LATER),))],
        name="backward",
        compiler_params=pltpu.CompilerParams(
            collective_id=2, has_side_effects=True, vmem_limit_bytes=VMEM_LIMIT
        ),
    )(down_grad, *operands)


def join(halved):
    return jnp.concatenate([halved[0], halved[1]], axis=1)


def on_device(
    ny,
    nz,
    layer_input,
    segments,
    positions,
    attn_gain,
    query_proj,
    key_proj,
    value_proj,
    out_proj,
    mlp_gain,
    gate_proj,
    up_proj,
    down_proj,
    out_grad,
):
    _, span, width = layer_input.shape
    block = query_proj.shape[0]
    rows_per = span // LANES
    small = jnp.concatenate(
        [
            jnp.pad(attn_gain.astype(F32), (0, LANES - block))[None],
            jnp.pad(mlp_gain.astype(F32), (0, LANES - block))[None],
            segments.astype(F32).reshape(rows_per, LANES),
            jnp.zeros((6 - rows_per, LANES), F32),
        ]
    )
    lane = jnp.arange(LANES)[None]
    info = jnp.where(
        lane == 0, positions.reshape(span, 1).astype(F32), segments.reshape(span, 1).astype(F32)
    )
    freq_index = (lane % (LANES // 2)).astype(F32)
    freq = THETA ** (-2.0 * freq_index / DH)
    kv_half = key_proj.shape[1] // 2
    kv_proj = jnp.concatenate(
        [
            key_proj[:, :kv_half],
            value_proj[:, :kv_half],
            key_proj[:, kv_half:],
            value_proj[:, kv_half:],
        ],
        axis=1,
    )
    lane_from = jnp.arange(4 * DH)
    lane_to = lane_from // DH * LANES + lane_from % DH
    lane_to = jnp.where(lane_from % DH < DH // 2, lane_to, lane_to + LANES // 2 - DH // 2)
    spread_mat = (lane_to[:, None] == jnp.arange(4 * LANES)[None]).astype(BF16)
    rows = layer_input.reshape(span, width)
    upstream = out_grad.reshape(span, width)
    (
        w_qkv, w_out, q_items, kv_all, mixed_wide, mixed_low, row_lse, residual, normed_attn, dx_part,
        out_part, normed_mlp, gate_grad, up_grad, down_grad, cos_wide, sin_wide, q_seg, k_seg, full_gains,
    ) = forward(
        (query_proj, kv_proj, out_proj.T, gate_proj, up_proj, down_proj.T),
        rows, upstream, small, info, freq, spread_mat, ny, nz,
    )
    operands = (
        dx_part, out_part, residual, rows, upstream, full_gains, cos_wide, sin_wide, q_seg, k_seg,
        spread_mat, q_items, kv_all, mixed_wide, mixed_low, row_lse, w_qkv, w_out,
        normed_attn, normed_mlp, gate_grad, up_grad,
    )
    layer_output, input_grad, down_g, gate_g, up_g, out_g, qkv_g, gains_all, *_ = backward(
        down_grad, operands, ny, nz
    )
    gain_sum = jnp.sum(gains_all, axis=(0, 1, 2))
    y = lax.axis_index("fy")
    c = lax.axis_index("pr")
    z = lax.axis_index("ctx")
    place = ((y * 2 + c) * nz + z) * block
    gain_own = lax.dynamic_slice_in_dim(gain_sum, place, block, 1)
    q_width, kv_width = 4 * DH, 2 * DH
    return (
        layer_output.reshape(1, span, width),
        input_grad.reshape(1, span, width),
        gain_own[0],
        join(qkv_g[:, :, :q_width]),
        join(qkv_g[:, :, q_width : q_width + kv_width]),
        join(qkv_g[:, :, q_width + kv_width :]),
        join(out_g).T,
        gain_own[1],
        join(gate_g),
        join(up_g),
        join(down_g).T,
    )


def solution(mesh):
    sizes = mesh.shape
    ny, nz = sizes["fsdp"] // 2, sizes["ctx"]
    inner = Mesh(
        mesh.devices.reshape(ny, 2, nz, sizes["tp"]), ("fy", "pr", "ctx", "tp")
    )
    seqs = ("fy", "pr")
    rows = P(seqs, "ctx", None)
    marks = P(seqs, "ctx")
    gain = P(GROUP)
    tall = P(GROUP, "tp")
    wide = P("tp", GROUP)
    return jax.shard_map(
        functools.partial(on_device, ny, nz),
        mesh=inner,
        in_specs=(
            rows, marks, marks, gain, tall, tall, tall, wide, gain, tall, tall, wide, rows,
        ),
        out_specs=(rows, rows, gain, tall, tall, tall, wide, gain, tall, tall, wide),
        check_vma=False,
    )
```

```python
import functools

import jax
import jax.numpy as jnp
import numpy as np
from jax import lax
from jax.experimental import pallas as pl
from jax.experimental.pallas import tpu as pltpu
from jax.sharding import Mesh, PartitionSpec as P

HQ = 16
HK = 8
DH = 96


EPS = 1e-05
THETA = 100000.0
NEGATIVE = -1e30


def contract(left, right, left_dim, right_dim):
    return lax.dot_general(
        left, right, (((left_dim,), (right_dim,)), ((), ())), preferred_element_type=jnp.float32
    )


MESH_ID = pl.DeviceIdType.MESH
BF16 = jnp.bfloat16
F32 = jnp.float32
GROUP = ("fy", "pr", "ctx")
VMEM_LIMIT = 62 * 1024 * 1024
LANES = 128


def remote(src, dst, send_sem, recv_sem, device):
    return pltpu.make_async_remote_copy(
        src_ref=src,
        dst_ref=dst,
        send_sem=send_sem,
        recv_sem=recv_sem,
        device_id=device,
        device_id_type=MESH_ID,
    )


def greet(devices_and_conditions, count):
    barrier = pltpu.get_barrier_semaphore()
    for device, condition in devices_and_conditions:
        if condition is None:
            pl.semaphore_signal(barrier, inc=1, device_id=device, device_id_type=MESH_ID)
        else:

            @pl.when(condition)
            def _(device=device):
                pl.semaphore_signal(barrier, inc=1, device_id=device, device_id_type=MESH_ID)

    pl.semaphore_wait(barrier, count)


def dot(left, right, left_dim=1, right_dim=0):
    return lax.dot_general(
        left, right, (((left_dim,), (right_dim,)), ((), ())), preferred_element_type=F32
    )


def low_bit(number):
    return (number & -number).bit_length() - 1


class Line:
    def __init__(self, nz):
        self.nz, self.levels = nz, nz.bit_length() - 1
        self.z = lax.axis_index("ctx")
        self.bits = [lax.rem(self.z // (1 << level), 2) for level in range(self.levels)]

    def at(self, offset):
        place = self.z
        for level in range(self.levels):
            if offset >> level & 1:
                place = place + (1 << level) - (2 << level) * self.bits[level]
        return place

    def partner(self, level):
        return self.at(1 << level)


class Gather:
    def __init__(self, line, outs, zs, zr, ys, yr):
        self.line, self.outs = line, outs
        self.zs, self.zr, self.ys, self.yr = zs, zr, ys, yr
        self.y = lax.axis_index("fy")
        offsets = range(1, line.nz)
        self.arrivals = sorted(offsets, key=lambda offset: (-low_bit(offset), offset))

    def hop(self, g, offset, level):
        piece = self.outs[g].at[self.y, :, self.line.at(offset)]
        slot = offset + (1 << level)
        return remote(
            piece, piece, self.zs.at[g, slot], self.zr.at[g, slot], {"ctx": self.line.partner(level)}
        )

    def hop_from(self, g, offset):
        piece = self.outs[g].at[self.y, :, self.line.at(offset)]
        partner = self.line.partner(low_bit(offset))
        return remote(piece, piece, self.zs.at[g, offset], self.zr.at[g, offset], {"ctx": partner})

    def across(self, g, offset, row):
        piece = self.outs[g].at[row, :, self.line.at(offset)]
        return remote(
            piece, piece, self.ys.at[g, offset], self.yr.at[g, offset], {"fy": 1 - self.y}
        )

    def hops(self, offset):
        last = low_bit(offset) if offset else self.line.levels
        return reversed(range(last))

    def own_z(self, g):
        for level in self.hops(0):
            self.hop(g, 0, level).start()

    def own_y(self, g):
        self.across(g, 0, self.y).start()

    def step(self, g, offset):
        self.hop_from(g, offset).wait_recv()
        for level in self.hops(offset):
            self.hop(g, offset, level).start()
        self.across(g, offset, self.y).start()

    def finish(self, g):
        for offset in (0, *self.arrivals):
            self.across(g, offset, 1 - self.y).wait_recv()

    def drain(self, g):
        for offset in (0, *self.arrivals):
            for level in self.hops(offset):
                self.hop(g, offset, level).wait_send()
            self.across(g, offset, self.y).wait_send()


class TokenSum:
    def __init__(self, part, bufs, sems, n):
        self.part, self.n = part, n
        self.core_send, self.core_land, self.x_send, self.x_land = bufs
        self.cs, self.cr, self.xs, self.xr = sems
        self.c = lax.axis_index("pr")
        self.x = lax.axis_index("tp")

    def core(self, i):
        return remote(
            self.core_send.at[i],
            self.core_land.at[self.n % 2, i],
            self.cs.at[self.n, i],
            self.cr.at[self.n, i],
            {"pr": 1 - self.c},
        )

    def sideways(self, i):
        return remote(
            self.x_send.at[i],
            self.x_land.at[self.n % 2, i],
            self.xs.at[self.n, i],
            self.xr.at[self.n, i],
            {"tp": 1 - self.x},
        )

    def start(self):
        def give(i, _):
            self.core_send[i] = self.part(1 - self.c, i).astype(BF16)
            self.core(i).start()
            return 0

        def add(i, _):
            mine = self.part(self.c, i).astype(F32)
            self.core(i).wait_recv()
            self.x_send[i] = (mine + self.core_land[self.n % 2, i].astype(F32)).astype(BF16)
            self.sideways(i).start()
            return 0

        lax.fori_loop(0, 4, give, 0)
        lax.fori_loop(0, 4, add, 0)

    def arrived(self, i):
        self.sideways(i).wait_recv()

    def total(self, i):
        return self.x_send[i].astype(F32) + self.x_land[self.n % 2, i].astype(F32)

    def drain(self):
        for i in range(4):
            self.core(i).wait_send()
            self.sideways(i).wait_send()


def weight_grad(into, left, right, stage, sems):
    _, span, width = left.shape
    chunk = width // 4

    def stored_part(i):
        slot = lax.rem(i, 2)
        return pltpu.make_async_copy(stage.at[slot], into.at[i // 2, slot], sems.at[slot])

    def one(i, _):
        here = pl.ds(pl.multiple_of(i * chunk, LANES), chunk)
        part = dot(left[0, :, here], right[:span], 0, 0) + dot(left[1, :, here], right[span:], 0, 0)

        @pl.when(i > 1)
        def _():
            stored_part(i - 2).wait()

        stage[lax.rem(i, 2)] = part.astype(BF16).reshape(stage.shape[1:])
        stored_part(i).start()
        return 0

    lax.fori_loop(0, 4, one, 0)
    for i in (2, 3):
        stored_part(i).wait()


def forward_kernel(nz, items, scale, *refs):
    weights = refs[:6]
    rows, upstream, segments, positions, attn_gain, mlp_gain, freq = refs[6:13]
    stored = refs[13:28]
    down_grad = refs[28]
    cos, sin, q_seg, k_seg, gains = refs[29:34]
    made = refs[34:49]
    (
        w_qkv, w_out, q_out, kvu, mixed_out, mixed_low, lse_out, residual, normed, dx_part, out_part,
        normed_mlp, gate_grad, up_grad, spread_mat,
    ) = made
    (
        w_gate, w_up, w_down, acc, keys, values, top, core_send, core_land, x_send, x_land, smalls, info_both,
        rows_both, gate_pre, up_pre, upstream_both, hidden, stage, small, info,
    ) = refs[49:70]
    (
        loc, ps, pr, ws, wr, ts, tr, zs, zr, ys, yr, ks, kr, cs, cr, xs, xr, ns, nr, hs, gs,
    ) = refs[70:]

    def store(n):
        return pltpu.make_async_copy(made[n], stored[n], hs.at[n])

    outs = (w_qkv, w_out, w_gate, w_up, w_down)
    y = lax.axis_index("fy")
    c = lax.axis_index("pr")
    z = lax.axis_index("ctx")
    x = lax.axis_index("tp")
    span, width = rows.shape
    other_y, other_c, other_x = {"fy": 1 - y}, {"pr": 1 - c}, {"tp": 1 - x}
    line = Line(nz)
    gather = Gather(line, outs, zs, zr, ys, yr)
    chunk = width // 4
    half = w_out.shape[4]
    block = w_out.shape[3]
    late = (2, 3, 4)

    def columns(i):
        return pl.ds(pl.multiple_of(i * chunk, LANES), chunk)

    small[...] = jnp.zeros_like(small)
    small[0:1, :block] = attn_gain[...].astype(F32)
    small[1:2, :block] = mlp_gain[...].astype(F32)
    square = (LANES, LANES)
    for part in range(span // LANES):
        here = pl.ds(part * LANES, LANES)
        segment = segments[:, here].astype(F32)
        position = positions[:, here].astype(F32)
        small[2 + part : 3 + part] = segment
        lane = lax.broadcasted_iota(jnp.int32, square, 1)
        info[here] = jnp.where(
            lane == 0,
            jnp.transpose(jnp.broadcast_to(position, square)),
            jnp.transpose(jnp.broadcast_to(segment, square)),
        )

    greet(
        [(other_y, None), (other_c, None), (other_x, None)]
        + [({"ctx": line.at(offset)}, None) for offset in range(1, nz)],
        2 + nz,
    )

    places = [(0, 0, half), (0, half, half), (1, 0, half)]
    places += [(g, 0, outs[g].shape[4]) for g in late]

    def half_of(n, which):
        size = places[n][2]
        return weights[n].at[:, pl.ds(pl.multiple_of(which * size, LANES), size)]

    def piece_of(n):
        g, first, size = places[n]
        return outs[g].at[y, c, z, :, pl.ds(first, size)]

    def other_piece(n):
        g, first, size = places[n]
        return outs[g].at[y, 1 - c, z, :, pl.ds(first, size)]

    moved = [(rows, rows_both), (upstream, upstream_both), (info, info_both)]
    local = [pltpu.make_async_copy(half_of(n, c), piece_of(n), loc.at[n]) for n in range(6)]
    local += [
        pltpu.make_async_copy(src, dst.at[c], loc.at[6 + n]) for n, (src, dst) in enumerate(moved)
    ]
    sent = [
        remote(half_of(n, 1 - c), piece_of(n), ps.at[n], pr.at[n], other_c) for n in range(6)
    ]
    sent += [
        remote(src, dst.at[c], ps.at[6 + n], pr.at[6 + n], other_c)
        for n, (src, dst) in enumerate(moved)
    ]
    landed = [
        remote(half_of(n, 1 - c), other_piece(n), ps.at[n], pr.at[n], other_c) for n in range(6)
    ]
    landed += [
        remote(src, dst.at[1 - c], ps.at[6 + n], pr.at[6 + n], other_c)
        for n, (src, dst) in enumerate(moved)
    ]

    def small_to(offset):
        return remote(
            small, smalls.at[y, c, z], ws.at[offset], wr.at[offset], {"ctx": line.at(offset)}
        )

    def small_from(offset):
        return remote(
            small, smalls.at[y, c, line.at(offset)], ws.at[offset], wr.at[offset],
            {"ctx": line.at(offset)},
        )

    small_here = pltpu.make_async_copy(small, smalls.at[y, c, z], loc.at[9])
    small_here.start()
    for n in range(3):
        local[n].start()
        sent[n].start()
    for offset in range(1, nz):
        small_to(offset).start()
    for n in (6, 8, 3, 4, 5, 7):
        local[n].start()
        sent[n].start()
    for n in range(2):
        local[n].wait()
        landed[n].wait_recv()
    gather.own_z(0)
    small_here.wait()
    for offset in range(1, nz):
        small_from(offset).wait_recv()
    small_line = remote(smalls.at[y, c], smalls.at[y, c], ts.at[0], tr.at[0], other_y)
    small_line.start()
    small_plane = remote(smalls.at[:, c], smalls.at[:, c], ts.at[1], tr.at[1], other_c)
    gather.own_y(0)
    for n in (5, 4, 2, 3):
        local[n].wait()
        landed[n].wait_recv()

    def prepare():
        row = lax.broadcasted_iota(jnp.int32, spread_mat.shape, 0)
        column = lax.broadcasted_iota(jnp.int32, spread_mat.shape, 1)
        head = sum((row >= k * DH).astype(jnp.int32) for k in range(1, 4))
        row = row - head * DH
        row = row + head * LANES + jnp.where(row >= DH // 2, LANES // 2 - DH // 2, 0)
        spread_mat[...] = jnp.where(row == column, 1.0, 0.0).astype(BF16)
        store(14).start()
        remote(smalls.at[1 - y, c], smalls.at[1 - y, c], ts.at[0], tr.at[0], other_y).wait_recv()
        small_plane.start()
        for n in (6, 7, 8):
            local[n].wait()
            landed[n].wait_recv()
        factors = []
        for b in range(2):
            value = rows_both[b].astype(F32)
            factors.append(lax.rsqrt(jnp.sum(value * value, axis=1, keepdims=True) / width + EPS))
            angles = info_both[b, :, 0:1] * freq[...]
            lane = lax.broadcasted_iota(jnp.int32, (span, LANES), 1)
            used = lax.rem(lane, LANES // 2) < DH // 2
            here = pl.ds(b * span, span)
            cos[here] = jnp.where(used, jnp.cos(angles), 0.0)
            turn = jnp.where(used, jnp.sin(angles), 0.0)
            sin[here] = jnp.where(lane < LANES // 2, -turn, turn)
            for j in range(2):
                q_seg[b, pl.ds(j * span, span)] = info_both[b, :, 1:2]
        remote(smalls.at[:, 1 - c], smalls.at[:, 1 - c], ts.at[1], tr.at[1], other_c).wait_recv()
        per = span // LANES
        for b in range(2):
            for j in range(nz):
                for part in range(per):
                    k_seg[b, j, :, pl.ds(part * LANES, LANES)] = smalls[
                        y, b, j, pl.ds(2 + part, 1)
                    ]
        for which in range(2):
            gain_row = jnp.zeros((1, width), F32)
            blank = jnp.zeros((1, width - LANES), F32)
            for n in range(4 * nz):
                own = smalls[n // (2 * nz), n // nz % 2, n % nz, pl.ds(which, 1)]
                wide = jnp.concatenate([own, blank], axis=1)
                gain_row = gain_row + (pltpu.roll(wide, n * block, 1) if n else wide)
            gains[which] = gain_row
        for b in range(2):
            normed[b] = (rows_both[b].astype(F32) * factors[b] * gains[0]).astype(BF16)
        store(8).start()

    def head_fields():
        acc[...] = jnp.zeros_like(acc)

        def one(i, _):
            part = w_qkv[i // 2, lax.rem(i, 2)].reshape(chunk, 2 * half)
            wide = jnp.concatenate(
                [
                    dot(part[:, :half], spread_mat[...]).astype(BF16),
                    dot(part[:, half:], spread_mat[...]).astype(BF16),
                ],
                axis=1,
            )
            for b in range(2):
                acc[pl.ds(b * span, span)] += dot(normed[b, :, columns(i)], wide)
            return 0

        lax.fori_loop(0, 4, one, 0)

    def rotated(b, lane):
        here = pl.ds(b * span, span)
        field = acc[here, pl.ds(lane * LANES, LANES)]
        turned = pltpu.roll(field, LANES // 2, 1)
        return (field * cos[here] + turned * sin[here]).astype(BF16)

    def keys_hop(b, offset, level):
        piece = kvu.at[line.at(offset), b]
        slot = offset + (1 << level)
        return remote(
            piece, piece, ks.at[b, slot], kr.at[b, slot], {"ctx": line.partner(level)}
        )

    def keys_from(b, offset):
        piece = kvu.at[line.at(offset), b]
        partner = line.partner(low_bit(offset))
        return remote(piece, piece, ks.at[b, offset], kr.at[b, offset], {"ctx": partner})

    def each_hop(offset, act):
        for level in gather.hops(offset):

            @pl.when(line.at(offset) <= line.partner(level))
            def _(level=level):
                act(level)

    def project_heads():
        head_fields()
        for b in range(2):
            fields = []
            for k in range(2):
                keys[b * 2 + k] = rotated(b, 4 + k)
                fields.append(keys[b * 2 + k])
            for k in range(2):
                values[b * 2 + k] = acc[
                    pl.ds(b * span, span), pl.ds((6 + k) * LANES, LANES)
                ].astype(BF16)
                fields.append(values[b * 2 + k])
            kvu[z, b] = dot(jnp.concatenate(fields, axis=1), spread_mat[...], 1, 1).astype(BF16)
            each_hop(0, lambda level, b=b: keys_hop(b, 0, level).start())

        for b in range(2):
            for k in range(2):
                for j in range(2):
                    q_out[b * 2 + k, pl.ds(j * span, span)] = rotated(b, 2 * k + j)

    def attend(there, first):
        def one(n, _):
            i = n // 2
            b = i // 2
            here = pl.ds(pl.multiple_of(lax.rem(n, 2) * span, span), span)
            scores = dot(q_out[i, here], keys[i], 1, 1) * scale
            allowed = q_seg[b, :span] == k_seg[b, there]
            if first:
                row = lax.broadcasted_iota(jnp.int32, scores.shape, 0)
                column = lax.broadcasted_iota(jnp.int32, scores.shape, 1)
                allowed = allowed & (row >= column)
            scores = jnp.where(allowed, scores, NEGATIVE)
            peak = jnp.max(scores, axis=1, keepdims=True)
            if first:
                probs = jnp.exp(scores - peak)
                total = jnp.sum(probs, axis=1, keepdims=True)
                mixed_out[i, here] = dot(probs.astype(BF16), values[i])
            else:
                old = top[i, here][:, :1]
                peak = jnp.maximum(old, peak)
                keep = jnp.exp(old - peak)
                probs = jnp.exp(scores - peak)
                total = keep * lse_out[i, here][:, :1] + jnp.sum(probs, axis=1, keepdims=True)
                mixed_out[i, here] = keep * mixed_out[i, here] + dot(
                    probs.astype(BF16), values[i]
                )
            top[i, here] = jnp.broadcast_to(peak, (span, LANES))
            lse_out[i, here] = jnp.broadcast_to(total, (span, LANES))
            return 0

        lax.fori_loop(0, 2 * items, one, 0)

    def attend_own():
        attend(z, True)

    def keys_in(offset):
        @pl.when(line.at(offset) <= z)
        def _():
            for b in range(2):
                keys_from(b, offset).wait_recv()
                each_hop(offset, lambda level, b=b: keys_hop(b, offset, level).start())

    def attend_at(offset):
        there = line.at(offset)

        @pl.when(there <= z)
        def _():
            for b in range(2):
                wide = dot(kvu[there, b], spread_mat[...]).astype(BF16)
                for k in range(2):
                    keys[b * 2 + k] = wide[:, k * LANES : (k + 1) * LANES]
                    values[b * 2 + k] = wide[:, (2 + k) * LANES : (3 + k) * LANES]
            attend(there, False)

    def close():
        def divide(i, _):
            total = lse_out[i]
            mixed_out[i] = mixed_out[i] / total
            lse_out[i] = top[i] + jnp.log(total)
            return 0

        lax.fori_loop(0, items, divide, 0)
        for b in range(2):
            heads = [
                mixed_out[b * 2 + k, pl.ds(j * span, span)].astype(BF16)
                for k in range(2)
                for j in range(2)
            ]
            mixed_low[pl.ds(b * span, span)] = dot(
                jnp.concatenate(heads, axis=1), spread_mat[...], 1, 1
            ).astype(BF16)
        for n in (2, 3, 4, 5, 6):
            store(n).start()

    def projected(who, i):
        part = w_out[i // 2, lax.rem(i, 2)].reshape(chunk, half)
        return dot(mixed_low[pl.ds(pl.multiple_of(who * span, span), span)], part, 1, 1)

    token_sum = TokenSum(
        projected, (core_send, core_land, x_send, x_land), (cs, cr, xs, xr), 0
    )
    swap = remote(normed_mlp.at[c], normed_mlp.at[c], ns.at[0], nr.at[0], other_c)

    def add_residual():
        def one(i, _):
            token_sum.arrived(i)
            residual[:, columns(i)] = rows[:, columns(i)].astype(F32) + token_sum.total(i)
            return 0

        lax.fori_loop(0, 4, one, 0)
        store(7).start()

    def norm():
        def one(i, squares):
            total = residual[:, columns(i)]
            return squares + jnp.sum(total * total, axis=1, keepdims=True)

        squares = lax.fori_loop(0, 4, one, jnp.zeros((span, 1), F32))
        factor = lax.rsqrt(squares / width + EPS)

        def two(i, _):
            here = columns(i)
            normed_mlp[c, :, here] = (residual[:, here] * factor * gains[1, :, here]).astype(BF16)
            return 0

        lax.fori_loop(0, 4, two, 0)
        swap.start()

    def swapped():
        remote(normed_mlp.at[1 - c], normed_mlp.at[1 - c], ns.at[0], nr.at[0], other_c).wait_recv()

    size = 256
    blocks = w_gate.shape[4] // size

    def column_block(ref, n):
        part = ref[:, :, :, :, pl.ds(pl.multiple_of(n * size, size), size)]
        return part.reshape(width, size)

    def project(into, ref):
        def one(n, _):
            cols = pl.ds(pl.multiple_of(n * size, size), size)
            part = column_block(ref, n)
            for b in range(2):
                into[pl.ds(b * span, span), cols] = dot(normed_mlp[b], part)
            return 0

        lax.fori_loop(0, blocks, one, 0)

    def hidden_block(n, _):
        cols = pl.ds(pl.multiple_of(n * size, size), size)
        for b in range(2):
            here = pl.ds(b * span, span)
            gate = gate_pre[here, cols]
            hidden[here, cols] = (gate * jax.nn.sigmoid(gate) * up_pre[here, cols]).astype(BF16)
        return 0

    def grads_block(n, _):
        cols = pl.ds(pl.multiple_of(n * size, size), size)
        part = column_block(w_down, n)
        for b in range(2):
            here = pl.ds(b * span, span)
            back = dot(upstream_both[b], part)
            gate, up = gate_pre[here, cols], up_pre[here, cols]
            open_part = jax.nn.sigmoid(gate)
            gate_grad[here, cols] = (
                back * up * open_part * (1.0 + gate * (1.0 - open_part))
            ).astype(BF16)
            up_grad[here, cols] = (back * (gate * open_part)).astype(BF16)
        return 0

    def back_block(i, _):
        cols = pl.ds(pl.multiple_of(i * chunk, LANES), chunk)
        gate_part = w_gate[i // 2, lax.rem(i, 2)].reshape(chunk, blocks * size)
        up_part = w_up[i // 2, lax.rem(i, 2)].reshape(chunk, blocks * size)
        down_part = w_down[i // 2, lax.rem(i, 2)].reshape(chunk, blocks * size)
        for b in range(2):
            here = pl.ds(b * span, span)
            dx_part[b, :, cols] = (
                dot(gate_grad[here], gate_part, 1, 1) + dot(up_grad[here], up_part, 1, 1)
            ).astype(BF16)
            out_part[b, :, cols] = dot(hidden[here], down_part, 1, 1).astype(BF16)
        return 0

    own_z, own_y, step = gather.own_z, gather.own_y, gather.step

    def finish(g):
        gather.finish(g)
        if g < 2:
            store(g).start()

    start_sum = token_sum.start

    def gate():
        project(gate_pre, w_gate)

    def up():
        project(up_pre, w_up)

    def hide():
        lax.fori_loop(0, blocks, hidden_block, 0)
        weight_grad(down_grad, upstream_both, hidden, stage, gs)

    def grads():
        lax.fori_loop(0, blocks, grads_block, 0)
        for n in (11, 12, 13):
            store(n).start()

    def back_rows():
        lax.fori_loop(0, 4, back_block, 0)
        store(9).start()
        store(10).start()

    arrivals = gather.arrivals
    if nz == 4:
        plan = [
            (own_y, 4), (own_y, 3), (step, 0, 2), (own_y, 1), (own_z, 1), (prepare,), (own_z, 2),
            (step, 0, 1), (step, 0, 3), (step, 1, 2), (step, 1, 1), (own_z, 3), (step, 2, 2),
            (step, 2, 1), (finish, 0), (project_heads,), (step, 3, 1), (step, 1, 3),
            (step, 2, 3), (attend_own,), (keys_in, 2), (own_y, 2), (finish, 1), (own_z, 4),
            (attend_at, 2), (keys_in, 1), (step, 3, 2), (attend_at, 1), (keys_in, 3),
            (attend_at, 3), (close,), (step, 4, 2), (start_sum,), (step, 4, 1), (step, 3, 3),
            (add_residual,), (finish, 2), (norm,), (step, 4, 3), (finish, 3), (swapped,),
            (gate,), (up,), (hide,), (finish, 4), (grads,), (back_rows,),
        ]
    else:
        plan = [(own_z, 1), (own_y, 1), (prepare,)]
        plan += [(step, g, offset) for offset in arrivals for g in (0, 1)]
        plan += [(run, g) for g in late for run in (own_z, own_y)]
        plan += [(finish, 0), (project_heads,), (attend_own,)]
        plan += [(run, offset) for offset in arrivals for run in (keys_in, attend_at)]
        plan += [(close,), (finish, 1), (start_sum,)]
        plan += [(step, g, offset) for offset in arrivals for g in late]
        plan += [(add_residual,), (norm,), (swapped,), (finish, 2), (gate,), (finish, 3), (up,)]
        plan += [(hide,), (finish, 4), (grads,), (back_rows,)]
    for run, *which in plan:
        run(*which)

    for g in range(5):
        gather.drain(g)
    for b in range(2):
        each_hop(0, lambda level, b=b: keys_hop(b, 0, level).wait_send())
        for offset in gather.arrivals:

            @pl.when(line.at(offset) <= z)
            def _(b=b, offset=offset):
                each_hop(offset, lambda level: keys_hop(b, offset, level).wait_send())

    for n in range(15):
        store(n).wait()
    token_sum.drain()
    swap.wait_send()
    for copy in sent:
        copy.wait_send()
    small_line.wait_send()
    small_plane.wait_send()
    for offset in range(1, nz):
        small_to(offset).wait_send()


def forward(weights, rows, upstream, segments, positions, attn_gain, mlp_gain, freq, ny, nz):
    dma = pltpu.SemaphoreType.DMA
    vmem = pl.BlockSpec(memory_space=pltpu.VMEM)
    span, width = rows.shape
    block, half, wide = weights[0].shape[0], weights[0].shape[1] // 2, weights[3].shape[1] // 2
    items, q_rows, both = 4, 2 * span, 2 * span
    shape = jax.ShapeDtypeStruct
    chunk = width // 4
    anywhere = pl.BlockSpec(memory_space=pl.ANY)
    weight = (ny, 2, nz, block)
    made = [
        (weight + (2 * half,), BF16),
        (weight + (half,), BF16),
        ((items, q_rows, LANES), BF16),
        ((nz, 2, span, half), BF16),
        ((items, q_rows, LANES), F32),
        ((both, half), BF16),
        ((items, q_rows, LANES), F32),
        ((span, width), F32),
        ((2, span, width), BF16),
        ((2, span, width), BF16),
        ((2, span, width), BF16),
        ((2, span, width), BF16),
        ((both, wide), BF16),
        ((both, wide), BF16),
        ((half, 4 * LANES), BF16),
    ]
    out_shape = [shape(*each) for each in made] + [shape(weight + (wide,), BF16)]
    out_shape += [
        shape((both, LANES), F32),
        shape((both, LANES), F32),
        shape((2, q_rows, 1), F32),
        shape((2, nz, 1, span), F32),
        shape((2, 1, width), F32),
    ]
    return pl.pallas_call(
        functools.partial(forward_kernel, nz, items, DH ** (-0.5)),
        out_shape=out_shape,
        in_specs=[vmem] * 13,
        out_specs=[anywhere] * 16 + [vmem] * 5,
        scratch_shapes=[pltpu.VMEM(*each) for each in made]
        + [pltpu.VMEM(weight + (wide,), BF16)] * 3
        + [
            pltpu.VMEM((both, 8 * LANES), F32),
            pltpu.VMEM((items, span, LANES), BF16),
            pltpu.VMEM((items, span, LANES), BF16),
            pltpu.VMEM((items, q_rows, LANES), F32),
            pltpu.VMEM((4, span, chunk), BF16),
            pltpu.VMEM((1, 4, span, chunk), BF16),
            pltpu.VMEM((4, span, chunk), BF16),
            pltpu.VMEM((1, 4, span, chunk), BF16),
            pltpu.VMEM((ny, 2, nz, 8, LANES), F32),
            pltpu.VMEM((2, span, LANES), F32),
            pltpu.VMEM((2, span, width), BF16),
            pltpu.VMEM((both, wide), F32),
            pltpu.VMEM((both, wide), F32),
            pltpu.VMEM((2, span, width), BF16),
            pltpu.VMEM((both, wide), BF16),
            pltpu.VMEM((2, nz, block, wide), BF16),
            pltpu.VMEM((8, LANES), F32),
            pltpu.VMEM((span, LANES), F32),
        ]
        + [dma((10,)), dma((9,)), dma((9,)), dma((nz,)), dma((nz,)), dma((2,)), dma((2,))]
        + [dma((5, nz))] * 4
        + [dma((2, nz))] * 2
        + [dma((1, 4))] * 4
        + [dma((1,))] * 2
        + [dma((15,)), dma((2,))],
        name="forward",
        compiler_params=pltpu.CompilerParams(
            collective_id=1, has_side_effects=True, vmem_limit_bytes=VMEM_LIMIT
        ),
    )(*weights, rows, upstream, segments, positions, attn_gain, mlp_gain, freq)


RELAYED = (0,)
LATER = (19, 21, 20, 17, 14, 13, 11, 15, 1, 18, 16, 3)


class Scatter:
    def __init__(self, line, sources, owns, lands, ins, mids, extras, totals, outs, sems):
        self.line, self.sources, self.owns, self.lands = line, sources, owns, lands
        self.ins, self.mids, self.extras = ins, mids, extras
        self.totals, self.outs, self.sems = totals, outs, sems
        self.y = lax.axis_index("fy")
        self.c = lax.axis_index("pr")
        nz = line.nz
        self.order = sorted(range(1, nz), key=lambda offset: (low_bit(offset), -offset)) + [0]

    def own_copy(self, g, place):
        return pltpu.make_async_copy(
            self.sources[g].at[self.y, :, self.line.at(self.order[place])],
            self.owns[g].at[place % 2],
            self.sems[0].at[g, 3 + place % 2],
        )

    def own(self, g, place, k, rows):
        if self.owns[g] is None:
            place_at = self.line.at(self.order[place])
            return self.sources[g][self.y, k, place_at, rows].astype(F32)
        return self.owns[g][place % 2, k, rows].astype(F32)

    def fetch(self, g, place):
        if self.owns[g] is not None and place < self.line.nz:
            self.own_copy(g, place).start()

    def fetched(self, g, place):
        if self.owns[g] is not None:
            self.own_copy(g, place).wait()

    def middle(self, g):
        return pltpu.make_async_copy(
            self.sources[g].at[1 - self.y, 1, self.line.z], self.mids[g], self.sems[0].at[g, 1]
        )

    def across(self, g, offset):
        ys, yr = self.sems[1], self.sems[2]
        src, dst, place = self.sources[g], self.lands[g], self.line.at(offset)
        if offset > 1 or g not in RELAYED:
            src, dst = src.at[1 - self.y, :, place], dst.at[offset]
        else:
            src, dst = src.at[1 - self.y, 0, place], dst.at[offset, 0]
        return remote(src, dst, ys.at[g, offset], yr.at[g, offset], {"fy": 1 - self.y})

    def relayed(self, g):
        ys, yr = self.sems[1], self.sems[2]
        slot = self.line.nz
        return remote(
            self.mids[g], self.lands[g].at[0, 1], ys.at[g, slot], yr.at[g, slot], {"fy": 1 - self.y}
        )

    def extra(self, g):
        es, er = self.sems[3], self.sems[4]
        src = self.sources[g].at[1 - self.y, 1, self.line.at(1)]
        return remote(src, self.extras[g], es.at[g], er.at[g], {"ctx": self.line.partner(0)})

    def hop(self, g, offset):
        zs, zr = self.sems[5], self.sems[6]
        return remote(
            self.lands[g].at[offset],
            self.ins[g].at[offset - 1],
            zs.at[g, offset],
            zr.at[g, offset],
            {"ctx": self.line.partner(low_bit(offset))},
        )

    def swap(self, g, slot):
        cs, cr = self.sems[7], self.sems[8]
        return remote(
            self.totals[g].at[1 - self.c], self.outs[g].at[slot], cs.at[g], cr.at[g], {"pr": 1 - self.c}
        )

    def keep(self, g):
        return pltpu.make_async_copy(
            self.totals[g].at[self.c], self.outs[g].at[self.c], self.sems[0].at[g, 2]
        )

    def each_tile(self, g, body):
        block = self.lands[g].shape[2]
        rows = 32 if block % 32 == 0 else block
        per = block // rows

        def step(i, _):
            body(i // per, pl.ds(pl.multiple_of(lax.rem(i, per) * rows, 8), rows))
            return 0

        lax.fori_loop(0, 2 * per, step, 0)

    def start(self, g):
        self.fetch(g, 0)
        self.fetch(g, 1)
        if g in RELAYED:
            self.middle(g).start()
            self.extra(g).start()
            self.lands[g][1, 1] = jnp.zeros(self.lands[g].shape[2:], BF16)
        for offset in self.order:
            self.across(g, offset).start()

    def relay(self, g):
        self.middle(g).wait()
        self.extra(g).wait_recv()
        self.mids[g][...] = (
            self.mids[g][...].astype(F32) + self.extras[g][...].astype(F32)
        ).astype(BF16)
        self.relayed(g).start()

    def step(self, g, place):
        offset = self.order[place]
        land, into = self.lands[g], self.ins[g]
        self.fetched(g, place)
        self.across(g, offset).wait_recv()
        arrived = [offset ^ (1 << level) for level in range(low_bit(offset))]
        for other in arrived:
            self.hop(g, other).wait_recv()

        def add(k, rows):
            total = self.own(g, place, k, rows) + land[offset, k, rows].astype(F32)
            for other in arrived:
                total = total + into[other - 1, k, rows].astype(F32)
            land[offset, k, rows] = total.astype(BF16)

        self.each_tile(g, add)
        self.hop(g, offset).start()
        self.fetch(g, place + 2)

    def last(self, g):
        place = self.line.nz - 1
        land, into = self.lands[g], self.ins[g]
        total = self.totals[g]
        self.fetched(g, place)
        self.across(g, 0).wait_recv()
        if g in RELAYED:
            self.relayed(g).wait_recv()
        arrived = [1 << level for level in range(self.line.levels)]
        for other in arrived:
            self.hop(g, other).wait_recv()

        def add(k, rows):
            value = self.own(g, place, k, rows) + land[0, k, rows].astype(F32)
            for other in arrived:
                value = value + into[other - 1, k, rows].astype(F32)
            total[k, rows] = value

        self.each_tile(g, add)
        self.swap(g, self.c).start()
        self.keep(g).start()

    def finish(self, g):
        self.swap(g, 1 - self.c).wait_recv()
        self.swap(g, self.c).wait_send()
        self.keep(g).wait()
        if g in RELAYED:
            self.extra(g).wait_send()
            self.relayed(g).wait_send()
        for offset in self.order:
            self.across(g, offset).wait_send()
            if offset:
                self.hop(g, offset).wait_send()


def backward_kernel(nz, scale, *refs):
    operands = list(refs[1:23])
    layer_out, input_grad = refs[23:25]
    outs = refs[25:30]
    gains = refs[30]
    sources = (refs[0], refs[31], refs[32])
    fetched, scratch = refs[33 : 33 + len(LATER)], refs[33 + len(LATER) : -3]
    stage, stage_sems = refs[-3], refs[-2]
    fetch = {}
    for n, which in enumerate(LATER):
        fetch[which] = pltpu.make_async_copy(operands[which], fetched[n], refs[-1].at[n])
        operands[which] = fetched[n]
    (
        dx_part, out_part, residual, rows, upstream, full_gains, cos, sin, q_seg, k_seg,
        spread_mat, q_items, kv_all, mixed_wide, mixed_low, lse, w_qkv, w_out, normed,
        normed_mlp, gate_grad, up_grad,
    ) = operands
    kept = 3
    owns = (*scratch[:kept], None, None)
    lands, ins, totals = (scratch[kept + 5 * i : kept + 5 * i + 5] for i in range(3))
    mids, extras = ({g: ref} for g, ref in zip(RELAYED * 2, scratch[kept + 15 : kept + 17]))
    (
        o_part, qkv_part, core_send, core_land, x_send, x_land, back_rows, low_rows, grad_items,
        delta, dq, kv_send, kv_land, qkv_rows, gain_rows, kv_here,
    ) = scratch[kept + 17 : kept + 33]
    (
        loc, ys, yr, es, er, zs, zr, ss, sr, cs, cr, xs, xr, ns, nr, ks, kr, gs, gr, ts, tr, bs,
    ) = scratch[kept + 33 :]
    y = lax.axis_index("fy")
    c = lax.axis_index("pr")
    z = lax.axis_index("ctx")
    span, width = rows.shape
    chunk = width // 4
    half = 4 * DH
    sources = (*sources, o_part, qkv_part)
    line = Line(nz)
    scatter = Scatter(
        line, sources, owns, lands, ins, mids, extras, totals, outs,
        (loc, ys, yr, es, er, zs, zr, ss, sr),
    )
    greet(
        [
            ({"fy": 1 - y}, None),
            ({"pr": 1 - c}, None),
            ({"tp": 1 - lax.axis_index("tp")}, None),
        ]
        + [({"ctx": t}, z != t) for t in range(nz)],
        2 + nz,
    )
    for which in LATER:
        fetch[which].start()
    bufs = (core_send, core_land, x_send, x_land)
    sems = (cs, cr, xs, xr)
    def columns(i):
        return pl.ds(pl.multiple_of(i * chunk, LANES), chunk)

    def back_in(who, i):
        weights = w_qkv[i // 2, lax.rem(i, 2)].reshape(chunk, 2 * half)
        return dot(qkv_rows[who], weights, 1, 1)

    first = TokenSum(lambda who, i: dx_part[who, :, columns(i)], bufs, sems, 0)
    second = TokenSum(lambda who, i: out_part[who, :, columns(i)], bufs, sems, 1)
    third = TokenSum(back_in, bufs, sems, 2)
    swap = remote(low_rows.at[c], low_rows.at[c], ns.at[0], nr.at[0], {"pr": 1 - c})

    def residual_back():
        def one(i, sums):
            here = columns(i)
            first.arrived(i)
            grad = first.total(i)
            back_rows[:, here] = grad
            value = residual[:, here]
            return (
                sums[0] + jnp.sum(value * value, axis=1, keepdims=True),
                sums[1] + jnp.sum(grad * full_gains[1, :, here] * value, axis=1, keepdims=True),
            )

        zero = jnp.zeros((span, 1), F32)
        squares, inner_sum = lax.fori_loop(0, 4, one, (zero, zero))
        factor = lax.rsqrt(squares / width + EPS)
        slope = factor * factor * factor * (inner_sum / width)

        def two(i, _):
            here = columns(i)
            grad = back_rows[:, here]
            value = residual[:, here]
            gain_rows[1:2, here] = jnp.sum(grad * value * factor, axis=0, keepdims=True)
            back = (
                upstream[:, here].astype(F32)
                + factor * (grad * full_gains[1, :, here])
                - value * slope
            )
            back_rows[:, here] = back
            low_rows[c, :, here] = back.astype(BF16)
            return 0

        lax.fori_loop(0, 4, two, 0)
        first.drain()
        swap.start()

    def low_rows_in():
        remote(low_rows.at[1 - c], low_rows.at[1 - c], ns.at[0], nr.at[0], {"pr": 1 - c}).wait_recv()

    def heads_back():
        fetch[17].wait()
        fetch[14].wait()
        for b in range(2):

            def add(i, total, b=b):
                weights = w_out[i // 2, lax.rem(i, 2)].reshape(chunk, half)
                return total + dot(low_rows[b, :, columns(i)], weights)

            grads = lax.fori_loop(0, 4, add, jnp.zeros((span, half), F32))
            wide = dot(grads.astype(BF16), spread_mat[...]).astype(BF16)
            for k in range(2):
                for j in range(2):
                    head = 2 * k + j
                    grad_items[b * 2 + k, pl.ds(j * span, span)] = wide[
                        :, head * LANES : (head + 1) * LANES
                    ]

        def one(i, _):
            part = dot(low_rows[0, :, columns(i)], mixed_low[:span], 0, 0) + dot(
                low_rows[1, :, columns(i)], mixed_low[span:], 0, 0
            )
            o_part[i // 2, lax.rem(i, 2)] = part.astype(BF16).reshape(o_part.shape[2:])
            return 0

        lax.fori_loop(0, 4, one, 0)

    def deltas():
        fetch[13].wait()
        for i in range(4):
            delta[i] = jnp.broadcast_to(
                jnp.sum(grad_items[i].astype(F32) * mixed_wide[i], axis=1, keepdims=True),
                delta.shape[1:],
            )
        dq[...] = jnp.zeros_like(dq)
        load_start(0)

    slots = kv_send.shape[0]
    order = scatter.order

    def keys_hop(b, place):
        offset = order[place]
        return remote(
            kv_send.at[place % slots, b],
            kv_land.at[offset, b],
            ks.at[b, offset],
            kr.at[b, offset],
            {"ctx": line.partner(low_bit(offset))},
        )

    def keys_add(b, place, offset):
        remote(
            kv_send.at[place % slots, b],
            kv_land.at[offset, b],
            ks.at[b, offset],
            kr.at[b, offset],
            {"ctx": line.partner(low_bit(offset))},
        ).wait_recv()
        kv_send[place % slots, b] = (
            kv_send[place % slots, b].astype(F32) + kv_land[offset, b].astype(F32)
        ).astype(BF16)

    def load(place):
        block = line.at(order[place])
        return pltpu.make_async_copy(kv_all.at[block], kv_here.at[place % 2], bs.at[place % 2])

    def load_start(place):
        @pl.when(line.at(order[place]) <= z)
        def _():
            load(place).start()

    def back_block(place, diagonal):
        block, slot = line.at(order[place]), place % 2
        load(place).wait()

        def one(b, _):
            key_grads, value_grads = [], []
            wide_kv = dot(kv_here[slot, b], spread_mat[...]).astype(BF16)
            for k in range(2):
                item = b * 2 + k
                keys = wide_kv[:, k * LANES : (k + 1) * LANES]
                values = wide_kv[:, (2 + k) * LANES : (3 + k) * LANES]
                scores = dot(q_items[item], keys, 1, 1) * scale
                allowed = q_seg[b] == k_seg[b, block]
                if diagonal:
                    row = lax.broadcasted_iota(jnp.int32, scores.shape, 0)
                    column = lax.broadcasted_iota(jnp.int32, scores.shape, 1)
                    allowed = allowed & (lax.rem(row, span) >= column)
                probs = jnp.where(allowed, jnp.exp(scores - lse[item][:, :1]), 0.0)
                prob_grad = dot(grad_items[item], values, 1, 1)
                score_grad = (probs * (prob_grad - delta[item][:, :1])).astype(BF16)
                value_grads.append(dot(probs.astype(BF16), grad_items[item], 0, 0))
                key_grads.append(dot(score_grad, q_items[item], 0, 0) * scale)
                dq[item] += dot(score_grad, keys) * scale
            wide = jnp.concatenate(key_grads + value_grads, axis=1).astype(BF16)
            kv_send[place % slots, b] = dot(wide, spread_mat[...], 1, 1).astype(BF16)
            return 0

        lax.fori_loop(0, 2, one, 0)

    def keys_pass(place):
        offset = order[place]

        @pl.when(line.at(offset) <= z)
        def _():
            for b in range(2):
                for level in range(low_bit(offset)):
                    keys_add(b, place, offset ^ (1 << level))
                keys_hop(b, place).start()

    def keys_sent(place):
        @pl.when(line.at(order[place]) <= z)
        def _():
            for b in range(2):
                keys_hop(b, place).wait_send()

    final = nz - 1

    def attend_back(place):
        if place == 0:
            fetch[11].wait()
            fetch[15].wait()
        if place < final:
            load_start(place + 1)
        if place >= slots:
            keys_sent(place - slots)
        if place == final:
            back_block(final, True)
            return

        @pl.when(line.at(order[place]) <= z)
        def _():
            back_block(place, False)

        if low_bit(order[place]) == 0 or slots < nz:
            keys_pass(place)

    def keys_final():
        for level in range(line.levels):

            @pl.when(line.bits[level] == 0)
            def _(level=level):
                for b in range(2):
                    keys_add(b, final, 1 << level)

    def layer_rows():
        def one(i, _):
            second.arrived(i)
            layer_out[:, columns(i)] = (residual[:, columns(i)] + second.total(i)).astype(BF16)
            return 0

        lax.fori_loop(0, 4, one, 0)
        second.drain()

    def unrotated(field, b):
        turned = pltpu.roll(field, LANES // 2, 1)
        here = pl.ds(b * span, span)
        return (field * cos[here] - turned * sin[here]).astype(BF16)

    def qkv_back():
        fetch[18].wait()
        for b in range(2):
            heads = [
                unrotated(dq[b * 2 + k, pl.ds(j * span, span)], b) for k in range(2) for j in range(2)
            ]
            qkv_rows[b, :, :half] = dot(
                jnp.concatenate(heads, axis=1), spread_mat[...], 1, 1
            ).astype(BF16)
        for b in range(2):
            wide = dot(kv_send[final % slots, b], spread_mat[...])
            fields = [unrotated(wide[:, k * LANES : (k + 1) * LANES], b) for k in range(2)]
            fields += [wide[:, (2 + k) * LANES : (3 + k) * LANES].astype(BF16) for k in range(2)]
            qkv_rows[b, :, half:] = dot(
                jnp.concatenate(fields, axis=1), spread_mat[...], 1, 1
            ).astype(BF16)

        def one(i, _):
            part = dot(normed[0, :, columns(i)], qkv_rows[0], 0, 0) + dot(
                normed[1, :, columns(i)], qkv_rows[1], 0, 0
            )
            qkv_part[i // 2, lax.rem(i, 2)] = part.astype(BF16).reshape(qkv_part.shape[2:])
            return 0

        lax.fori_loop(0, 4, one, 0)

    mine = pltpu.make_async_copy(gain_rows, gains.at[y, c, z], ts.at[2])
    core_gain = remote(gains.at[y, c, z], gains.at[y, c, z], ts.at[1], tr.at[1], {"pr": 1 - c})
    gain_line = remote(gains.at[y], gains.at[y], ts.at[0], tr.at[0], {"fy": 1 - y})

    def gain_to(t):
        return remote(gains.at[y, :, z], gains.at[y, :, z], gs.at[t], gr.at[z], {"ctx": t})

    def gain_from(t):
        return remote(gains.at[y, :, t], gains.at[y, :, t], gs.at[t], gr.at[t], {"ctx": t})

    def input_back():
        fetch[3].wait()
        def one(i, sums):
            here = columns(i)
            third.arrived(i)
            value = rows[:, here].astype(F32)
            weighed = third.total(i) * full_gains[0, :, here] * value
            return (
                sums[0] + jnp.sum(value * value, axis=1, keepdims=True),
                sums[1] + jnp.sum(weighed, axis=1, keepdims=True),
            )

        zero = jnp.zeros((span, 1), F32)
        squares, inner_sum = lax.fori_loop(0, 4, one, (zero, zero))
        factor = lax.rsqrt(squares / width + EPS)
        slope = factor * factor * factor * (inner_sum / width)

        def two(i, _):
            here = columns(i)
            value = rows[:, here].astype(F32)
            grad = third.total(i)
            gain_rows[0:1, here] = jnp.sum(grad * value * factor, axis=0, keepdims=True)
            input_grad[:, here] = (
                back_rows[:, here] + factor * (grad * full_gains[0, :, here]) - value * slope
            ).astype(BF16)
            return 0

        lax.fori_loop(0, 4, two, 0)
        third.drain()
        mine.start()
        mine.wait()
        core_gain.start()
        remote(
            gains.at[y, 1 - c, z], gains.at[y, 1 - c, z], ts.at[1], tr.at[1], {"pr": 1 - c}
        ).wait_recv()
        for t in range(nz):

            @pl.when(z != t)
            def _(t=t):
                gain_to(t).start()

    def gains_in():
        for t in range(nz):

            @pl.when(z != t)
            def _(t=t):
                gain_from(t).wait_recv()

        gain_line.start()

    start, relay, step, last = scatter.start, scatter.relay, scatter.step, scatter.last

    def grow(g):
        if g == 2:
            fetch[19].wait()
        which = 19 + g
        fetch[which].wait()
        weight_grad(sources[g], normed_mlp, operands[which], stage, stage_sems)

    def start_sum(n):
        if n:
            fetch[(None, 1, 16)[n]].wait()
        (first, second, third)[n].start()

    if nz == 4:
        plan = [
            (start, 0), (start_sum, 0), (grow, 2), (start, 2), (step, 0, 0), (grow, 1),
            (step, 0, 1), (residual_back,),
            (step, 0, 2), (low_rows_in,), (heads_back,), (start, 3), (start, 1), (deltas,),
            (step, 2, 0), (attend_back, 0), (start_sum, 1), (step, 2, 1), (attend_back, 1),
            (attend_back, 2), (step, 3, 0), (step, 3, 1), (keys_pass, 2), (step, 2, 2),
            (attend_back, 3), (keys_final,), (layer_rows,), (qkv_back,), (start, 4),
            (step, 1, 0), (step, 3, 2), (step, 1, 1), (relay, 0), (start_sum, 2), (step, 1, 2),
            (step, 4, 0), (step, 4, 1), (input_back,), (last, 2), (step, 4, 2), (last, 0),
            (last, 1), (last, 3), (gains_in,), (last, 4),
        ]
    else:
        plan = [(start, 0), (start_sum, 0), (grow, 2), (start, 2), (grow, 1), (start, 1)]
        plan += [(residual_back,)]
        plan += [(low_rows_in,), (heads_back,), (start, 3), (deltas,)]
        plan += [(attend_back, place) for place in range(nz)]
        plan += [(keys_pass, place) for place in range(nz // 2, nz - 1) if nz <= 4]
        plan += [(start_sum, 1), (keys_final,), (layer_rows,), (qkv_back,), (start, 4)]
        plan += [(relay, g) for g in RELAYED] + [(start_sum, 2)]
        plan += [(step, g, place) for g in range(4) for place in range(nz - 1)]
        plan += [(input_back,), (gains_in,)] + [(step, 4, place) for place in range(nz - 1)]
        plan += [(last, g) for g in range(5)]
    for run, *which in plan:
        run(*which)
    remote(gains.at[1 - y], gains.at[1 - y], ts.at[0], tr.at[0], {"fy": 1 - y}).wait_recv()
    for g in range(5):
        scatter.finish(g)
    core_gain.wait_send()
    gain_line.wait_send()
    swap.wait_send()
    for t in range(nz):

        @pl.when(z != t)
        def _(t=t):
            gain_to(t).wait_send()

    for place in range(max(0, nz - slots), final):
        keys_sent(place)


def backward(down_grad, operands, ny, nz):
    dma = pltpu.SemaphoreType.DMA
    anywhere = pl.BlockSpec(memory_space=pl.ANY)
    vmem = pl.BlockSpec(memory_space=pltpu.VMEM)
    residual = operands[2]
    span, width = residual.shape
    chunk = width // 4
    block = down_grad.shape[3]
    half = 4 * DH
    wide = [down_grad.shape[4]] * 3 + [half, 2 * half]
    shape = jax.ShapeDtypeStruct
    out_shape = (
        [shape((span, width), BF16)] * 2
        + [shape((2, block, w), F32) for w in wide]
        + [shape((ny, 2, nz, 2, width), F32)]
        + [shape(down_grad.shape, BF16)] * 2
    )

    def bufs(lead, dtype=BF16):
        return [pltpu.VMEM(lead + (block, w), dtype) for w in wide]

    return pl.pallas_call(
        functools.partial(backward_kernel, nz, DH ** (-0.5)),
        out_shape=out_shape,
        in_specs=[anywhere] + [anywhere if n in (12, *LATER) else vmem for n in range(22)],
        out_specs=[vmem] * 2 + [anywhere] * 8,
        scratch_shapes=[pltpu.VMEM(operands[n].shape, operands[n].dtype) for n in LATER]
        + bufs((2, 2))[:3]
        + bufs((nz, 2))
        + bufs((nz - 1, 2))
        + bufs((2,), F32)
        + [pltpu.VMEM((block, wide[g]), BF16) for g in RELAYED * 2]
        + [
            pltpu.VMEM((ny, 2, nz, block, half), BF16),
            pltpu.VMEM((ny, 2, nz, block, 2 * half), BF16),
            pltpu.VMEM((4, span, chunk), BF16),
            pltpu.VMEM((2, 4, span, chunk), BF16),
            pltpu.VMEM((4, span, chunk), BF16),
            pltpu.VMEM((2, 4, span, chunk), BF16),
            pltpu.VMEM((span, width), F32),
            pltpu.VMEM((2, span, width), BF16),
            pltpu.VMEM((4, 2 * span, LANES), BF16),
            pltpu.VMEM((4, 2 * span, LANES), F32),
            pltpu.VMEM((4, 2 * span, LANES), F32),
            pltpu.VMEM((min(nz, 4), 2, span, half), BF16),
            pltpu.VMEM((nz, 2, span, half), BF16),
            pltpu.VMEM((2, span, 2 * half), BF16),
            pltpu.VMEM((2, width), F32),
            pltpu.VMEM((2, 2, span, half), BF16),
        ]
        + [dma((5, 5))]
        + [dma((5, nz + 1))] * 2
        + [dma((5,))] * 2
        + [dma((5, nz))] * 2
        + [dma((5,))] * 2
        + [dma((3, 4))] * 4
        + [dma((1,))] * 2
        + [dma((2, nz))] * 2
        + [dma((nz,))] * 2
        + [dma((3,)), dma((2,)), dma((2,))]
        + [pltpu.VMEM((2,) + down_grad.shape[2:], BF16), dma((2,)), dma((len(LATER),))],
        name="backward",
        compiler_params=pltpu.CompilerParams(
            collective_id=2, has_side_effects=True, vmem_limit_bytes=VMEM_LIMIT
        ),
    )(down_grad, *operands)


def on_device(
    ny,
    nz,
    layer_input,
    segments,
    positions,
    attn_gain,
    query_proj,
    key_proj,
    value_proj,
    out_proj,
    mlp_gain,
    gate_proj,
    up_proj,
    down_proj,
    out_grad,
):
    _, span, width = layer_input.shape
    block = query_proj.shape[0]
    freq_index = np.arange(LANES) % (LANES // 2)
    freq = jnp.asarray((THETA ** (-2.0 * freq_index / DH)).astype(np.float32)[None])
    kv_half = key_proj.shape[1] // 2
    kv_proj = jnp.concatenate(
        [
            key_proj[:, :kv_half],
            value_proj[:, :kv_half],
            key_proj[:, kv_half:],
            value_proj[:, kv_half:],
        ],
        axis=1,
    )
    rows = layer_input.reshape(span, width)
    upstream = out_grad.reshape(span, width)
    (
        w_qkv, w_out, q_items, kv_all, mixed_wide, mixed_low, row_lse, residual, normed_attn, dx_part,
        out_part, normed_mlp, gate_grad, up_grad, spread_mat, down_grad, cos_wide, sin_wide, q_seg, k_seg, full_gains,
    ) = forward(
        (query_proj, kv_proj, out_proj.T, gate_proj, up_proj, down_proj.T),
        rows, upstream, segments, positions, attn_gain.reshape(1, block), mlp_gain.reshape(1, block),
        freq, ny, nz,
    )
    operands = (
        dx_part, out_part, residual, rows, upstream, full_gains, cos_wide, sin_wide, q_seg, k_seg,
        spread_mat, q_items, kv_all, mixed_wide, mixed_low, row_lse, w_qkv, w_out,
        normed_attn, normed_mlp, gate_grad, up_grad,
    )
    layer_output, input_grad, down_g, gate_g, up_g, out_g, qkv_g, gains_all, *_ = backward(
        down_grad, operands, ny, nz
    )
    layer_output, input_grad, q_g, k_g, v_g, o_g, gate_g, up_g, down_g, attn_g, mlp_g = assemble(
        down_g, gate_g, up_g, out_g, qkv_g, gains_all, layer_output, input_grad, nz
    )
    return (
        layer_output.reshape(1, span, width),
        input_grad.reshape(1, span, width),
        attn_g.reshape(block),
        q_g,
        k_g,
        v_g,
        o_g.T,
        mlp_g.reshape(block),
        gate_g,
        up_g,
        down_g.T,
    )


def assemble_kernel(nz, down, gate, up, out, qkv, gains, layer, back, *refs):
    layer_out, back_out, q_out, k_out, v_out, o_out, gate_out, up_out, down_out, attn, mlp = refs
    layer_out[...] = layer[...]
    back_out[...] = back[...]
    for halves, whole in ((gate, gate_out), (up, up_out), (down, down_out), (out, o_out)):
        size = halves.shape[2]
        whole[:, :size] = halves[0]
        whole[:, size:] = halves[1]
    size = q_out.shape[1] // 2
    q_out[:, :size] = qkv[0, :, :size]
    q_out[:, size:] = qkv[1, :, :size]
    both = [qkv[which, :, size:] for which in range(2)]
    k_out[...] = jnp.concatenate([part[:, : size // 2] for part in both], axis=1)
    v_out[...] = jnp.concatenate([part[:, size // 2 :] for part in both], axis=1)
    block, width = attn.shape[1], gains.shape[4]
    total = gains[0, 0, 0]
    for n in range(1, 4 * nz):
        total = total + gains[n // (2 * nz), n // nz % 2, n % nz]
    place = ((lax.axis_index("fy") * 2 + lax.axis_index("pr")) * nz + lax.axis_index("ctx")) * block
    own = pltpu.roll(total, lax.rem(width - place, width), 1)
    attn[...] = own[0:1, :block]
    mlp[...] = own[1:2, :block]


def assemble(down, gate, up, out, qkv, gains, layer, back, nz):
    vmem = pl.BlockSpec(memory_space=pltpu.VMEM)
    shape = jax.ShapeDtypeStruct
    block = down.shape[1]
    size = out.shape[2]
    outs = [shape(layer.shape, BF16), shape(back.shape, BF16), shape((block, 2 * size), F32)]
    outs += [shape((block, size), F32)] * 2 + [shape((block, 2 * size), F32)]
    outs += [shape((block, 2 * down.shape[2]), F32)] * 3 + [shape((1, block), F32)] * 2
    return pl.pallas_call(
        functools.partial(assemble_kernel, nz),
        out_shape=outs,
        in_specs=[vmem] * 8,
        out_specs=[vmem] * len(outs),
        name="assemble",
        compiler_params=pltpu.CompilerParams(vmem_limit_bytes=VMEM_LIMIT),
    )(down, gate, up, out, qkv, gains, layer, back)


def solution(mesh):
    sizes = mesh.shape
    ny, nz = sizes["fsdp"] // 2, sizes["ctx"]
    inner = Mesh(
        mesh.devices.reshape(ny, 2, nz, sizes["tp"]), ("fy", "pr", "ctx", "tp")
    )
    seqs = ("fy", "pr")
    rows = P(seqs, "ctx", None)
    marks = P(seqs, "ctx")
    gain = P(GROUP)
    tall = P(GROUP, "tp")
    wide = P("tp", GROUP)
    return jax.shard_map(
        functools.partial(on_device, ny, nz),
        mesh=inner,
        in_specs=(
            rows, marks, marks, gain, tall, tall, tall, wide, gain, tall, tall, wide, rows,
        ),
        out_specs=(rows, rows, gain, tall, tall, tall, wide, gain, tall, tall, wide),
        check_vma=False,
    )
```

```python
import functools

import jax
import jax.numpy as jnp
import numpy as np
from jax import lax
from jax.experimental import pallas as pl
from jax.experimental.pallas import tpu as pltpu
from jax.sharding import Mesh, PartitionSpec as P

HQ = 16
HK = 8
DH = 96


EPS = 1e-05
THETA = 100000.0
NEGATIVE = -1e30


def contract(left, right, left_dim, right_dim):
    return lax.dot_general(
        left, right, (((left_dim,), (right_dim,)), ((), ())), preferred_element_type=jnp.float32
    )


MESH_ID = pl.DeviceIdType.MESH
BF16 = jnp.bfloat16
F32 = jnp.float32
GROUP = ("fy", "pr", "ctx")
VMEM_LIMIT = 62 * 1024 * 1024
LANES = 128


def remote(src, dst, send_sem, recv_sem, device):
    return pltpu.make_async_remote_copy(
        src_ref=src,
        dst_ref=dst,
        send_sem=send_sem,
        recv_sem=recv_sem,
        device_id=device,
        device_id_type=MESH_ID,
    )


def greet(devices_and_conditions, count):
    barrier = pltpu.get_barrier_semaphore()
    for device, condition in devices_and_conditions:
        if condition is None:
            pl.semaphore_signal(barrier, inc=1, device_id=device, device_id_type=MESH_ID)
        else:

            @pl.when(condition)
            def _(device=device):
                pl.semaphore_signal(barrier, inc=1, device_id=device, device_id_type=MESH_ID)

    pl.semaphore_wait(barrier, count)


def dot(left, right, left_dim=1, right_dim=0):
    return lax.dot_general(
        left, right, (((left_dim,), (right_dim,)), ((), ())), preferred_element_type=F32
    )


def low_bit(number):
    return (number & -number).bit_length() - 1


class Line:
    def __init__(self, nz):
        self.nz, self.levels = nz, nz.bit_length() - 1
        self.z = lax.axis_index("ctx")
        self.bits = [lax.rem(self.z // (1 << level), 2) for level in range(self.levels)]

    def at(self, offset):
        place = self.z
        for level in range(self.levels):
            if offset >> level & 1:
                place = place + (1 << level) - (2 << level) * self.bits[level]
        return place

    def partner(self, level):
        return self.at(1 << level)


class Gather:
    def __init__(self, line, outs, zs, zr, ys, yr):
        self.line, self.outs = line, outs
        self.zs, self.zr, self.ys, self.yr = zs, zr, ys, yr
        self.y = lax.axis_index("fy")
        offsets = range(1, line.nz)
        self.arrivals = sorted(offsets, key=lambda offset: (-low_bit(offset), offset))

    def hop(self, g, offset, level):
        piece = self.outs[g].at[self.y, :, self.line.at(offset)]
        slot = offset + (1 << level)
        return remote(
            piece, piece, self.zs.at[g, slot], self.zr.at[g, slot], {"ctx": self.line.partner(level)}
        )

    def hop_from(self, g, offset):
        piece = self.outs[g].at[self.y, :, self.line.at(offset)]
        partner = self.line.partner(low_bit(offset))
        return remote(piece, piece, self.zs.at[g, offset], self.zr.at[g, offset], {"ctx": partner})

    def across(self, g, offset, row):
        piece = self.outs[g].at[row, :, self.line.at(offset)]
        return remote(
            piece, piece, self.ys.at[g, offset], self.yr.at[g, offset], {"fy": 1 - self.y}
        )

    def hops(self, offset):
        last = low_bit(offset) if offset else self.line.levels
        return reversed(range(last))

    def own_z(self, g):
        for level in self.hops(0):
            self.hop(g, 0, level).start()

    def own_y(self, g):
        self.across(g, 0, self.y).start()

    def step(self, g, offset):
        self.hop_from(g, offset).wait_recv()
        for level in self.hops(offset):
            self.hop(g, offset, level).start()
        self.across(g, offset, self.y).start()

    def finish(self, g):
        for offset in (0, *self.arrivals):
            self.across(g, offset, 1 - self.y).wait_recv()

    def drain(self, g):
        for offset in (0, *self.arrivals):
            for level in self.hops(offset):
                self.hop(g, offset, level).wait_send()
            self.across(g, offset, self.y).wait_send()


class TokenSum:
    def __init__(self, part, bufs, sems, n):
        self.part, self.n = part, n
        self.core_send, self.core_land, self.x_send, self.x_land = bufs
        self.cs, self.cr, self.xs, self.xr = sems
        self.c = lax.axis_index("pr")
        self.x = lax.axis_index("tp")

    def core(self, i):
        return remote(
            self.core_send.at[i],
            self.core_land.at[self.n % 2, i],
            self.cs.at[self.n, i],
            self.cr.at[self.n, i],
            {"pr": 1 - self.c},
        )

    def sideways(self, i):
        return remote(
            self.x_send.at[i],
            self.x_land.at[self.n % 2, i],
            self.xs.at[self.n, i],
            self.xr.at[self.n, i],
            {"tp": 1 - self.x},
        )

    def start(self):
        def give(i, _):
            self.core_send[i] = self.part(1 - self.c, i).astype(BF16)
            self.core(i).start()
            return 0

        def add(i, _):
            mine = self.part(self.c, i).astype(F32)
            self.core(i).wait_recv()
            self.x_send[i] = (mine + self.core_land[self.n % 2, i].astype(F32)).astype(BF16)
            self.sideways(i).start()
            return 0

        lax.fori_loop(0, 4, give, 0)
        lax.fori_loop(0, 4, add, 0)

    def arrived(self, i):
        self.sideways(i).wait_recv()

    def total(self, i):
        return self.x_send[i].astype(F32) + self.x_land[self.n % 2, i].astype(F32)

    def drain(self):
        for i in range(4):
            self.core(i).wait_send()
            self.sideways(i).wait_send()


def weight_grad(into, left, right, stage, sems):
    _, span, width = left.shape
    chunk = width // 4

    def stored_part(i):
        slot = lax.rem(i, 2)
        return pltpu.make_async_copy(stage.at[slot], into.at[i // 2, slot], sems.at[slot])

    def one(i, _):
        here = pl.ds(pl.multiple_of(i * chunk, LANES), chunk)
        part = dot(left[0, :, here], right[:span], 0, 0) + dot(left[1, :, here], right[span:], 0, 0)

        @pl.when(i > 1)
        def _():
            stored_part(i - 2).wait()

        stage[lax.rem(i, 2)] = part.astype(BF16).reshape(stage.shape[1:])
        stored_part(i).start()
        return 0

    lax.fori_loop(0, 4, one, 0)
    for i in (2, 3):
        stored_part(i).wait()


def forward_kernel(nz, items, scale, *refs):
    query_w, key_w, value_w, *other_w = refs[:7]
    rows, upstream, segments, positions, attn_gain, mlp_gain, freq = refs[7:14]
    stored = refs[14:29]
    down_grad = refs[29]
    cos, sin, q_seg, k_seg, gains = refs[30:35]
    made = refs[35:50]
    (
        w_qkv, w_out, q_out, kvu, mixed_out, mixed_low, lse_out, residual, normed, dx_part, out_part,
        normed_mlp, gate_grad, up_grad, spread_mat,
    ) = made
    (
        w_gate, w_up, w_down, acc, keys, values, top, core_send, core_land, x_send, x_land, smalls, info_both,
        rows_both, gate_pre, up_pre, upstream_both, hidden, stage, small, info, kv_w,
    ) = refs[50:72]
    (
        loc, ps, pr, ws, wr, ts, tr, zs, zr, ys, yr, ks, kr, cs, cr, xs, xr, ns, nr, hs, gs,
    ) = refs[72:]

    def store(n):
        return pltpu.make_async_copy(made[n], stored[n], hs.at[n])

    outs = (w_qkv, w_out, w_gate, w_up, w_down)
    y = lax.axis_index("fy")
    c = lax.axis_index("pr")
    z = lax.axis_index("ctx")
    x = lax.axis_index("tp")
    span, width = rows.shape
    other_y, other_c, other_x = {"fy": 1 - y}, {"pr": 1 - c}, {"tp": 1 - x}
    line = Line(nz)
    gather = Gather(line, outs, zs, zr, ys, yr)
    chunk = width // 4
    half = w_out.shape[4]
    block = w_out.shape[3]
    late = (2, 3, 4)

    def columns(i):
        return pl.ds(pl.multiple_of(i * chunk, LANES), chunk)

    weights = (query_w, kv_w, *other_w)
    near = key_w.shape[1] // 2
    kv_w[...] = jnp.concatenate(
        [key_w[:, :near], value_w[:, :near], key_w[:, near:], value_w[:, near:]], axis=1
    )

    small[...] = jnp.zeros_like(small)
    small[0:1, :block] = attn_gain[...].astype(F32)
    small[1:2, :block] = mlp_gain[...].astype(F32)
    square = (LANES, LANES)
    for part in range(span // LANES):
        here = pl.ds(part * LANES, LANES)
        segment = segments[:, here].astype(F32)
        position = positions[:, here].astype(F32)
        small[2 + part : 3 + part] = segment
        lane = lax.broadcasted_iota(jnp.int32, square, 1)
        info[here] = jnp.where(
            lane == 0,
            jnp.transpose(jnp.broadcast_to(position, square)),
            jnp.transpose(jnp.broadcast_to(segment, square)),
        )

    greet(
        [(other_y, None), (other_c, None), (other_x, None)]
        + [({"ctx": line.at(offset)}, None) for offset in range(1, nz)],
        2 + nz,
    )

    places = [(0, 0, half), (0, half, half), (1, 0, half)]
    places += [(g, 0, outs[g].shape[4]) for g in late]

    def half_of(n, which):
        size = places[n][2]
        return weights[n].at[:, pl.ds(pl.multiple_of(which * size, LANES), size)]

    def piece_of(n):
        g, first, size = places[n]
        return outs[g].at[y, c, z, :, pl.ds(first, size)]

    def other_piece(n):
        g, first, size = places[n]
        return outs[g].at[y, 1 - c, z, :, pl.ds(first, size)]

    moved = [(rows, rows_both), (upstream, upstream_both), (info, info_both)]
    local = [pltpu.make_async_copy(half_of(n, c), piece_of(n), loc.at[n]) for n in range(6)]
    local += [
        pltpu.make_async_copy(src, dst.at[c], loc.at[6 + n]) for n, (src, dst) in enumerate(moved)
    ]
    sent = [
        remote(half_of(n, 1 - c), piece_of(n), ps.at[n], pr.at[n], other_c) for n in range(6)
    ]
    sent += [
        remote(src, dst.at[c], ps.at[6 + n], pr.at[6 + n], other_c)
        for n, (src, dst) in enumerate(moved)
    ]
    landed = [
        remote(half_of(n, 1 - c), other_piece(n), ps.at[n], pr.at[n], other_c) for n in range(6)
    ]
    landed += [
        remote(src, dst.at[1 - c], ps.at[6 + n], pr.at[6 + n], other_c)
        for n, (src, dst) in enumerate(moved)
    ]

    def small_to(offset):
        return remote(
            small, smalls.at[y, c, z], ws.at[offset], wr.at[offset], {"ctx": line.at(offset)}
        )

    def small_from(offset):
        return remote(
            small, smalls.at[y, c, line.at(offset)], ws.at[offset], wr.at[offset],
            {"ctx": line.at(offset)},
        )

    small_here = pltpu.make_async_copy(small, smalls.at[y, c, z], loc.at[9])
    small_here.start()
    for n in range(3):
        local[n].start()
        sent[n].start()
    for offset in range(1, nz):
        small_to(offset).start()
    for n in (6, 8, 3, 4, 5, 7):
        local[n].start()
        sent[n].start()
    for n in range(2):
        local[n].wait()
        landed[n].wait_recv()
    gather.own_z(0)
    small_here.wait()
    for offset in range(1, nz):
        small_from(offset).wait_recv()
    small_line = remote(smalls.at[y, c], smalls.at[y, c], ts.at[0], tr.at[0], other_y)
    small_line.start()
    small_plane = remote(smalls.at[:, c], smalls.at[:, c], ts.at[1], tr.at[1], other_c)
    gather.own_y(0)
    for n in (5, 4, 2, 3):
        local[n].wait()
        landed[n].wait_recv()

    def prepare():
        row = lax.broadcasted_iota(jnp.int32, spread_mat.shape, 0)
        column = lax.broadcasted_iota(jnp.int32, spread_mat.shape, 1)
        head = sum((row >= k * DH).astype(jnp.int32) for k in range(1, 4))
        row = row - head * DH
        row = row + head * LANES + jnp.where(row >= DH // 2, LANES // 2 - DH // 2, 0)
        spread_mat[...] = jnp.where(row == column, 1.0, 0.0).astype(BF16)
        store(14).start()
        remote(smalls.at[1 - y, c], smalls.at[1 - y, c], ts.at[0], tr.at[0], other_y).wait_recv()
        small_plane.start()
        for n in (6, 7, 8):
            local[n].wait()
            landed[n].wait_recv()
        factors = []
        for b in range(2):
            value = rows_both[b].astype(F32)
            factors.append(lax.rsqrt(jnp.sum(value * value, axis=1, keepdims=True) / width + EPS))
            angles = info_both[b, :, 0:1] * freq[...]
            lane = lax.broadcasted_iota(jnp.int32, (span, LANES), 1)
            used = lax.rem(lane, LANES // 2) < DH // 2
            here = pl.ds(b * span, span)
            cos[here] = jnp.where(used, jnp.cos(angles), 0.0)
            turn = jnp.where(used, jnp.sin(angles), 0.0)
            sin[here] = jnp.where(lane < LANES // 2, -turn, turn)
            for j in range(2):
                q_seg[b, pl.ds(j * span, span)] = info_both[b, :, 1:2]
        remote(smalls.at[:, 1 - c], smalls.at[:, 1 - c], ts.at[1], tr.at[1], other_c).wait_recv()
        per = span // LANES
        for b in range(2):
            for j in range(nz):
                for part in range(per):
                    k_seg[b, j, :, pl.ds(part * LANES, LANES)] = smalls[
                        y, b, j, pl.ds(2 + part, 1)
                    ]
        for which in range(2):
            gain_row = jnp.zeros((1, width), F32)
            blank = jnp.zeros((1, width - LANES), F32)
            for n in range(4 * nz):
                own = smalls[n // (2 * nz), n // nz % 2, n % nz, pl.ds(which, 1)]
                wide = jnp.concatenate([own, blank], axis=1)
                gain_row = gain_row + (pltpu.roll(wide, n * block, 1) if n else wide)
            gains[which] = gain_row
        for b in range(2):
            normed[b] = (rows_both[b].astype(F32) * factors[b] * gains[0]).astype(BF16)
        store(8).start()

    def head_fields():
        acc[...] = jnp.zeros_like(acc)

        def one(i, _):
            part = w_qkv[i // 2, lax.rem(i, 2)].reshape(chunk, 2 * half)
            wide = jnp.concatenate(
                [
                    dot(part[:, :half], spread_mat[...]).astype(BF16),
                    dot(part[:, half:], spread_mat[...]).astype(BF16),
                ],
                axis=1,
            )
            for b in range(2):
                acc[pl.ds(b * span, span)] += dot(normed[b, :, columns(i)], wide)
            return 0

        lax.fori_loop(0, 4, one, 0)

    def rotated(b, lane):
        here = pl.ds(b * span, span)
        field = acc[here, pl.ds(lane * LANES, LANES)]
        turned = pltpu.roll(field, LANES // 2, 1)
        return (field * cos[here] + turned * sin[here]).astype(BF16)

    def keys_hop(b, offset, level):
        piece = kvu.at[line.at(offset), b]
        slot = offset + (1 << level)
        return remote(
            piece, piece, ks.at[b, slot], kr.at[b, slot], {"ctx": line.partner(level)}
        )

    def keys_from(b, offset):
        piece = kvu.at[line.at(offset), b]
        partner = line.partner(low_bit(offset))
        return remote(piece, piece, ks.at[b, offset], kr.at[b, offset], {"ctx": partner})

    def each_hop(offset, act):
        for level in gather.hops(offset):

            @pl.when(line.at(offset) <= line.partner(level))
            def _(level=level):
                act(level)

    def project_heads():
        head_fields()
        for b in range(2):
            fields = []
            for k in range(2):
                keys[b * 2 + k] = rotated(b, 4 + k)
                fields.append(keys[b * 2 + k])
            for k in range(2):
                values[b * 2 + k] = acc[
                    pl.ds(b * span, span), pl.ds((6 + k) * LANES, LANES)
                ].astype(BF16)
                fields.append(values[b * 2 + k])
            kvu[z, b] = dot(jnp.concatenate(fields, axis=1), spread_mat[...], 1, 1).astype(BF16)
            each_hop(0, lambda level, b=b: keys_hop(b, 0, level).start())

        for b in range(2):
            for k in range(2):
                for j in range(2):
                    q_out[b * 2 + k, pl.ds(j * span, span)] = rotated(b, 2 * k + j)

    def attend(there, first):
        def one(n, _):
            i = n // 2
            b = i // 2
            here = pl.ds(pl.multiple_of(lax.rem(n, 2) * span, span), span)
            scores = dot(q_out[i, here], keys[i], 1, 1) * scale
            allowed = q_seg[b, :span] == k_seg[b, there]
            if first:
                row = lax.broadcasted_iota(jnp.int32, scores.shape, 0)
                column = lax.broadcasted_iota(jnp.int32, scores.shape, 1)
                allowed = allowed & (row >= column)
            scores = jnp.where(allowed, scores, NEGATIVE)
            peak = jnp.max(scores, axis=1, keepdims=True)
            if first:
                probs = jnp.exp(scores - peak)
                total = jnp.sum(probs, axis=1, keepdims=True)
                mixed_out[i, here] = dot(probs.astype(BF16), values[i])
            else:
                old = top[i, here][:, :1]
                peak = jnp.maximum(old, peak)
                keep = jnp.exp(old - peak)
                probs = jnp.exp(scores - peak)
                total = keep * lse_out[i, here][:, :1] + jnp.sum(probs, axis=1, keepdims=True)
                mixed_out[i, here] = keep * mixed_out[i, here] + dot(
                    probs.astype(BF16), values[i]
                )
            top[i, here] = jnp.broadcast_to(peak, (span, LANES))
            lse_out[i, here] = jnp.broadcast_to(total, (span, LANES))
            return 0

        lax.fori_loop(0, 2 * items, one, 0)

    def attend_own():
        attend(z, True)

    def keys_in(offset):
        @pl.when(line.at(offset) <= z)
        def _():
            for b in range(2):
                keys_from(b, offset).wait_recv()
                each_hop(offset, lambda level, b=b: keys_hop(b, offset, level).start())

    def attend_at(offset):
        there = line.at(offset)

        @pl.when(there <= z)
        def _():
            for b in range(2):
                wide = dot(kvu[there, b], spread_mat[...]).astype(BF16)
                for k in range(2):
                    keys[b * 2 + k] = wide[:, k * LANES : (k + 1) * LANES]
                    values[b * 2 + k] = wide[:, (2 + k) * LANES : (3 + k) * LANES]
            attend(there, False)

    def close():
        def divide(i, _):
            total = lse_out[i]
            mixed_out[i] = mixed_out[i] / total
            lse_out[i] = top[i] + jnp.log(total)
            return 0

        lax.fori_loop(0, items, divide, 0)
        for b in range(2):
            heads = [
                mixed_out[b * 2 + k, pl.ds(j * span, span)].astype(BF16)
                for k in range(2)
                for j in range(2)
            ]
            mixed_low[pl.ds(b * span, span)] = dot(
                jnp.concatenate(heads, axis=1), spread_mat[...], 1, 1
            ).astype(BF16)
        for n in (2, 3, 4, 5, 6):
            store(n).start()

    def projected(who, i):
        part = w_out[i // 2, lax.rem(i, 2)].reshape(chunk, half)
        return dot(mixed_low[pl.ds(pl.multiple_of(who * span, span), span)], part, 1, 1)

    token_sum = TokenSum(
        projected, (core_send, core_land, x_send, x_land), (cs, cr, xs, xr), 0
    )
    swap = remote(normed_mlp.at[c], normed_mlp.at[c], ns.at[0], nr.at[0], other_c)

    def add_residual():
        def one(i, _):
            token_sum.arrived(i)
            residual[:, columns(i)] = rows[:, columns(i)].astype(F32) + token_sum.total(i)
            return 0

        lax.fori_loop(0, 4, one, 0)
        store(7).start()

    def norm():
        def one(i, squares):
            total = residual[:, columns(i)]
            return squares + jnp.sum(total * total, axis=1, keepdims=True)

        squares = lax.fori_loop(0, 4, one, jnp.zeros((span, 1), F32))
        factor = lax.rsqrt(squares / width + EPS)

        def two(i, _):
            here = columns(i)
            normed_mlp[c, :, here] = (residual[:, here] * factor * gains[1, :, here]).astype(BF16)
            return 0

        lax.fori_loop(0, 4, two, 0)
        swap.start()

    def swapped():
        remote(normed_mlp.at[1 - c], normed_mlp.at[1 - c], ns.at[0], nr.at[0], other_c).wait_recv()

    size = 256
    blocks = w_gate.shape[4] // size

    def column_block(ref, n):
        part = ref[:, :, :, :, pl.ds(pl.multiple_of(n * size, size), size)]
        return part.reshape(width, size)

    def project(into, ref):
        def one(n, _):
            cols = pl.ds(pl.multiple_of(n * size, size), size)
            part = column_block(ref, n)
            for b in range(2):
                into[pl.ds(b * span, span), cols] = dot(normed_mlp[b], part)
            return 0

        lax.fori_loop(0, blocks, one, 0)

    def hidden_block(n, _):
        cols = pl.ds(pl.multiple_of(n * size, size), size)
        for b in range(2):
            here = pl.ds(b * span, span)
            gate = gate_pre[here, cols]
            hidden[here, cols] = (gate * jax.nn.sigmoid(gate) * up_pre[here, cols]).astype(BF16)
        return 0

    def grads_block(n, _):
        cols = pl.ds(pl.multiple_of(n * size, size), size)
        part = column_block(w_down, n)
        for b in range(2):
            here = pl.ds(b * span, span)
            back = dot(upstream_both[b], part)
            gate, up = gate_pre[here, cols], up_pre[here, cols]
            open_part = jax.nn.sigmoid(gate)
            gate_grad[here, cols] = (
                back * up * open_part * (1.0 + gate * (1.0 - open_part))
            ).astype(BF16)
            up_grad[here, cols] = (back * (gate * open_part)).astype(BF16)
        return 0

    def back_block(i, _):
        cols = pl.ds(pl.multiple_of(i * chunk, LANES), chunk)
        gate_part = w_gate[i // 2, lax.rem(i, 2)].reshape(chunk, blocks * size)
        up_part = w_up[i // 2, lax.rem(i, 2)].reshape(chunk, blocks * size)
        down_part = w_down[i // 2, lax.rem(i, 2)].reshape(chunk, blocks * size)
        for b in range(2):
            here = pl.ds(b * span, span)
            dx_part[b, :, cols] = (
                dot(gate_grad[here], gate_part, 1, 1) + dot(up_grad[here], up_part, 1, 1)
            ).astype(BF16)
            out_part[b, :, cols] = dot(hidden[here], down_part, 1, 1).astype(BF16)
        return 0

    own_z, own_y, step = gather.own_z, gather.own_y, gather.step

    def finish(g):
        gather.finish(g)
        if g < 2:
            store(g).start()

    start_sum = token_sum.start

    def gate():
        project(gate_pre, w_gate)

    def up():
        project(up_pre, w_up)

    def hide():
        lax.fori_loop(0, blocks, hidden_block, 0)
        weight_grad(down_grad, upstream_both, hidden, stage, gs)

    def grads():
        lax.fori_loop(0, blocks, grads_block, 0)
        for n in (11, 12, 13):
            store(n).start()

    def back_rows():
        lax.fori_loop(0, 4, back_block, 0)
        store(9).start()
        store(10).start()

    arrivals = gather.arrivals
    if nz == 4:
        plan = [
            (own_y, 3), (step, 0, 2), (step, 0, 1), (own_z, 1), (step, 0, 3), (step, 1, 2),
            (own_z, 2), (own_y, 4), (prepare,), (own_y, 2), (finish, 0), (own_y, 1),
            (project_heads,), (attend_own,), (step, 2, 1), (step, 1, 1), (step, 2, 2),
            (keys_in, 2), (own_z, 3), (step, 1, 3), (keys_in, 1), (attend_at, 2), (attend_at, 1),
            (step, 2, 3), (step, 3, 2), (keys_in, 3), (attend_at, 3), (step, 3, 1), (close,),
            (finish, 1), (own_z, 4), (start_sum,), (finish, 2), (step, 3, 3), (step, 4, 2),
            (add_residual,), (finish, 3), (step, 4, 1), (norm,), (swapped,), (gate,),
            (step, 4, 3), (up,), (hide,), (finish, 4), (grads,), (back_rows,),
        ]
    else:
        plan = [(own_z, 1), (own_y, 1), (prepare,)]
        plan += [(step, g, offset) for offset in arrivals for g in (0, 1)]
        plan += [(run, g) for g in late for run in (own_z, own_y)]
        plan += [(finish, 0), (project_heads,), (attend_own,)]
        plan += [(run, offset) for offset in arrivals for run in (keys_in, attend_at)]
        plan += [(close,), (finish, 1), (start_sum,)]
        plan += [(step, g, offset) for offset in arrivals for g in late]
        plan += [(add_residual,), (norm,), (swapped,), (finish, 2), (gate,), (finish, 3), (up,)]
        plan += [(hide,), (finish, 4), (grads,), (back_rows,)]
    for run, *which in plan:
        run(*which)

    for g in range(5):
        gather.drain(g)
    for b in range(2):
        each_hop(0, lambda level, b=b: keys_hop(b, 0, level).wait_send())
        for offset in gather.arrivals:

            @pl.when(line.at(offset) <= z)
            def _(b=b, offset=offset):
                each_hop(offset, lambda level: keys_hop(b, offset, level).wait_send())

    for n in range(15):
        store(n).wait()
    token_sum.drain()
    swap.wait_send()
    for copy in sent:
        copy.wait_send()
    small_line.wait_send()
    small_plane.wait_send()
    for offset in range(1, nz):
        small_to(offset).wait_send()


def forward(weights, rows, upstream, segments, positions, attn_gain, mlp_gain, freq, ny, nz):
    dma = pltpu.SemaphoreType.DMA
    vmem = pl.BlockSpec(memory_space=pltpu.VMEM)
    span, width = rows.shape
    block, half, wide = weights[0].shape[0], weights[0].shape[1] // 2, weights[4].shape[1] // 2
    items, q_rows, both = 4, 2 * span, 2 * span
    shape = jax.ShapeDtypeStruct
    chunk = width // 4
    anywhere = pl.BlockSpec(memory_space=pl.ANY)
    weight = (ny, 2, nz, block)
    made = [
        (weight + (2 * half,), BF16),
        (weight + (half,), BF16),
        ((items, q_rows, LANES), BF16),
        ((nz, 2, span, half), BF16),
        ((items, q_rows, LANES), F32),
        ((both, half), BF16),
        ((items, q_rows, LANES), F32),
        ((span, width), F32),
        ((2, span, width), BF16),
        ((2, span, width), BF16),
        ((2, span, width), BF16),
        ((2, span, width), BF16),
        ((both, wide), BF16),
        ((both, wide), BF16),
        ((half, 4 * LANES), BF16),
    ]
    out_shape = [shape(*each) for each in made] + [shape(weight + (wide,), BF16)]
    out_shape += [
        shape((both, LANES), F32),
        shape((both, LANES), F32),
        shape((2, q_rows, 1), F32),
        shape((2, nz, 1, span), F32),
        shape((2, 1, width), F32),
    ]
    return pl.pallas_call(
        functools.partial(forward_kernel, nz, items, DH ** (-0.5)),
        out_shape=out_shape,
        in_specs=[vmem] * 14,
        out_specs=[anywhere] * 16 + [vmem] * 5,
        scratch_shapes=[pltpu.VMEM(*each) for each in made]
        + [pltpu.VMEM(weight + (wide,), BF16)] * 3
        + [
            pltpu.VMEM((both, 8 * LANES), F32),
            pltpu.VMEM((items, span, LANES), BF16),
            pltpu.VMEM((items, span, LANES), BF16),
            pltpu.VMEM((items, q_rows, LANES), F32),
            pltpu.VMEM((4, span, chunk), BF16),
            pltpu.VMEM((1, 4, span, chunk), BF16),
            pltpu.VMEM((4, span, chunk), BF16),
            pltpu.VMEM((1, 4, span, chunk), BF16),
            pltpu.VMEM((ny, 2, nz, 8, LANES), F32),
            pltpu.VMEM((2, span, LANES), F32),
            pltpu.VMEM((2, span, width), BF16),
            pltpu.VMEM((both, wide), F32),
            pltpu.VMEM((both, wide), F32),
            pltpu.VMEM((2, span, width), BF16),
            pltpu.VMEM((both, wide), BF16),
            pltpu.VMEM((2, nz, block, wide), BF16),
            pltpu.VMEM((8, LANES), F32),
            pltpu.VMEM((span, LANES), F32),
            pltpu.VMEM((block, 2 * half), BF16),
        ]
        + [dma((10,)), dma((9,)), dma((9,)), dma((nz,)), dma((nz,)), dma((2,)), dma((2,))]
        + [dma((5, nz))] * 4
        + [dma((2, nz))] * 2
        + [dma((1, 4))] * 4
        + [dma((1,))] * 2
        + [dma((15,)), dma((2,))],
        name="forward",
        compiler_params=pltpu.CompilerParams(
            collective_id=1, has_side_effects=True, vmem_limit_bytes=VMEM_LIMIT
        ),
    )(*weights, rows, upstream, segments, positions, attn_gain, mlp_gain, freq)


RELAYED = (0,)
LATER = (19, 21, 20, 17, 14, 13, 11, 15, 1, 18, 16, 3)


class Scatter:
    def __init__(self, line, sources, owns, lands, ins, mids, extras, totals, outs, sems):
        self.line, self.sources, self.owns, self.lands = line, sources, owns, lands
        self.ins, self.mids, self.extras = ins, mids, extras
        self.totals, self.outs, self.sems = totals, outs, sems
        self.y = lax.axis_index("fy")
        self.c = lax.axis_index("pr")
        nz = line.nz
        self.order = sorted(range(1, nz), key=lambda offset: (low_bit(offset), -offset)) + [0]

    def own_copy(self, g, place):
        return pltpu.make_async_copy(
            self.sources[g].at[self.y, :, self.line.at(self.order[place])],
            self.owns[g].at[place % 2],
            self.sems[0].at[g, 3 + place % 2],
        )

    def own(self, g, place, k, rows):
        if self.owns[g] is None:
            place_at = self.line.at(self.order[place])
            return self.sources[g][self.y, k, place_at, rows].astype(F32)
        return self.owns[g][place % 2, k, rows].astype(F32)

    def fetch(self, g, place):
        if self.owns[g] is not None and place < self.line.nz:
            self.own_copy(g, place).start()

    def fetched(self, g, place):
        if self.owns[g] is not None:
            self.own_copy(g, place).wait()

    def middle(self, g):
        return pltpu.make_async_copy(
            self.sources[g].at[1 - self.y, 1, self.line.z], self.mids[g], self.sems[0].at[g, 1]
        )

    def across(self, g, offset):
        ys, yr = self.sems[1], self.sems[2]
        src, dst, place = self.sources[g], self.lands[g], self.line.at(offset)
        if offset > 1 or g not in RELAYED:
            src, dst = src.at[1 - self.y, :, place], dst.at[offset]
        else:
            src, dst = src.at[1 - self.y, 0, place], dst.at[offset, 0]
        return remote(src, dst, ys.at[g, offset], yr.at[g, offset], {"fy": 1 - self.y})

    def relayed(self, g):
        ys, yr = self.sems[1], self.sems[2]
        slot = self.line.nz
        return remote(
            self.mids[g], self.lands[g].at[0, 1], ys.at[g, slot], yr.at[g, slot], {"fy": 1 - self.y}
        )

    def extra(self, g):
        es, er = self.sems[3], self.sems[4]
        src = self.sources[g].at[1 - self.y, 1, self.line.at(1)]
        return remote(src, self.extras[g], es.at[g], er.at[g], {"ctx": self.line.partner(0)})

    def hop(self, g, offset):
        zs, zr = self.sems[5], self.sems[6]
        return remote(
            self.lands[g].at[offset],
            self.ins[g].at[offset - 1],
            zs.at[g, offset],
            zr.at[g, offset],
            {"ctx": self.line.partner(low_bit(offset))},
        )

    def swap(self, g, slot):
        cs, cr = self.sems[7], self.sems[8]
        return remote(
            self.totals[g].at[1 - self.c], self.outs[g].at[slot], cs.at[g], cr.at[g], {"pr": 1 - self.c}
        )

    def keep(self, g):
        return pltpu.make_async_copy(
            self.totals[g].at[self.c], self.outs[g].at[self.c], self.sems[0].at[g, 2]
        )

    def each_tile(self, g, body):
        block = self.lands[g].shape[2]
        rows = 32 if block % 32 == 0 else block
        per = block // rows

        def step(i, _):
            body(i // per, pl.ds(pl.multiple_of(lax.rem(i, per) * rows, 8), rows))
            return 0

        lax.fori_loop(0, 2 * per, step, 0)

    def start(self, g):
        self.fetch(g, 0)
        self.fetch(g, 1)
        if g in RELAYED:
            self.middle(g).start()
            self.extra(g).start()
            self.lands[g][1, 1] = jnp.zeros(self.lands[g].shape[2:], BF16)
        for offset in self.order:
            self.across(g, offset).start()

    def relay(self, g):
        self.middle(g).wait()
        self.extra(g).wait_recv()
        self.mids[g][...] = (
            self.mids[g][...].astype(F32) + self.extras[g][...].astype(F32)
        ).astype(BF16)
        self.relayed(g).start()

    def step(self, g, place):
        offset = self.order[place]
        land, into = self.lands[g], self.ins[g]
        self.fetched(g, place)
        self.across(g, offset).wait_recv()
        arrived = [offset ^ (1 << level) for level in range(low_bit(offset))]
        for other in arrived:
            self.hop(g, other).wait_recv()

        def add(k, rows):
            total = self.own(g, place, k, rows) + land[offset, k, rows].astype(F32)
            for other in arrived:
                total = total + into[other - 1, k, rows].astype(F32)
            land[offset, k, rows] = total.astype(BF16)

        self.each_tile(g, add)
        self.hop(g, offset).start()
        self.fetch(g, place + 2)

    def last(self, g):
        place = self.line.nz - 1
        land, into = self.lands[g], self.ins[g]
        total = self.totals[g]
        self.fetched(g, place)
        self.across(g, 0).wait_recv()
        if g in RELAYED:
            self.relayed(g).wait_recv()
        arrived = [1 << level for level in range(self.line.levels)]
        for other in arrived:
            self.hop(g, other).wait_recv()

        def add(k, rows):
            value = self.own(g, place, k, rows) + land[0, k, rows].astype(F32)
            for other in arrived:
                value = value + into[other - 1, k, rows].astype(F32)
            total[k, rows] = value

        self.each_tile(g, add)
        self.swap(g, self.c).start()
        self.keep(g).start()

    def finish(self, g):
        self.swap(g, 1 - self.c).wait_recv()
        self.swap(g, self.c).wait_send()
        self.keep(g).wait()
        if g in RELAYED:
            self.extra(g).wait_send()
            self.relayed(g).wait_send()
        for offset in self.order:
            self.across(g, offset).wait_send()
            if offset:
                self.hop(g, offset).wait_send()


def backward_kernel(nz, scale, *refs):
    operands = list(refs[1:23])
    layer_out, input_grad = refs[23:25]
    outs = refs[25:30]
    gains = refs[30]
    sources = (refs[0], refs[31], refs[32])
    fetched, scratch = refs[33 : 33 + len(LATER)], refs[33 + len(LATER) : -3]
    stage, stage_sems = refs[-3], refs[-2]
    fetch = {}
    for n, which in enumerate(LATER):
        fetch[which] = pltpu.make_async_copy(operands[which], fetched[n], refs[-1].at[n])
        operands[which] = fetched[n]
    (
        dx_part, out_part, residual, rows, upstream, full_gains, cos, sin, q_seg, k_seg,
        spread_mat, q_items, kv_all, mixed_wide, mixed_low, lse, w_qkv, w_out, normed,
        normed_mlp, gate_grad, up_grad,
    ) = operands
    kept = 3
    owns = (*scratch[:kept], None, None)
    lands, ins, totals = (scratch[kept + 5 * i : kept + 5 * i + 5] for i in range(3))
    mids, extras = ({g: ref} for g, ref in zip(RELAYED * 2, scratch[kept + 15 : kept + 17]))
    (
        o_part, qkv_part, core_send, core_land, x_send, x_land, back_rows, low_rows, grad_items,
        delta, dq, kv_send, kv_land, qkv_rows, gain_rows, kv_here,
    ) = scratch[kept + 17 : kept + 33]
    (
        loc, ys, yr, es, er, zs, zr, ss, sr, cs, cr, xs, xr, ns, nr, ks, kr, gs, gr, ts, tr, bs,
    ) = scratch[kept + 33 :]
    y = lax.axis_index("fy")
    c = lax.axis_index("pr")
    z = lax.axis_index("ctx")
    span, width = rows.shape
    chunk = width // 4
    half = 4 * DH
    sources = (*sources, o_part, qkv_part)
    line = Line(nz)
    scatter = Scatter(
        line, sources, owns, lands, ins, mids, extras, totals, outs,
        (loc, ys, yr, es, er, zs, zr, ss, sr),
    )
    greet(
        [
            ({"fy": 1 - y}, None),
            ({"pr": 1 - c}, None),
            ({"tp": 1 - lax.axis_index("tp")}, None),
        ]
        + [({"ctx": t}, z != t) for t in range(nz)],
        2 + nz,
    )
    for which in LATER:
        fetch[which].start()
    bufs = (core_send, core_land, x_send, x_land)
    sems = (cs, cr, xs, xr)
    def columns(i):
        return pl.ds(pl.multiple_of(i * chunk, LANES), chunk)

    def back_in(who, i):
        weights = w_qkv[i // 2, lax.rem(i, 2)].reshape(chunk, 2 * half)
        return dot(qkv_rows[who], weights, 1, 1)

    first = TokenSum(lambda who, i: dx_part[who, :, columns(i)], bufs, sems, 0)
    second = TokenSum(lambda who, i: out_part[who, :, columns(i)], bufs, sems, 1)
    third = TokenSum(back_in, bufs, sems, 2)
    swap = remote(low_rows.at[c], low_rows.at[c], ns.at[0], nr.at[0], {"pr": 1 - c})

    def residual_back():
        def one(i, sums):
            here = columns(i)
            first.arrived(i)
            grad = first.total(i)
            back_rows[:, here] = grad
            value = residual[:, here]
            return (
                sums[0] + jnp.sum(value * value, axis=1, keepdims=True),
                sums[1] + jnp.sum(grad * full_gains[1, :, here] * value, axis=1, keepdims=True),
            )

        zero = jnp.zeros((span, 1), F32)
        squares, inner_sum = lax.fori_loop(0, 4, one, (zero, zero))
        factor = lax.rsqrt(squares / width + EPS)
        slope = factor * factor * factor * (inner_sum / width)

        def two(i, _):
            here = columns(i)
            grad = back_rows[:, here]
            value = residual[:, here]
            gain_rows[1:2, here] = jnp.sum(grad * value * factor, axis=0, keepdims=True)
            back = (
                upstream[:, here].astype(F32)
                + factor * (grad * full_gains[1, :, here])
                - value * slope
            )
            back_rows[:, here] = back
            low_rows[c, :, here] = back.astype(BF16)
            return 0

        lax.fori_loop(0, 4, two, 0)
        first.drain()
        swap.start()

    def low_rows_in():
        remote(low_rows.at[1 - c], low_rows.at[1 - c], ns.at[0], nr.at[0], {"pr": 1 - c}).wait_recv()

    def heads_back():
        fetch[17].wait()
        fetch[14].wait()
        for b in range(2):

            def add(i, total, b=b):
                weights = w_out[i // 2, lax.rem(i, 2)].reshape(chunk, half)
                return total + dot(low_rows[b, :, columns(i)], weights)

            grads = lax.fori_loop(0, 4, add, jnp.zeros((span, half), F32))
            wide = dot(grads.astype(BF16), spread_mat[...]).astype(BF16)
            for k in range(2):
                for j in range(2):
                    head = 2 * k + j
                    grad_items[b * 2 + k, pl.ds(j * span, span)] = wide[
                        :, head * LANES : (head + 1) * LANES
                    ]

        def one(i, _):
            part = dot(low_rows[0, :, columns(i)], mixed_low[:span], 0, 0) + dot(
                low_rows[1, :, columns(i)], mixed_low[span:], 0, 0
            )
            o_part[i // 2, lax.rem(i, 2)] = part.astype(BF16).reshape(o_part.shape[2:])
            return 0

        lax.fori_loop(0, 4, one, 0)

    def deltas():
        fetch[13].wait()
        for i in range(4):
            delta[i] = jnp.broadcast_to(
                jnp.sum(grad_items[i].astype(F32) * mixed_wide[i], axis=1, keepdims=True),
                delta.shape[1:],
            )
        dq[...] = jnp.zeros_like(dq)
        load_start(0)

    slots = kv_send.shape[0]
    order = scatter.order

    def keys_hop(b, place):
        offset = order[place]
        return remote(
            kv_send.at[place % slots, b],
            kv_land.at[offset, b],
            ks.at[b, offset],
            kr.at[b, offset],
            {"ctx": line.partner(low_bit(offset))},
        )

    def keys_add(b, place, offset):
        remote(
            kv_send.at[place % slots, b],
            kv_land.at[offset, b],
            ks.at[b, offset],
            kr.at[b, offset],
            {"ctx": line.partner(low_bit(offset))},
        ).wait_recv()
        kv_send[place % slots, b] = (
            kv_send[place % slots, b].astype(F32) + kv_land[offset, b].astype(F32)
        ).astype(BF16)

    def load(place):
        block = line.at(order[place])
        return pltpu.make_async_copy(kv_all.at[block], kv_here.at[place % 2], bs.at[place % 2])

    def load_start(place):
        @pl.when(line.at(order[place]) <= z)
        def _():
            load(place).start()

    def back_block(place, diagonal):
        block, slot = line.at(order[place]), place % 2
        load(place).wait()

        def one(b, _):
            key_grads, value_grads = [], []
            wide_kv = dot(kv_here[slot, b], spread_mat[...]).astype(BF16)
            for k in range(2):
                item = b * 2 + k
                keys = wide_kv[:, k * LANES : (k + 1) * LANES]
                values = wide_kv[:, (2 + k) * LANES : (3 + k) * LANES]
                scores = dot(q_items[item], keys, 1, 1) * scale
                allowed = q_seg[b] == k_seg[b, block]
                if diagonal:
                    row = lax.broadcasted_iota(jnp.int32, scores.shape, 0)
                    column = lax.broadcasted_iota(jnp.int32, scores.shape, 1)
                    allowed = allowed & (lax.rem(row, span) >= column)
                probs = jnp.where(allowed, jnp.exp(scores - lse[item][:, :1]), 0.0)
                prob_grad = dot(grad_items[item], values, 1, 1)
                score_grad = (probs * (prob_grad - delta[item][:, :1])).astype(BF16)
                value_grads.append(dot(probs.astype(BF16), grad_items[item], 0, 0))
                key_grads.append(dot(score_grad, q_items[item], 0, 0) * scale)
                dq[item] += dot(score_grad, keys) * scale
            wide = jnp.concatenate(key_grads + value_grads, axis=1).astype(BF16)
            kv_send[place % slots, b] = dot(wide, spread_mat[...], 1, 1).astype(BF16)
            return 0

        lax.fori_loop(0, 2, one, 0)

    def keys_pass(place):
        offset = order[place]

        @pl.when(line.at(offset) <= z)
        def _():
            for b in range(2):
                for level in range(low_bit(offset)):
                    keys_add(b, place, offset ^ (1 << level))
                keys_hop(b, place).start()

    def keys_sent(place):
        @pl.when(line.at(order[place]) <= z)
        def _():
            for b in range(2):
                keys_hop(b, place).wait_send()

    final = nz - 1

    def attend_back(place):
        if place == 0:
            fetch[11].wait()
            fetch[15].wait()
        if place < final:
            load_start(place + 1)
        if place >= slots:
            keys_sent(place - slots)
        if place == final:
            back_block(final, True)
            return

        @pl.when(line.at(order[place]) <= z)
        def _():
            back_block(place, False)

        if low_bit(order[place]) == 0 or slots < nz:
            keys_pass(place)

    def keys_final():
        for level in range(line.levels):

            @pl.when(line.bits[level] == 0)
            def _(level=level):
                for b in range(2):
                    keys_add(b, final, 1 << level)

    def layer_rows():
        def one(i, _):
            second.arrived(i)
            layer_out[:, columns(i)] = (residual[:, columns(i)] + second.total(i)).astype(BF16)
            return 0

        lax.fori_loop(0, 4, one, 0)
        second.drain()

    def unrotated(field, b):
        turned = pltpu.roll(field, LANES // 2, 1)
        here = pl.ds(b * span, span)
        return (field * cos[here] - turned * sin[here]).astype(BF16)

    def qkv_back():
        fetch[18].wait()
        for b in range(2):
            heads = [
                unrotated(dq[b * 2 + k, pl.ds(j * span, span)], b) for k in range(2) for j in range(2)
            ]
            qkv_rows[b, :, :half] = dot(
                jnp.concatenate(heads, axis=1), spread_mat[...], 1, 1
            ).astype(BF16)
        for b in range(2):
            wide = dot(kv_send[final % slots, b], spread_mat[...])
            fields = [unrotated(wide[:, k * LANES : (k + 1) * LANES], b) for k in range(2)]
            fields += [wide[:, (2 + k) * LANES : (3 + k) * LANES].astype(BF16) for k in range(2)]
            qkv_rows[b, :, half:] = dot(
                jnp.concatenate(fields, axis=1), spread_mat[...], 1, 1
            ).astype(BF16)

        def one(i, _):
            part = dot(normed[0, :, columns(i)], qkv_rows[0], 0, 0) + dot(
                normed[1, :, columns(i)], qkv_rows[1], 0, 0
            )
            qkv_part[i // 2, lax.rem(i, 2)] = part.astype(BF16).reshape(qkv_part.shape[2:])
            return 0

        lax.fori_loop(0, 4, one, 0)

    mine = pltpu.make_async_copy(gain_rows, gains.at[y, c, z], ts.at[2])
    core_gain = remote(gains.at[y, c, z], gains.at[y, c, z], ts.at[1], tr.at[1], {"pr": 1 - c})
    gain_line = remote(gains.at[y], gains.at[y], ts.at[0], tr.at[0], {"fy": 1 - y})

    def gain_to(t):
        return remote(gains.at[y, :, z], gains.at[y, :, z], gs.at[t], gr.at[z], {"ctx": t})

    def gain_from(t):
        return remote(gains.at[y, :, t], gains.at[y, :, t], gs.at[t], gr.at[t], {"ctx": t})

    def input_back():
        fetch[3].wait()
        def one(i, sums):
            here = columns(i)
            third.arrived(i)
            value = rows[:, here].astype(F32)
            weighed = third.total(i) * full_gains[0, :, here] * value
            return (
                sums[0] + jnp.sum(value * value, axis=1, keepdims=True),
                sums[1] + jnp.sum(weighed, axis=1, keepdims=True),
            )

        zero = jnp.zeros((span, 1), F32)
        squares, inner_sum = lax.fori_loop(0, 4, one, (zero, zero))
        factor = lax.rsqrt(squares / width + EPS)
        slope = factor * factor * factor * (inner_sum / width)

        def two(i, _):
            here = columns(i)
            value = rows[:, here].astype(F32)
            grad = third.total(i)
            gain_rows[0:1, here] = jnp.sum(grad * value * factor, axis=0, keepdims=True)
            input_grad[:, here] = (
                back_rows[:, here] + factor * (grad * full_gains[0, :, here]) - value * slope
            ).astype(BF16)
            return 0

        lax.fori_loop(0, 4, two, 0)
        third.drain()
        mine.start()
        mine.wait()
        core_gain.start()
        remote(
            gains.at[y, 1 - c, z], gains.at[y, 1 - c, z], ts.at[1], tr.at[1], {"pr": 1 - c}
        ).wait_recv()
        for t in range(nz):

            @pl.when(z != t)
            def _(t=t):
                gain_to(t).start()

    def gains_in():
        for t in range(nz):

            @pl.when(z != t)
            def _(t=t):
                gain_from(t).wait_recv()

        gain_line.start()

    start, relay, step, last = scatter.start, scatter.relay, scatter.step, scatter.last

    def grow(g):
        if g == 2:
            fetch[19].wait()
        which = 19 + g
        fetch[which].wait()
        weight_grad(sources[g], normed_mlp, operands[which], stage, stage_sems)

    def start_sum(n):
        if n:
            fetch[(None, 1, 16)[n]].wait()
        (first, second, third)[n].start()

    if nz == 4:
        plan = [
            (start, 0), (start_sum, 0), (grow, 2), (start, 2), (step, 0, 0), (grow, 1),
            (step, 0, 1), (residual_back,),
            (step, 0, 2), (low_rows_in,), (heads_back,), (start, 3), (start, 1), (deltas,),
            (step, 2, 0), (attend_back, 0), (start_sum, 1), (step, 2, 1), (attend_back, 1),
            (attend_back, 2), (step, 3, 0), (step, 3, 1), (keys_pass, 2), (step, 2, 2),
            (attend_back, 3), (keys_final,), (layer_rows,), (qkv_back,), (start, 4),
            (step, 1, 0), (step, 3, 2), (step, 1, 1), (relay, 0), (start_sum, 2), (step, 1, 2),
            (step, 4, 0), (step, 4, 1), (input_back,), (last, 2), (step, 4, 2), (last, 0),
            (last, 1), (last, 3), (gains_in,), (last, 4),
        ]
    else:
        plan = [(start, 0), (start_sum, 0), (grow, 2), (start, 2), (grow, 1), (start, 1)]
        plan += [(residual_back,)]
        plan += [(low_rows_in,), (heads_back,), (start, 3), (deltas,)]
        plan += [(attend_back, place) for place in range(nz)]
        plan += [(keys_pass, place) for place in range(nz // 2, nz - 1) if nz <= 4]
        plan += [(start_sum, 1), (keys_final,), (layer_rows,), (qkv_back,), (start, 4)]
        plan += [(relay, g) for g in RELAYED] + [(start_sum, 2)]
        plan += [(step, g, place) for g in range(4) for place in range(nz - 1)]
        plan += [(input_back,), (gains_in,)] + [(step, 4, place) for place in range(nz - 1)]
        plan += [(last, g) for g in range(5)]
    for run, *which in plan:
        run(*which)
    remote(gains.at[1 - y], gains.at[1 - y], ts.at[0], tr.at[0], {"fy": 1 - y}).wait_recv()
    for g in range(5):
        scatter.finish(g)
    core_gain.wait_send()
    gain_line.wait_send()
    swap.wait_send()
    for t in range(nz):

        @pl.when(z != t)
        def _(t=t):
            gain_to(t).wait_send()

    for place in range(max(0, nz - slots), final):
        keys_sent(place)


def backward(down_grad, operands, ny, nz):
    dma = pltpu.SemaphoreType.DMA
    anywhere = pl.BlockSpec(memory_space=pl.ANY)
    vmem = pl.BlockSpec(memory_space=pltpu.VMEM)
    residual = operands[2]
    span, width = residual.shape
    chunk = width // 4
    block = down_grad.shape[3]
    half = 4 * DH
    wide = [down_grad.shape[4]] * 3 + [half, 2 * half]
    shape = jax.ShapeDtypeStruct
    out_shape = (
        [shape((span, width), BF16)] * 2
        + [shape((2, block, w), F32) for w in wide]
        + [shape((ny, 2, nz, 2, width), F32)]
        + [shape(down_grad.shape, BF16)] * 2
    )

    def bufs(lead, dtype=BF16):
        return [pltpu.VMEM(lead + (block, w), dtype) for w in wide]

    return pl.pallas_call(
        functools.partial(backward_kernel, nz, DH ** (-0.5)),
        out_shape=out_shape,
        in_specs=[anywhere] + [anywhere if n in (12, *LATER) else vmem for n in range(22)],
        out_specs=[vmem] * 2 + [anywhere] * 8,
        scratch_shapes=[pltpu.VMEM(operands[n].shape, operands[n].dtype) for n in LATER]
        + bufs((2, 2))[:3]
        + bufs((nz, 2))
        + bufs((nz - 1, 2))
        + bufs((2,), F32)
        + [pltpu.VMEM((block, wide[g]), BF16) for g in RELAYED * 2]
        + [
            pltpu.VMEM((ny, 2, nz, block, half), BF16),
            pltpu.VMEM((ny, 2, nz, block, 2 * half), BF16),
            pltpu.VMEM((4, span, chunk), BF16),
            pltpu.VMEM((2, 4, span, chunk), BF16),
            pltpu.VMEM((4, span, chunk), BF16),
            pltpu.VMEM((2, 4, span, chunk), BF16),
            pltpu.VMEM((span, width), F32),
            pltpu.VMEM((2, span, width), BF16),
            pltpu.VMEM((4, 2 * span, LANES), BF16),
            pltpu.VMEM((4, 2 * span, LANES), F32),
            pltpu.VMEM((4, 2 * span, LANES), F32),
            pltpu.VMEM((min(nz, 4), 2, span, half), BF16),
            pltpu.VMEM((nz, 2, span, half), BF16),
            pltpu.VMEM((2, span, 2 * half), BF16),
            pltpu.VMEM((2, width), F32),
            pltpu.VMEM((2, 2, span, half), BF16),
        ]
        + [dma((5, 5))]
        + [dma((5, nz + 1))] * 2
        + [dma((5,))] * 2
        + [dma((5, nz))] * 2
        + [dma((5,))] * 2
        + [dma((3, 4))] * 4
        + [dma((1,))] * 2
        + [dma((2, nz))] * 2
        + [dma((nz,))] * 2
        + [dma((3,)), dma((2,)), dma((2,))]
        + [pltpu.VMEM((2,) + down_grad.shape[2:], BF16), dma((2,)), dma((len(LATER),))],
        name="backward",
        compiler_params=pltpu.CompilerParams(
            collective_id=2, has_side_effects=True, vmem_limit_bytes=VMEM_LIMIT
        ),
    )(down_grad, *operands)


def on_device(
    ny,
    nz,
    layer_input,
    segments,
    positions,
    attn_gain,
    query_proj,
    key_proj,
    value_proj,
    out_proj,
    mlp_gain,
    gate_proj,
    up_proj,
    down_proj,
    out_grad,
):
    _, span, width = layer_input.shape
    block = query_proj.shape[0]
    freq_index = np.arange(LANES) % (LANES // 2)
    freq = jnp.asarray((THETA ** (-2.0 * freq_index / DH)).astype(np.float32)[None])
    rows = layer_input.reshape(span, width)
    upstream = out_grad.reshape(span, width)
    (
        w_qkv, w_out, q_items, kv_all, mixed_wide, mixed_low, row_lse, residual, normed_attn, dx_part,
        out_part, normed_mlp, gate_grad, up_grad, spread_mat, down_grad, cos_wide, sin_wide, q_seg, k_seg, full_gains,
    ) = forward(
        (query_proj, key_proj, value_proj, out_proj.T, gate_proj, up_proj, down_proj.T),
        rows, upstream, segments, positions, attn_gain.reshape(1, block), mlp_gain.reshape(1, block),
        freq, ny, nz,
    )
    operands = (
        dx_part, out_part, residual, rows, upstream, full_gains, cos_wide, sin_wide, q_seg, k_seg,
        spread_mat, q_items, kv_all, mixed_wide, mixed_low, row_lse, w_qkv, w_out,
        normed_attn, normed_mlp, gate_grad, up_grad,
    )
    layer_output, input_grad, down_g, gate_g, up_g, out_g, qkv_g, gains_all, *_ = backward(
        down_grad, operands, ny, nz
    )
    layer_output, input_grad, q_g, k_g, v_g, o_g, gate_g, up_g, down_g, attn_g, mlp_g = assemble(
        down_g, gate_g, up_g, out_g, qkv_g, gains_all, layer_output, input_grad, nz
    )
    return (
        layer_output.reshape(1, span, width),
        input_grad.reshape(1, span, width),
        attn_g.reshape(block),
        q_g,
        k_g,
        v_g,
        o_g.T,
        mlp_g.reshape(block),
        gate_g,
        up_g,
        down_g.T,
    )


def assemble_kernel(nz, down, gate, up, out, qkv, gains, layer, back, *refs):
    layer_out, back_out, q_out, k_out, v_out, o_out, gate_out, up_out, down_out, attn, mlp = refs
    layer_out[...] = layer[...]
    back_out[...] = back[...]
    for halves, whole in ((gate, gate_out), (up, up_out), (down, down_out), (out, o_out)):
        size = halves.shape[2]
        whole[:, :size] = halves[0]
        whole[:, size:] = halves[1]
    size = q_out.shape[1] // 2
    q_out[:, :size] = qkv[0, :, :size]
    q_out[:, size:] = qkv[1, :, :size]
    both = [qkv[which, :, size:] for which in range(2)]
    k_out[...] = jnp.concatenate([part[:, : size // 2] for part in both], axis=1)
    v_out[...] = jnp.concatenate([part[:, size // 2 :] for part in both], axis=1)
    block, width = attn.shape[1], gains.shape[4]
    total = gains[0, 0, 0]
    for n in range(1, 4 * nz):
        total = total + gains[n // (2 * nz), n // nz % 2, n % nz]
    place = ((lax.axis_index("fy") * 2 + lax.axis_index("pr")) * nz + lax.axis_index("ctx")) * block
    own = pltpu.roll(total, lax.rem(width - place, width), 1)
    attn[...] = own[0:1, :block]
    mlp[...] = own[1:2, :block]


def assemble(down, gate, up, out, qkv, gains, layer, back, nz):
    vmem = pl.BlockSpec(memory_space=pltpu.VMEM)
    shape = jax.ShapeDtypeStruct
    block = down.shape[1]
    size = out.shape[2]
    outs = [shape(layer.shape, BF16), shape(back.shape, BF16), shape((block, 2 * size), F32)]
    outs += [shape((block, size), F32)] * 2 + [shape((block, 2 * size), F32)]
    outs += [shape((block, 2 * down.shape[2]), F32)] * 3 + [shape((1, block), F32)] * 2
    return pl.pallas_call(
        functools.partial(assemble_kernel, nz),
        out_shape=outs,
        in_specs=[vmem] * 8,
        out_specs=[vmem] * len(outs),
        name="assemble",
        compiler_params=pltpu.CompilerParams(vmem_limit_bytes=VMEM_LIMIT),
    )(down, gate, up, out, qkv, gains, layer, back)


def solution(mesh):
    sizes = mesh.shape
    ny, nz = sizes["fsdp"] // 2, sizes["ctx"]
    inner = Mesh(
        mesh.devices.reshape(ny, 2, nz, sizes["tp"]), ("fy", "pr", "ctx", "tp")
    )
    seqs = ("fy", "pr")
    rows = P(seqs, "ctx", None)
    marks = P(seqs, "ctx")
    gain = P(GROUP)
    tall = P(GROUP, "tp")
    wide = P("tp", GROUP)
    return jax.shard_map(
        functools.partial(on_device, ny, nz),
        mesh=inner,
        in_specs=(
            rows, marks, marks, gain, tall, tall, tall, wide, gain, tall, tall, wide, rows,
        ),
        out_specs=(rows, rows, gain, tall, tall, tall, wide, gain, tall, tall, wide),
        check_vma=False,
    )
```

```python
import functools

import jax
import jax.numpy as jnp
import numpy as np
from jax import lax
from jax.experimental import pallas as pl
from jax.experimental.pallas import tpu as pltpu
from jax.sharding import Mesh, PartitionSpec as P

HQ = 16
HK = 8
DH = 96


EPS = 1e-05
THETA = 100000.0
NEGATIVE = -1e30


def contract(left, right, left_dim, right_dim):
    return lax.dot_general(
        left, right, (((left_dim,), (right_dim,)), ((), ())), preferred_element_type=jnp.float32
    )


MESH_ID = pl.DeviceIdType.MESH
BF16 = jnp.bfloat16
F32 = jnp.float32
GROUP = ("fy", "pr", "ctx")
VMEM_LIMIT = 62 * 1024 * 1024
LANES = 128


def remote(src, dst, send_sem, recv_sem, device):
    return pltpu.make_async_remote_copy(
        src_ref=src,
        dst_ref=dst,
        send_sem=send_sem,
        recv_sem=recv_sem,
        device_id=device,
        device_id_type=MESH_ID,
    )


def greet(devices_and_conditions, count):
    barrier = pltpu.get_barrier_semaphore()
    for device, condition in devices_and_conditions:
        if condition is None:
            pl.semaphore_signal(barrier, inc=1, device_id=device, device_id_type=MESH_ID)
        else:

            @pl.when(condition)
            def _(device=device):
                pl.semaphore_signal(barrier, inc=1, device_id=device, device_id_type=MESH_ID)

    pl.semaphore_wait(barrier, count)


def dot(left, right, left_dim=1, right_dim=0):
    return lax.dot_general(
        left, right, (((left_dim,), (right_dim,)), ((), ())), preferred_element_type=F32
    )


def low_bit(number):
    return (number & -number).bit_length() - 1


class Line:
    def __init__(self, nz):
        self.nz, self.levels = nz, nz.bit_length() - 1
        self.z = lax.axis_index("ctx")
        self.bits = [lax.rem(self.z // (1 << level), 2) for level in range(self.levels)]

    def at(self, offset):
        place = self.z
        for level in range(self.levels):
            if offset >> level & 1:
                place = place + (1 << level) - (2 << level) * self.bits[level]
        return place

    def partner(self, level):
        return self.at(1 << level)


class Gather:
    def __init__(self, line, outs, zs, zr, ys, yr):
        self.line, self.outs = line, outs
        self.zs, self.zr, self.ys, self.yr = zs, zr, ys, yr
        self.y = lax.axis_index("fy")
        offsets = range(1, line.nz)
        self.arrivals = sorted(offsets, key=lambda offset: (-low_bit(offset), offset))

    def hop(self, g, offset, level):
        piece = self.outs[g].at[self.y, :, self.line.at(offset)]
        slot = offset + (1 << level)
        return remote(
            piece, piece, self.zs.at[g, slot], self.zr.at[g, slot], {"ctx": self.line.partner(level)}
        )

    def hop_from(self, g, offset):
        piece = self.outs[g].at[self.y, :, self.line.at(offset)]
        partner = self.line.partner(low_bit(offset))
        return remote(piece, piece, self.zs.at[g, offset], self.zr.at[g, offset], {"ctx": partner})

    def across(self, g, offset, row):
        piece = self.outs[g].at[row, :, self.line.at(offset)]
        return remote(
            piece, piece, self.ys.at[g, offset], self.yr.at[g, offset], {"fy": 1 - self.y}
        )

    def hops(self, offset):
        last = low_bit(offset) if offset else self.line.levels
        return reversed(range(last))

    def own_z(self, g):
        for level in self.hops(0):
            self.hop(g, 0, level).start()

    def own_y(self, g):
        self.across(g, 0, self.y).start()

    def step(self, g, offset):
        self.hop_from(g, offset).wait_recv()
        for level in self.hops(offset):
            self.hop(g, offset, level).start()
        self.across(g, offset, self.y).start()

    def finish(self, g):
        for offset in (0, *self.arrivals):
            self.across(g, offset, 1 - self.y).wait_recv()

    def drain(self, g):
        for offset in (0, *self.arrivals):
            for level in self.hops(offset):
                self.hop(g, offset, level).wait_send()
            self.across(g, offset, self.y).wait_send()


class TokenSum:
    def __init__(self, part, bufs, sems, n):
        self.part, self.n = part, n
        self.core_send, self.core_land, self.x_send, self.x_land = bufs
        self.cs, self.cr, self.xs, self.xr = sems
        self.c = lax.axis_index("pr")
        self.x = lax.axis_index("tp")

    def core(self, i):
        return remote(
            self.core_send.at[i],
            self.core_land.at[self.n % 2, i],
            self.cs.at[self.n, i],
            self.cr.at[self.n, i],
            {"pr": 1 - self.c},
        )

    def sideways(self, i):
        return remote(
            self.x_send.at[i],
            self.x_land.at[self.n % 2, i],
            self.xs.at[self.n, i],
            self.xr.at[self.n, i],
            {"tp": 1 - self.x},
        )

    def start(self):
        def give(i, _):
            self.core_send[i] = self.part(1 - self.c, i).astype(BF16)
            self.core(i).start()
            return 0

        def add(i, _):
            mine = self.part(self.c, i).astype(F32)
            self.core(i).wait_recv()
            self.x_send[i] = (mine + self.core_land[self.n % 2, i].astype(F32)).astype(BF16)
            self.sideways(i).start()
            return 0

        lax.fori_loop(0, 4, give, 0)
        lax.fori_loop(0, 4, add, 0)

    def arrived(self, i):
        self.sideways(i).wait_recv()

    def total(self, i):
        return self.x_send[i].astype(F32) + self.x_land[self.n % 2, i].astype(F32)

    def drain(self):
        for i in range(4):
            self.core(i).wait_send()
            self.sideways(i).wait_send()


def weight_grad(into, left, right, stage, sems):
    _, span, width = left.shape
    chunk = width // 4

    def stored_part(i):
        slot = lax.rem(i, 2)
        return pltpu.make_async_copy(stage.at[slot], into.at[i // 2, slot], sems.at[slot])

    def one(i, _):
        here = pl.ds(pl.multiple_of(i * chunk, LANES), chunk)
        part = dot(left[0, :, here], right[:span], 0, 0) + dot(left[1, :, here], right[span:], 0, 0)

        @pl.when(i > 1)
        def _():
            stored_part(i - 2).wait()

        stage[lax.rem(i, 2)] = part.astype(BF16).reshape(stage.shape[1:])
        stored_part(i).start()
        return 0

    lax.fori_loop(0, 4, one, 0)
    for i in (2, 3):
        stored_part(i).wait()


def forward_kernel(nz, items, scale, *refs):
    query_w, key_w, value_w, *other_w = refs[:7]
    rows, upstream, segments, positions, attn_gain, mlp_gain, freq = refs[7:14]
    stored = refs[14:29]
    down_grad = refs[29]
    cos, sin, q_seg, k_seg, gains = refs[30:35]
    made = refs[35:50]
    (
        w_qkv, w_out, q_out, kvu, mixed_out, mixed_low, lse_out, residual, normed, dx_part, out_part,
        normed_mlp, gate_grad, up_grad, spread_mat,
    ) = made
    (
        w_gate, w_up, w_down, acc, keys, values, top, core_send, core_land, x_send, x_land, smalls, info_both,
        rows_both, gate_pre, up_pre, upstream_both, hidden, stage, small, info, kv_w,
    ) = refs[50:72]
    (
        loc, ps, pr, ws, wr, ts, tr, zs, zr, ys, yr, ks, kr, cs, cr, xs, xr, ns, nr, hs, gs,
    ) = refs[72:]

    def store(n):
        return pltpu.make_async_copy(made[n], stored[n], hs.at[n])

    outs = (w_qkv, w_out, w_gate, w_up, w_down)
    y = lax.axis_index("fy")
    c = lax.axis_index("pr")
    z = lax.axis_index("ctx")
    x = lax.axis_index("tp")
    span, width = rows.shape
    other_y, other_c, other_x = {"fy": 1 - y}, {"pr": 1 - c}, {"tp": 1 - x}
    line = Line(nz)
    gather = Gather(line, outs, zs, zr, ys, yr)
    chunk = width // 4
    half = w_out.shape[4]
    block = w_out.shape[3]
    late = (2, 3, 4)

    def columns(i):
        return pl.ds(pl.multiple_of(i * chunk, LANES), chunk)

    weights = (query_w, kv_w, *other_w)
    near = key_w.shape[1] // 2
    kv_w[...] = jnp.concatenate(
        [key_w[:, :near], value_w[:, :near], key_w[:, near:], value_w[:, near:]], axis=1
    )

    small[...] = jnp.zeros_like(small)
    small[0:1, :block] = attn_gain[...].astype(F32)
    small[1:2, :block] = mlp_gain[...].astype(F32)
    square = (LANES, LANES)
    for part in range(span // LANES):
        here = pl.ds(part * LANES, LANES)
        segment = segments[:, here].astype(F32)
        position = positions[:, here].astype(F32)
        small[2 + part : 3 + part] = segment
        lane = lax.broadcasted_iota(jnp.int32, square, 1)
        info[here] = jnp.where(
            lane == 0,
            jnp.transpose(jnp.broadcast_to(position, square)),
            jnp.transpose(jnp.broadcast_to(segment, square)),
        )

    greet(
        [(other_y, None), (other_c, None), (other_x, None)]
        + [({"ctx": line.at(offset)}, None) for offset in range(1, nz)],
        2 + nz,
    )

    places = [(0, 0, half), (0, half, half), (1, 0, half)]
    places += [(g, 0, outs[g].shape[4]) for g in late]

    def half_of(n, which):
        size = places[n][2]
        return weights[n].at[:, pl.ds(pl.multiple_of(which * size, LANES), size)]

    def piece_of(n):
        g, first, size = places[n]
        return outs[g].at[y, c, z, :, pl.ds(first, size)]

    def other_piece(n):
        g, first, size = places[n]
        return outs[g].at[y, 1 - c, z, :, pl.ds(first, size)]

    moved = [(rows, rows_both), (upstream, upstream_both), (info, info_both)]
    local = [pltpu.make_async_copy(half_of(n, c), piece_of(n), loc.at[n]) for n in range(6)]
    local += [
        pltpu.make_async_copy(src, dst.at[c], loc.at[6 + n]) for n, (src, dst) in enumerate(moved)
    ]
    sent = [
        remote(half_of(n, 1 - c), piece_of(n), ps.at[n], pr.at[n], other_c) for n in range(6)
    ]
    sent += [
        remote(src, dst.at[c], ps.at[6 + n], pr.at[6 + n], other_c)
        for n, (src, dst) in enumerate(moved)
    ]
    landed = [
        remote(half_of(n, 1 - c), other_piece(n), ps.at[n], pr.at[n], other_c) for n in range(6)
    ]
    landed += [
        remote(src, dst.at[1 - c], ps.at[6 + n], pr.at[6 + n], other_c)
        for n, (src, dst) in enumerate(moved)
    ]

    def small_to(offset):
        return remote(
            small, smalls.at[y, c, z], ws.at[offset], wr.at[offset], {"ctx": line.at(offset)}
        )

    def small_from(offset):
        return remote(
            small, smalls.at[y, c, line.at(offset)], ws.at[offset], wr.at[offset],
            {"ctx": line.at(offset)},
        )

    small_here = pltpu.make_async_copy(small, smalls.at[y, c, z], loc.at[9])
    for n in range(2):
        sent[n].start()
        local[n].start()
    small_here.start()
    for offset in range(1, nz):
        small_to(offset).start()
    local[2].start()
    sent[2].start()
    for n in (6, 8, 3, 4, 5, 7):
        local[n].start()
        sent[n].start()
    for n in range(2):
        local[n].wait()
        landed[n].wait_recv()
    gather.own_y(0)
    gather.own_z(0)
    small_here.wait()
    for offset in range(1, nz):
        small_from(offset).wait_recv()
    small_line = remote(smalls.at[y, c], smalls.at[y, c], ts.at[0], tr.at[0], other_y)
    small_line.start()
    small_plane = remote(smalls.at[:, c], smalls.at[:, c], ts.at[1], tr.at[1], other_c)
    for n in (5, 4, 2, 3):
        local[n].wait()
        landed[n].wait_recv()

    def prepare():
        row = lax.broadcasted_iota(jnp.int32, spread_mat.shape, 0)
        column = lax.broadcasted_iota(jnp.int32, spread_mat.shape, 1)
        head = sum((row >= k * DH).astype(jnp.int32) for k in range(1, 4))
        row = row - head * DH
        row = row + head * LANES + jnp.where(row >= DH // 2, LANES // 2 - DH // 2, 0)
        spread_mat[...] = jnp.where(row == column, 1.0, 0.0).astype(BF16)
        store(14).start()
        remote(smalls.at[1 - y, c], smalls.at[1 - y, c], ts.at[0], tr.at[0], other_y).wait_recv()
        small_plane.start()
        for n in (6, 7, 8):
            local[n].wait()
            landed[n].wait_recv()
        factors = []
        for b in range(2):
            value = rows_both[b].astype(F32)
            factors.append(lax.rsqrt(jnp.sum(value * value, axis=1, keepdims=True) / width + EPS))
            angles = info_both[b, :, 0:1] * freq[...]
            lane = lax.broadcasted_iota(jnp.int32, (span, LANES), 1)
            used = lax.rem(lane, LANES // 2) < DH // 2
            here = pl.ds(b * span, span)
            cos[here] = jnp.where(used, jnp.cos(angles), 0.0)
            turn = jnp.where(used, jnp.sin(angles), 0.0)
            sin[here] = jnp.where(lane < LANES // 2, -turn, turn)
            for j in range(2):
                q_seg[b, pl.ds(j * span, span)] = info_both[b, :, 1:2]
        remote(smalls.at[:, 1 - c], smalls.at[:, 1 - c], ts.at[1], tr.at[1], other_c).wait_recv()
        per = span // LANES
        for b in range(2):
            for j in range(nz):
                for part in range(per):
                    k_seg[b, j, :, pl.ds(part * LANES, LANES)] = smalls[
                        y, b, j, pl.ds(2 + part, 1)
                    ]
        for which in range(2):
            gain_row = jnp.zeros((1, width), F32)
            blank = jnp.zeros((1, width - LANES), F32)
            for n in range(4 * nz):
                own = smalls[n // (2 * nz), n // nz % 2, n % nz, pl.ds(which, 1)]
                wide = jnp.concatenate([own, blank], axis=1)
                gain_row = gain_row + (pltpu.roll(wide, n * block, 1) if n else wide)
            gains[which] = gain_row
        for b in range(2):
            normed[b] = (rows_both[b].astype(F32) * factors[b] * gains[0]).astype(BF16)
        store(8).start()

    def head_fields():
        acc[...] = jnp.zeros_like(acc)

        def one(i, _):
            part = w_qkv[i // 2, lax.rem(i, 2)].reshape(chunk, 2 * half)
            wide = jnp.concatenate(
                [
                    dot(part[:, :half], spread_mat[...]).astype(BF16),
                    dot(part[:, half:], spread_mat[...]).astype(BF16),
                ],
                axis=1,
            )
            for b in range(2):
                acc[pl.ds(b * span, span)] += dot(normed[b, :, columns(i)], wide)
            return 0

        lax.fori_loop(0, 4, one, 0)

    def rotated(b, lane):
        here = pl.ds(b * span, span)
        field = acc[here, pl.ds(lane * LANES, LANES)]
        turned = pltpu.roll(field, LANES // 2, 1)
        return (field * cos[here] + turned * sin[here]).astype(BF16)

    def keys_hop(b, offset, level):
        piece = kvu.at[line.at(offset), b]
        slot = offset + (1 << level)
        return remote(
            piece, piece, ks.at[b, slot], kr.at[b, slot], {"ctx": line.partner(level)}
        )

    def keys_from(b, offset):
        piece = kvu.at[line.at(offset), b]
        partner = line.partner(low_bit(offset))
        return remote(piece, piece, ks.at[b, offset], kr.at[b, offset], {"ctx": partner})

    def each_hop(offset, act):
        for level in gather.hops(offset):

            @pl.when(line.at(offset) <= line.partner(level))
            def _(level=level):
                act(level)

    def project_heads():
        head_fields()
        for b in range(2):
            fields = []
            for k in range(2):
                keys[b * 2 + k] = rotated(b, 4 + k)
                fields.append(keys[b * 2 + k])
            for k in range(2):
                values[b * 2 + k] = acc[
                    pl.ds(b * span, span), pl.ds((6 + k) * LANES, LANES)
                ].astype(BF16)
                fields.append(values[b * 2 + k])
            kvu[z, b] = dot(jnp.concatenate(fields, axis=1), spread_mat[...], 1, 1).astype(BF16)
            each_hop(0, lambda level, b=b: keys_hop(b, 0, level).start())

        for b in range(2):
            for k in range(2):
                for j in range(2):
                    q_out[b * 2 + k, pl.ds(j * span, span)] = rotated(b, 2 * k + j)

    def attend(there, first):
        def one(n, _):
            i = n // 2
            b = i // 2
            here = pl.ds(pl.multiple_of(lax.rem(n, 2) * span, span), span)
            scores = dot(q_out[i, here], keys[i], 1, 1) * scale
            allowed = q_seg[b, :span] == k_seg[b, there]
            if first:
                row = lax.broadcasted_iota(jnp.int32, scores.shape, 0)
                column = lax.broadcasted_iota(jnp.int32, scores.shape, 1)
                allowed = allowed & (row >= column)
            scores = jnp.where(allowed, scores, NEGATIVE)
            peak = jnp.max(scores, axis=1, keepdims=True)
            if first:
                probs = jnp.exp(scores - peak)
                total = jnp.sum(probs, axis=1, keepdims=True)
                mixed_out[i, here] = dot(probs.astype(BF16), values[i])
            else:
                old = top[i, here][:, :1]
                peak = jnp.maximum(old, peak)
                keep = jnp.exp(old - peak)
                probs = jnp.exp(scores - peak)
                total = keep * lse_out[i, here][:, :1] + jnp.sum(probs, axis=1, keepdims=True)
                mixed_out[i, here] = keep * mixed_out[i, here] + dot(
                    probs.astype(BF16), values[i]
                )
            top[i, here] = jnp.broadcast_to(peak, (span, LANES))
            lse_out[i, here] = jnp.broadcast_to(total, (span, LANES))
            return 0

        lax.fori_loop(0, 2 * items, one, 0)

    def attend_own():
        attend(z, True)

    def keys_in(offset):
        @pl.when(line.at(offset) <= z)
        def _():
            for b in range(2):
                keys_from(b, offset).wait_recv()
                each_hop(offset, lambda level, b=b: keys_hop(b, offset, level).start())

    def attend_at(offset):
        there = line.at(offset)

        @pl.when(there <= z)
        def _():
            for b in range(2):
                wide = dot(kvu[there, b], spread_mat[...]).astype(BF16)
                for k in range(2):
                    keys[b * 2 + k] = wide[:, k * LANES : (k + 1) * LANES]
                    values[b * 2 + k] = wide[:, (2 + k) * LANES : (3 + k) * LANES]
            attend(there, False)

    def close():
        def divide(i, _):
            total = lse_out[i]
            mixed_out[i] = mixed_out[i] / total
            lse_out[i] = top[i] + jnp.log(total)
            return 0

        lax.fori_loop(0, items, divide, 0)
        for b in range(2):
            heads = [
                mixed_out[b * 2 + k, pl.ds(j * span, span)].astype(BF16)
                for k in range(2)
                for j in range(2)
            ]
            mixed_low[pl.ds(b * span, span)] = dot(
                jnp.concatenate(heads, axis=1), spread_mat[...], 1, 1
            ).astype(BF16)
        for n in (2, 3, 4, 5, 6):
            store(n).start()

    def projected(who, i):
        part = w_out[i // 2, lax.rem(i, 2)].reshape(chunk, half)
        return dot(mixed_low[pl.ds(pl.multiple_of(who * span, span), span)], part, 1, 1)

    token_sum = TokenSum(
        projected, (core_send, core_land, x_send, x_land), (cs, cr, xs, xr), 0
    )
    swap = remote(normed_mlp.at[c], normed_mlp.at[c], ns.at[0], nr.at[0], other_c)

    def add_residual():
        def one(i, _):
            token_sum.arrived(i)
            residual[:, columns(i)] = rows[:, columns(i)].astype(F32) + token_sum.total(i)
            return 0

        lax.fori_loop(0, 4, one, 0)
        store(7).start()

    def norm():
        def one(i, squares):
            total = residual[:, columns(i)]
            return squares + jnp.sum(total * total, axis=1, keepdims=True)

        squares = lax.fori_loop(0, 4, one, jnp.zeros((span, 1), F32))
        factor = lax.rsqrt(squares / width + EPS)

        def two(i, _):
            here = columns(i)
            normed_mlp[c, :, here] = (residual[:, here] * factor * gains[1, :, here]).astype(BF16)
            return 0

        lax.fori_loop(0, 4, two, 0)
        swap.start()

    def swapped():
        remote(normed_mlp.at[1 - c], normed_mlp.at[1 - c], ns.at[0], nr.at[0], other_c).wait_recv()

    size = 256
    blocks = w_gate.shape[4] // size

    def column_block(ref, n):
        part = ref[:, :, :, :, pl.ds(pl.multiple_of(n * size, size), size)]
        return part.reshape(width, size)

    def project(into, ref):
        def one(n, _):
            cols = pl.ds(pl.multiple_of(n * size, size), size)
            part = column_block(ref, n)
            for b in range(2):
                into[pl.ds(b * span, span), cols] = dot(normed_mlp[b], part)
            return 0

        lax.fori_loop(0, blocks, one, 0)

    def hidden_block(n, _):
        cols = pl.ds(pl.multiple_of(n * size, size), size)
        for b in range(2):
            here = pl.ds(b * span, span)
            gate = gate_pre[here, cols]
            hidden[here, cols] = (gate * jax.nn.sigmoid(gate) * up_pre[here, cols]).astype(BF16)
        return 0

    def grads_block(n, _):
        cols = pl.ds(pl.multiple_of(n * size, size), size)
        part = column_block(w_down, n)
        for b in range(2):
            here = pl.ds(b * span, span)
            back = dot(upstream_both[b], part)
            gate, up = gate_pre[here, cols], up_pre[here, cols]
            open_part = jax.nn.sigmoid(gate)
            gate_grad[here, cols] = (
                back * up * open_part * (1.0 + gate * (1.0 - open_part))
            ).astype(BF16)
            up_grad[here, cols] = (back * (gate * open_part)).astype(BF16)
        return 0

    def back_block(i, _):
        cols = pl.ds(pl.multiple_of(i * chunk, LANES), chunk)
        gate_part = w_gate[i // 2, lax.rem(i, 2)].reshape(chunk, blocks * size)
        up_part = w_up[i // 2, lax.rem(i, 2)].reshape(chunk, blocks * size)
        down_part = w_down[i // 2, lax.rem(i, 2)].reshape(chunk, blocks * size)
        for b in range(2):
            here = pl.ds(b * span, span)
            dx_part[b, :, cols] = (
                dot(gate_grad[here], gate_part, 1, 1) + dot(up_grad[here], up_part, 1, 1)
            ).astype(BF16)
            out_part[b, :, cols] = dot(hidden[here], down_part, 1, 1).astype(BF16)
        return 0

    own_z, own_y, step = gather.own_z, gather.own_y, gather.step

    def finish(g):
        gather.finish(g)
        if g < 2:
            store(g).start()

    start_sum = token_sum.start

    def gate():
        project(gate_pre, w_gate)

    def up():
        project(up_pre, w_up)

    def hide():
        lax.fori_loop(0, blocks, hidden_block, 0)
        weight_grad(down_grad, upstream_both, hidden, stage, gs)

    def grads():
        lax.fori_loop(0, blocks, grads_block, 0)
        for n in (11, 12, 13):
            store(n).start()

    def back_rows():
        lax.fori_loop(0, 4, back_block, 0)
        store(9).start()
        store(10).start()

    arrivals = gather.arrivals
    if nz == 4:
        plan = [
            (own_y, 3), (step, 0, 2), (step, 0, 1), (own_z, 1), (step, 0, 3), (step, 1, 2),
            (own_z, 2), (own_y, 4), (prepare,), (own_y, 2), (finish, 0), (own_y, 1),
            (project_heads,), (attend_own,), (step, 2, 1), (step, 1, 1), (step, 2, 2),
            (keys_in, 2), (own_z, 3), (step, 1, 3), (keys_in, 1), (attend_at, 2), (attend_at, 1),
            (step, 2, 3), (step, 3, 2), (keys_in, 3), (attend_at, 3), (step, 3, 1), (close,),
            (finish, 1), (own_z, 4), (start_sum,), (finish, 2), (step, 3, 3), (step, 4, 2),
            (add_residual,), (finish, 3), (step, 4, 1), (norm,), (swapped,), (gate,),
            (step, 4, 3), (up,), (hide,), (finish, 4), (grads,), (back_rows,),
        ]
    else:
        plan = [(own_z, 1), (own_y, 1), (prepare,)]
        plan += [(step, g, offset) for offset in arrivals for g in (0, 1)]
        plan += [(run, g) for g in late for run in (own_z, own_y)]
        plan += [(finish, 0), (project_heads,), (attend_own,)]
        plan += [(run, offset) for offset in arrivals for run in (keys_in, attend_at)]
        plan += [(close,), (finish, 1), (start_sum,)]
        plan += [(step, g, offset) for offset in arrivals for g in late]
        plan += [(add_residual,), (norm,), (swapped,), (finish, 2), (gate,), (finish, 3), (up,)]
        plan += [(hide,), (finish, 4), (grads,), (back_rows,)]
    for run, *which in plan:
        run(*which)

    for g in range(5):
        gather.drain(g)
    for b in range(2):
        each_hop(0, lambda level, b=b: keys_hop(b, 0, level).wait_send())
        for offset in gather.arrivals:

            @pl.when(line.at(offset) <= z)
            def _(b=b, offset=offset):
                each_hop(offset, lambda level: keys_hop(b, offset, level).wait_send())

    for n in range(15):
        store(n).wait()
    token_sum.drain()
    swap.wait_send()
    for copy in sent:
        copy.wait_send()
    small_line.wait_send()
    small_plane.wait_send()
    for offset in range(1, nz):
        small_to(offset).wait_send()


def forward(weights, rows, upstream, segments, positions, attn_gain, mlp_gain, freq, ny, nz):
    dma = pltpu.SemaphoreType.DMA
    vmem = pl.BlockSpec(memory_space=pltpu.VMEM)
    span, width = rows.shape
    block, half, wide = weights[0].shape[0], weights[0].shape[1] // 2, weights[4].shape[1] // 2
    items, q_rows, both = 4, 2 * span, 2 * span
    shape = jax.ShapeDtypeStruct
    chunk = width // 4
    anywhere = pl.BlockSpec(memory_space=pl.ANY)
    weight = (ny, 2, nz, block)
    made = [
        (weight + (2 * half,), BF16),
        (weight + (half,), BF16),
        ((items, q_rows, LANES), BF16),
        ((nz, 2, span, half), BF16),
        ((items, q_rows, LANES), F32),
        ((both, half), BF16),
        ((items, q_rows, LANES), F32),
        ((span, width), F32),
        ((2, span, width), BF16),
        ((2, span, width), BF16),
        ((2, span, width), BF16),
        ((2, span, width), BF16),
        ((both, wide), BF16),
        ((both, wide), BF16),
        ((half, 4 * LANES), BF16),
    ]
    out_shape = [shape(*each) for each in made] + [shape(weight + (wide,), BF16)]
    out_shape += [
        shape((both, LANES), F32),
        shape((both, LANES), F32),
        shape((2, q_rows, 1), F32),
        shape((2, nz, 1, span), F32),
        shape((2, 1, width), F32),
    ]
    return pl.pallas_call(
        functools.partial(forward_kernel, nz, items, DH ** (-0.5)),
        out_shape=out_shape,
        in_specs=[vmem] * 14,
        out_specs=[anywhere] * 16 + [vmem] * 5,
        scratch_shapes=[pltpu.VMEM(*each) for each in made]
        + [pltpu.VMEM(weight + (wide,), BF16)] * 3
        + [
            pltpu.VMEM((both, 8 * LANES), F32),
            pltpu.VMEM((items, span, LANES), BF16),
            pltpu.VMEM((items, span, LANES), BF16),
            pltpu.VMEM((items, q_rows, LANES), F32),
            pltpu.VMEM((4, span, chunk), BF16),
            pltpu.VMEM((1, 4, span, chunk), BF16),
            pltpu.VMEM((4, span, chunk), BF16),
            pltpu.VMEM((1, 4, span, chunk), BF16),
            pltpu.VMEM((ny, 2, nz, 8, LANES), F32),
            pltpu.VMEM((2, span, LANES), F32),
            pltpu.VMEM((2, span, width), BF16),
            pltpu.VMEM((both, wide), F32),
            pltpu.VMEM((both, wide), F32),
            pltpu.VMEM((2, span, width), BF16),
            pltpu.VMEM((both, wide), BF16),
            pltpu.VMEM((2, nz, block, wide), BF16),
            pltpu.VMEM((8, LANES), F32),
            pltpu.VMEM((span, LANES), F32),
            pltpu.VMEM((block, 2 * half), BF16),
        ]
        + [dma((10,)), dma((9,)), dma((9,)), dma((nz,)), dma((nz,)), dma((2,)), dma((2,))]
        + [dma((5, nz))] * 4
        + [dma((2, nz))] * 2
        + [dma((1, 4))] * 4
        + [dma((1,))] * 2
        + [dma((15,)), dma((2,))],
        name="forward",
        compiler_params=pltpu.CompilerParams(
            collective_id=1, has_side_effects=True, vmem_limit_bytes=VMEM_LIMIT
        ),
    )(*weights, rows, upstream, segments, positions, attn_gain, mlp_gain, freq)


RELAYED = (0,)
LATER = (19, 21, 20, 17, 14, 13, 11, 15, 1, 18, 16, 3)


class Scatter:
    def __init__(self, line, sources, owns, lands, ins, mids, extras, totals, outs, sems):
        self.line, self.sources, self.owns, self.lands = line, sources, owns, lands
        self.ins, self.mids, self.extras = ins, mids, extras
        self.totals, self.outs, self.sems = totals, outs, sems
        self.y = lax.axis_index("fy")
        self.c = lax.axis_index("pr")
        nz = line.nz
        self.order = sorted(range(1, nz), key=lambda offset: (low_bit(offset), -offset)) + [0]

    def own_copy(self, g, place):
        return pltpu.make_async_copy(
            self.sources[g].at[self.y, :, self.line.at(self.order[place])],
            self.owns[g].at[place % 2],
            self.sems[0].at[g, 3 + place % 2],
        )

    def own(self, g, place, k, rows):
        if self.owns[g] is None:
            place_at = self.line.at(self.order[place])
            return self.sources[g][self.y, k, place_at, rows].astype(F32)
        return self.owns[g][place % 2, k, rows].astype(F32)

    def fetch(self, g, place):
        if self.owns[g] is not None and place < self.line.nz:
            self.own_copy(g, place).start()

    def fetched(self, g, place):
        if self.owns[g] is not None:
            self.own_copy(g, place).wait()

    def middle(self, g):
        return pltpu.make_async_copy(
            self.sources[g].at[1 - self.y, 1, self.line.z], self.mids[g], self.sems[0].at[g, 1]
        )

    def across(self, g, offset):
        ys, yr = self.sems[1], self.sems[2]
        src, dst, place = self.sources[g], self.lands[g], self.line.at(offset)
        if offset > 1 or g not in RELAYED:
            src, dst = src.at[1 - self.y, :, place], dst.at[offset]
        else:
            src, dst = src.at[1 - self.y, 0, place], dst.at[offset, 0]
        return remote(src, dst, ys.at[g, offset], yr.at[g, offset], {"fy": 1 - self.y})

    def relayed(self, g):
        ys, yr = self.sems[1], self.sems[2]
        slot = self.line.nz
        return remote(
            self.mids[g], self.lands[g].at[0, 1], ys.at[g, slot], yr.at[g, slot], {"fy": 1 - self.y}
        )

    def extra(self, g):
        es, er = self.sems[3], self.sems[4]
        src = self.sources[g].at[1 - self.y, 1, self.line.at(1)]
        return remote(src, self.extras[g], es.at[g], er.at[g], {"ctx": self.line.partner(0)})

    def hop(self, g, offset):
        zs, zr = self.sems[5], self.sems[6]
        return remote(
            self.lands[g].at[offset],
            self.ins[g].at[offset - 1],
            zs.at[g, offset],
            zr.at[g, offset],
            {"ctx": self.line.partner(low_bit(offset))},
        )

    def swap(self, g, slot):
        cs, cr = self.sems[7], self.sems[8]
        return remote(
            self.totals[g].at[1 - self.c], self.outs[g].at[slot], cs.at[g], cr.at[g], {"pr": 1 - self.c}
        )

    def keep(self, g):
        return pltpu.make_async_copy(
            self.totals[g].at[self.c], self.outs[g].at[self.c], self.sems[0].at[g, 2]
        )

    def each_tile(self, g, body):
        block = self.lands[g].shape[2]
        rows = 32 if block % 32 == 0 else block
        per = block // rows

        def step(i, _):
            body(i // per, pl.ds(pl.multiple_of(lax.rem(i, per) * rows, 8), rows))
            return 0

        lax.fori_loop(0, 2 * per, step, 0)

    def start(self, g):
        self.fetch(g, 0)
        self.fetch(g, 1)
        if g in RELAYED:
            self.middle(g).start()
            self.extra(g).start()
            self.lands[g][1, 1] = jnp.zeros(self.lands[g].shape[2:], BF16)
        for offset in self.order:
            self.across(g, offset).start()

    def relay(self, g):
        self.middle(g).wait()
        self.extra(g).wait_recv()
        self.mids[g][...] = (
            self.mids[g][...].astype(F32) + self.extras[g][...].astype(F32)
        ).astype(BF16)
        self.relayed(g).start()

    def step(self, g, place):
        offset = self.order[place]
        land, into = self.lands[g], self.ins[g]
        self.fetched(g, place)
        self.across(g, offset).wait_recv()
        arrived = [offset ^ (1 << level) for level in range(low_bit(offset))]
        for other in arrived:
            self.hop(g, other).wait_recv()

        def add(k, rows):
            total = self.own(g, place, k, rows) + land[offset, k, rows].astype(F32)
            for other in arrived:
                total = total + into[other - 1, k, rows].astype(F32)
            land[offset, k, rows] = total.astype(BF16)

        self.each_tile(g, add)
        self.hop(g, offset).start()
        self.fetch(g, place + 2)

    def last(self, g):
        place = self.line.nz - 1
        land, into = self.lands[g], self.ins[g]
        total = self.totals[g]
        self.fetched(g, place)
        self.across(g, 0).wait_recv()
        if g in RELAYED:
            self.relayed(g).wait_recv()
        arrived = [1 << level for level in range(self.line.levels)]
        for other in arrived:
            self.hop(g, other).wait_recv()

        def add(k, rows):
            value = self.own(g, place, k, rows) + land[0, k, rows].astype(F32)
            for other in arrived:
                value = value + into[other - 1, k, rows].astype(F32)
            total[k, rows] = value

        self.each_tile(g, add)
        self.swap(g, self.c).start()
        self.keep(g).start()

    def finish(self, g):
        self.swap(g, 1 - self.c).wait_recv()
        self.swap(g, self.c).wait_send()
        self.keep(g).wait()
        if g in RELAYED:
            self.extra(g).wait_send()
            self.relayed(g).wait_send()
        for offset in self.order:
            self.across(g, offset).wait_send()
            if offset:
                self.hop(g, offset).wait_send()


def backward_kernel(nz, scale, *refs):
    operands = list(refs[1:23])
    layer_out, input_grad = refs[23:25]
    outs = refs[25:30]
    gains = refs[30]
    sources = (refs[0], refs[31], refs[32])
    fetched, scratch = refs[33 : 33 + len(LATER)], refs[33 + len(LATER) : -3]
    stage, stage_sems = refs[-3], refs[-2]
    fetch = {}
    for n, which in enumerate(LATER):
        fetch[which] = pltpu.make_async_copy(operands[which], fetched[n], refs[-1].at[n])
        operands[which] = fetched[n]
    (
        dx_part, out_part, residual, rows, upstream, full_gains, cos, sin, q_seg, k_seg,
        spread_mat, q_items, kv_all, mixed_wide, mixed_low, lse, w_qkv, w_out, normed,
        normed_mlp, gate_grad, up_grad,
    ) = operands
    kept = 3
    owns = (*scratch[:kept], None, None)
    lands, ins, totals = (scratch[kept + 5 * i : kept + 5 * i + 5] for i in range(3))
    mids, extras = ({g: ref} for g, ref in zip(RELAYED * 2, scratch[kept + 15 : kept + 17]))
    (
        o_part, qkv_part, core_send, core_land, x_send, x_land, back_rows, low_rows, grad_items,
        delta, dq, kv_send, kv_land, qkv_rows, gain_rows, kv_here,
    ) = scratch[kept + 17 : kept + 33]
    (
        loc, ys, yr, es, er, zs, zr, ss, sr, cs, cr, xs, xr, ns, nr, ks, kr, gs, gr, ts, tr, bs,
    ) = scratch[kept + 33 :]
    y = lax.axis_index("fy")
    c = lax.axis_index("pr")
    z = lax.axis_index("ctx")
    span, width = rows.shape
    chunk = width // 4
    half = 4 * DH
    sources = (*sources, o_part, qkv_part)
    line = Line(nz)
    scatter = Scatter(
        line, sources, owns, lands, ins, mids, extras, totals, outs,
        (loc, ys, yr, es, er, zs, zr, ss, sr),
    )
    greet(
        [
            ({"fy": 1 - y}, None),
            ({"pr": 1 - c}, None),
            ({"tp": 1 - lax.axis_index("tp")}, None),
        ]
        + [({"ctx": t}, z != t) for t in range(nz)],
        2 + nz,
    )
    for which in LATER[:3]:
        fetch[which].start()
    bufs = (core_send, core_land, x_send, x_land)
    sems = (cs, cr, xs, xr)
    def columns(i):
        return pl.ds(pl.multiple_of(i * chunk, LANES), chunk)

    def back_in(who, i):
        weights = w_qkv[i // 2, lax.rem(i, 2)].reshape(chunk, 2 * half)
        return dot(qkv_rows[who], weights, 1, 1)

    first = TokenSum(lambda who, i: dx_part[who, :, columns(i)], bufs, sems, 0)
    second = TokenSum(lambda who, i: out_part[who, :, columns(i)], bufs, sems, 1)
    third = TokenSum(back_in, bufs, sems, 2)
    swap = remote(low_rows.at[c], low_rows.at[c], ns.at[0], nr.at[0], {"pr": 1 - c})

    def residual_back():
        def one(i, sums):
            here = columns(i)
            first.arrived(i)
            grad = first.total(i)
            back_rows[:, here] = grad
            value = residual[:, here]
            return (
                sums[0] + jnp.sum(value * value, axis=1, keepdims=True),
                sums[1] + jnp.sum(grad * full_gains[1, :, here] * value, axis=1, keepdims=True),
            )

        zero = jnp.zeros((span, 1), F32)
        squares, inner_sum = lax.fori_loop(0, 4, one, (zero, zero))
        factor = lax.rsqrt(squares / width + EPS)
        slope = factor * factor * factor * (inner_sum / width)

        def two(i, _):
            here = columns(i)
            grad = back_rows[:, here]
            value = residual[:, here]
            gain_rows[1:2, here] = jnp.sum(grad * value * factor, axis=0, keepdims=True)
            back = (
                upstream[:, here].astype(F32)
                + factor * (grad * full_gains[1, :, here])
                - value * slope
            )
            back_rows[:, here] = back
            low_rows[c, :, here] = back.astype(BF16)
            return 0

        lax.fori_loop(0, 4, two, 0)
        first.drain()
        swap.start()

    def low_rows_in():
        remote(low_rows.at[1 - c], low_rows.at[1 - c], ns.at[0], nr.at[0], {"pr": 1 - c}).wait_recv()

    def heads_back():
        fetch[17].wait()
        fetch[14].wait()
        for b in range(2):

            def add(i, total, b=b):
                weights = w_out[i // 2, lax.rem(i, 2)].reshape(chunk, half)
                return total + dot(low_rows[b, :, columns(i)], weights)

            grads = lax.fori_loop(0, 4, add, jnp.zeros((span, half), F32))
            wide = dot(grads.astype(BF16), spread_mat[...]).astype(BF16)
            for k in range(2):
                for j in range(2):
                    head = 2 * k + j
                    grad_items[b * 2 + k, pl.ds(j * span, span)] = wide[
                        :, head * LANES : (head + 1) * LANES
                    ]

        def one(i, _):
            part = dot(low_rows[0, :, columns(i)], mixed_low[:span], 0, 0) + dot(
                low_rows[1, :, columns(i)], mixed_low[span:], 0, 0
            )
            o_part[i // 2, lax.rem(i, 2)] = part.astype(BF16).reshape(o_part.shape[2:])
            return 0

        lax.fori_loop(0, 4, one, 0)

    def deltas():
        fetch[13].wait()
        for i in range(4):
            delta[i] = jnp.broadcast_to(
                jnp.sum(grad_items[i].astype(F32) * mixed_wide[i], axis=1, keepdims=True),
                delta.shape[1:],
            )
        dq[...] = jnp.zeros_like(dq)
        load_start(0)

    slots = kv_send.shape[0]
    order = scatter.order

    def keys_hop(b, place):
        offset = order[place]
        return remote(
            kv_send.at[place % slots, b],
            kv_land.at[offset, b],
            ks.at[b, offset],
            kr.at[b, offset],
            {"ctx": line.partner(low_bit(offset))},
        )

    def keys_add(b, place, offset):
        remote(
            kv_send.at[place % slots, b],
            kv_land.at[offset, b],
            ks.at[b, offset],
            kr.at[b, offset],
            {"ctx": line.partner(low_bit(offset))},
        ).wait_recv()
        kv_send[place % slots, b] = (
            kv_send[place % slots, b].astype(F32) + kv_land[offset, b].astype(F32)
        ).astype(BF16)

    def load(place):
        block = line.at(order[place])
        return pltpu.make_async_copy(kv_all.at[block], kv_here.at[place % 2], bs.at[place % 2])

    def load_start(place):
        @pl.when(line.at(order[place]) <= z)
        def _():
            load(place).start()

    def back_block(place, diagonal):
        block, slot = line.at(order[place]), place % 2
        load(place).wait()

        def one(b, _):
            key_grads, value_grads = [], []
            wide_kv = dot(kv_here[slot, b], spread_mat[...]).astype(BF16)
            for k in range(2):
                item = b * 2 + k
                keys = wide_kv[:, k * LANES : (k + 1) * LANES]
                values = wide_kv[:, (2 + k) * LANES : (3 + k) * LANES]
                scores = dot(q_items[item], keys, 1, 1) * scale
                allowed = q_seg[b] == k_seg[b, block]
                if diagonal:
                    row = lax.broadcasted_iota(jnp.int32, scores.shape, 0)
                    column = lax.broadcasted_iota(jnp.int32, scores.shape, 1)
                    allowed = allowed & (lax.rem(row, span) >= column)
                probs = jnp.where(allowed, jnp.exp(scores - lse[item][:, :1]), 0.0)
                prob_grad = dot(grad_items[item], values, 1, 1)
                score_grad = (probs * (prob_grad - delta[item][:, :1])).astype(BF16)
                value_grads.append(dot(probs.astype(BF16), grad_items[item], 0, 0))
                key_grads.append(dot(score_grad, q_items[item], 0, 0) * scale)
                dq[item] += dot(score_grad, keys) * scale
            wide = jnp.concatenate(key_grads + value_grads, axis=1).astype(BF16)
            kv_send[place % slots, b] = dot(wide, spread_mat[...], 1, 1).astype(BF16)
            return 0

        lax.fori_loop(0, 2, one, 0)

    def keys_pass(place):
        offset = order[place]

        @pl.when(line.at(offset) <= z)
        def _():
            for b in range(2):
                for level in range(low_bit(offset)):
                    keys_add(b, place, offset ^ (1 << level))
                keys_hop(b, place).start()

    def keys_sent(place):
        @pl.when(line.at(order[place]) <= z)
        def _():
            for b in range(2):
                keys_hop(b, place).wait_send()

    final = nz - 1

    def attend_back(place):
        if place == 0:
            fetch[11].wait()
            fetch[15].wait()
        if place < final:
            load_start(place + 1)
        if place >= slots:
            keys_sent(place - slots)
        if place == final:
            back_block(final, True)
            return

        @pl.when(line.at(order[place]) <= z)
        def _():
            back_block(place, False)

        if low_bit(order[place]) == 0 or slots < nz:
            keys_pass(place)

    def keys_final():
        for level in range(line.levels):

            @pl.when(line.bits[level] == 0)
            def _(level=level):
                for b in range(2):
                    keys_add(b, final, 1 << level)

    def layer_rows():
        def one(i, _):
            second.arrived(i)
            layer_out[:, columns(i)] = (residual[:, columns(i)] + second.total(i)).astype(BF16)
            return 0

        lax.fori_loop(0, 4, one, 0)
        second.drain()

    def unrotated(field, b):
        turned = pltpu.roll(field, LANES // 2, 1)
        here = pl.ds(b * span, span)
        return (field * cos[here] - turned * sin[here]).astype(BF16)

    def qkv_back():
        fetch[18].wait()
        for b in range(2):
            heads = [
                unrotated(dq[b * 2 + k, pl.ds(j * span, span)], b) for k in range(2) for j in range(2)
            ]
            qkv_rows[b, :, :half] = dot(
                jnp.concatenate(heads, axis=1), spread_mat[...], 1, 1
            ).astype(BF16)
        for b in range(2):
            wide = dot(kv_send[final % slots, b], spread_mat[...])
            fields = [unrotated(wide[:, k * LANES : (k + 1) * LANES], b) for k in range(2)]
            fields += [wide[:, (2 + k) * LANES : (3 + k) * LANES].astype(BF16) for k in range(2)]
            qkv_rows[b, :, half:] = dot(
                jnp.concatenate(fields, axis=1), spread_mat[...], 1, 1
            ).astype(BF16)

        def one(i, _):
            part = dot(normed[0, :, columns(i)], qkv_rows[0], 0, 0) + dot(
                normed[1, :, columns(i)], qkv_rows[1], 0, 0
            )
            qkv_part[i // 2, lax.rem(i, 2)] = part.astype(BF16).reshape(qkv_part.shape[2:])
            return 0

        lax.fori_loop(0, 4, one, 0)

    mine = pltpu.make_async_copy(gain_rows, gains.at[y, c, z], ts.at[2])
    core_gain = remote(gains.at[y, c, z], gains.at[y, c, z], ts.at[1], tr.at[1], {"pr": 1 - c})
    gain_line = remote(gains.at[y], gains.at[y], ts.at[0], tr.at[0], {"fy": 1 - y})

    def gain_to(t):
        return remote(gains.at[y, :, z], gains.at[y, :, z], gs.at[t], gr.at[z], {"ctx": t})

    def gain_from(t):
        return remote(gains.at[y, :, t], gains.at[y, :, t], gs.at[t], gr.at[t], {"ctx": t})

    def input_back():
        fetch[3].wait()
        def one(i, sums):
            here = columns(i)
            third.arrived(i)
            value = rows[:, here].astype(F32)
            weighed = third.total(i) * full_gains[0, :, here] * value
            return (
                sums[0] + jnp.sum(value * value, axis=1, keepdims=True),
                sums[1] + jnp.sum(weighed, axis=1, keepdims=True),
            )

        zero = jnp.zeros((span, 1), F32)
        squares, inner_sum = lax.fori_loop(0, 4, one, (zero, zero))
        factor = lax.rsqrt(squares / width + EPS)
        slope = factor * factor * factor * (inner_sum / width)

        def two(i, _):
            here = columns(i)
            value = rows[:, here].astype(F32)
            grad = third.total(i)
            gain_rows[0:1, here] = jnp.sum(grad * value * factor, axis=0, keepdims=True)
            input_grad[:, here] = (
                back_rows[:, here] + factor * (grad * full_gains[0, :, here]) - value * slope
            ).astype(BF16)
            return 0

        lax.fori_loop(0, 4, two, 0)
        third.drain()
        mine.start()
        mine.wait()
        core_gain.start()
        remote(
            gains.at[y, 1 - c, z], gains.at[y, 1 - c, z], ts.at[1], tr.at[1], {"pr": 1 - c}
        ).wait_recv()
        for t in range(nz):

            @pl.when(z != t)
            def _(t=t):
                gain_to(t).start()

    def gains_in():
        for t in range(nz):

            @pl.when(z != t)
            def _(t=t):
                gain_from(t).wait_recv()

        gain_line.start()

    start, relay, step, last = scatter.start, scatter.relay, scatter.step, scatter.last

    def grow(g):
        if g == 2:
            fetch[19].wait()
        which = 19 + g
        fetch[which].wait()
        weight_grad(sources[g], normed_mlp, operands[which], stage, stage_sems)

    def start_sum(n):
        if n:
            fetch[(None, 1, 16)[n]].wait()
        (first, second, third)[n].start()

    if nz == 4:
        plan = [
            (start, 0), (start_sum, 0), (grow, 2), (start, 2), (step, 0, 0), (grow, 1),
            (step, 0, 1), (residual_back,),
            (step, 0, 2), (low_rows_in,), (heads_back,), (start, 3), (start, 1), (deltas,),
            (step, 2, 0), (attend_back, 0), (start_sum, 1), (step, 2, 1), (attend_back, 1),
            (attend_back, 2), (step, 3, 0), (step, 3, 1), (keys_pass, 2), (step, 2, 2),
            (attend_back, 3), (keys_final,), (layer_rows,), (qkv_back,), (start, 4),
            (step, 1, 0), (step, 3, 2), (step, 1, 1), (relay, 0), (start_sum, 2), (step, 1, 2),
            (step, 4, 0), (step, 4, 1), (input_back,), (last, 2), (step, 4, 2), (last, 0),
            (last, 1), (last, 3), (gains_in,), (last, 4),
        ]
    else:
        plan = [(start, 0), (start_sum, 0), (grow, 2), (start, 2), (grow, 1), (start, 1)]
        plan += [(residual_back,)]
        plan += [(low_rows_in,), (heads_back,), (start, 3), (deltas,)]
        plan += [(attend_back, place) for place in range(nz)]
        plan += [(keys_pass, place) for place in range(nz // 2, nz - 1) if nz <= 4]
        plan += [(start_sum, 1), (keys_final,), (layer_rows,), (qkv_back,), (start, 4)]
        plan += [(relay, g) for g in RELAYED] + [(start_sum, 2)]
        plan += [(step, g, place) for g in range(4) for place in range(nz - 1)]
        plan += [(input_back,), (gains_in,)] + [(step, 4, place) for place in range(nz - 1)]
        plan += [(last, g) for g in range(5)]
    plan[0][0](*plan[0][1:])
    for which in LATER[3:]:
        fetch[which].start()
    for run, *which in plan[1:]:
        run(*which)
    remote(gains.at[1 - y], gains.at[1 - y], ts.at[0], tr.at[0], {"fy": 1 - y}).wait_recv()
    for g in range(5):
        scatter.finish(g)
    core_gain.wait_send()
    gain_line.wait_send()
    swap.wait_send()
    for t in range(nz):

        @pl.when(z != t)
        def _(t=t):
            gain_to(t).wait_send()

    for place in range(max(0, nz - slots), final):
        keys_sent(place)


def backward(down_grad, operands, ny, nz):
    dma = pltpu.SemaphoreType.DMA
    anywhere = pl.BlockSpec(memory_space=pl.ANY)
    vmem = pl.BlockSpec(memory_space=pltpu.VMEM)
    residual = operands[2]
    span, width = residual.shape
    chunk = width // 4
    block = down_grad.shape[3]
    half = 4 * DH
    wide = [down_grad.shape[4]] * 3 + [half, 2 * half]
    shape = jax.ShapeDtypeStruct
    out_shape = (
        [shape((span, width), BF16)] * 2
        + [shape((2, block, w), F32) for w in wide]
        + [shape((ny, 2, nz, 2, width), F32)]
        + [shape(down_grad.shape, BF16)] * 2
    )

    def bufs(lead, dtype=BF16):
        return [pltpu.VMEM(lead + (block, w), dtype) for w in wide]

    return pl.pallas_call(
        functools.partial(backward_kernel, nz, DH ** (-0.5)),
        out_shape=out_shape,
        in_specs=[anywhere] + [anywhere if n in (12, *LATER) else vmem for n in range(22)],
        out_specs=[vmem] * 2 + [anywhere] * 8,
        scratch_shapes=[pltpu.VMEM(operands[n].shape, operands[n].dtype) for n in LATER]
        + bufs((2, 2))[:3]
        + bufs((nz, 2))
        + bufs((nz - 1, 2))
        + bufs((2,), F32)
        + [pltpu.VMEM((block, wide[g]), BF16) for g in RELAYED * 2]
        + [
            pltpu.VMEM((ny, 2, nz, block, half), BF16),
            pltpu.VMEM((ny, 2, nz, block, 2 * half), BF16),
            pltpu.VMEM((4, span, chunk), BF16),
            pltpu.VMEM((2, 4, span, chunk), BF16),
            pltpu.VMEM((4, span, chunk), BF16),
            pltpu.VMEM((2, 4, span, chunk), BF16),
            pltpu.VMEM((span, width), F32),
            pltpu.VMEM((2, span, width), BF16),
            pltpu.VMEM((4, 2 * span, LANES), BF16),
            pltpu.VMEM((4, 2 * span, LANES), F32),
            pltpu.VMEM((4, 2 * span, LANES), F32),
            pltpu.VMEM((min(nz, 4), 2, span, half), BF16),
            pltpu.VMEM((nz, 2, span, half), BF16),
            pltpu.VMEM((2, span, 2 * half), BF16),
            pltpu.VMEM((2, width), F32),
            pltpu.VMEM((2, 2, span, half), BF16),
        ]
        + [dma((5, 5))]
        + [dma((5, nz + 1))] * 2
        + [dma((5,))] * 2
        + [dma((5, nz))] * 2
        + [dma((5,))] * 2
        + [dma((3, 4))] * 4
        + [dma((1,))] * 2
        + [dma((2, nz))] * 2
        + [dma((nz,))] * 2
        + [dma((3,)), dma((2,)), dma((2,))]
        + [pltpu.VMEM((2,) + down_grad.shape[2:], BF16), dma((2,)), dma((len(LATER),))],
        name="backward",
        compiler_params=pltpu.CompilerParams(
            collective_id=2, has_side_effects=True, vmem_limit_bytes=VMEM_LIMIT
        ),
    )(down_grad, *operands)


def on_device(
    ny,
    nz,
    layer_input,
    segments,
    positions,
    attn_gain,
    query_proj,
    key_proj,
    value_proj,
    out_proj,
    mlp_gain,
    gate_proj,
    up_proj,
    down_proj,
    out_grad,
):
    _, span, width = layer_input.shape
    block = query_proj.shape[0]
    freq_index = np.arange(LANES) % (LANES // 2)
    freq = jnp.asarray((THETA ** (-2.0 * freq_index / DH)).astype(np.float32)[None])
    rows = layer_input.reshape(span, width)
    upstream = out_grad.reshape(span, width)
    (
        w_qkv, w_out, q_items, kv_all, mixed_wide, mixed_low, row_lse, residual, normed_attn, dx_part,
        out_part, normed_mlp, gate_grad, up_grad, spread_mat, down_grad, cos_wide, sin_wide, q_seg, k_seg, full_gains,
    ) = forward(
        (query_proj, key_proj, value_proj, out_proj.T, gate_proj, up_proj, down_proj.T),
        rows, upstream, segments, positions, attn_gain.reshape(1, block), mlp_gain.reshape(1, block),
        freq, ny, nz,
    )
    operands = (
        dx_part, out_part, residual, rows, upstream, full_gains, cos_wide, sin_wide, q_seg, k_seg,
        spread_mat, q_items, kv_all, mixed_wide, mixed_low, row_lse, w_qkv, w_out,
        normed_attn, normed_mlp, gate_grad, up_grad,
    )
    layer_output, input_grad, down_g, gate_g, up_g, out_g, qkv_g, gains_all, *_ = backward(
        down_grad, operands, ny, nz
    )
    layer_output, input_grad, q_g, k_g, v_g, o_g, gate_g, up_g, down_g, attn_g, mlp_g = assemble(
        down_g, gate_g, up_g, out_g, qkv_g, gains_all, layer_output, input_grad, nz
    )
    return (
        layer_output.reshape(1, span, width),
        input_grad.reshape(1, span, width),
        attn_g.reshape(block),
        q_g,
        k_g,
        v_g,
        o_g.T,
        mlp_g.reshape(block),
        gate_g,
        up_g,
        down_g.T,
    )


def assemble_kernel(nz, down, gate, up, out, qkv, gains, layer, back, *refs):
    layer_out, back_out, q_out, k_out, v_out, o_out, gate_out, up_out, down_out, attn, mlp = refs
    layer_out[...] = layer[...]
    back_out[...] = back[...]
    for halves, whole in ((gate, gate_out), (up, up_out), (down, down_out), (out, o_out)):
        size = halves.shape[2]
        whole[:, :size] = halves[0]
        whole[:, size:] = halves[1]
    size = q_out.shape[1] // 2
    q_out[:, :size] = qkv[0, :, :size]
    q_out[:, size:] = qkv[1, :, :size]
    both = [qkv[which, :, size:] for which in range(2)]
    k_out[...] = jnp.concatenate([part[:, : size // 2] for part in both], axis=1)
    v_out[...] = jnp.concatenate([part[:, size // 2 :] for part in both], axis=1)
    block, width = attn.shape[1], gains.shape[4]
    total = gains[0, 0, 0]
    for n in range(1, 4 * nz):
        total = total + gains[n // (2 * nz), n // nz % 2, n % nz]
    place = ((lax.axis_index("fy") * 2 + lax.axis_index("pr")) * nz + lax.axis_index("ctx")) * block
    own = pltpu.roll(total, lax.rem(width - place, width), 1)
    attn[...] = own[0:1, :block]
    mlp[...] = own[1:2, :block]


def assemble(down, gate, up, out, qkv, gains, layer, back, nz):
    vmem = pl.BlockSpec(memory_space=pltpu.VMEM)
    shape = jax.ShapeDtypeStruct
    block = down.shape[1]
    size = out.shape[2]
    outs = [shape(layer.shape, BF16), shape(back.shape, BF16), shape((block, 2 * size), F32)]
    outs += [shape((block, size), F32)] * 2 + [shape((block, 2 * size), F32)]
    outs += [shape((block, 2 * down.shape[2]), F32)] * 3 + [shape((1, block), F32)] * 2
    return pl.pallas_call(
        functools.partial(assemble_kernel, nz),
        out_shape=outs,
        in_specs=[vmem] * 8,
        out_specs=[vmem] * len(outs),
        name="assemble",
        compiler_params=pltpu.CompilerParams(vmem_limit_bytes=VMEM_LIMIT),
    )(down, gate, up, out, qkv, gains, layer, back)


def solution(mesh):
    sizes = mesh.shape
    ny, nz = sizes["fsdp"] // 2, sizes["ctx"]
    inner = Mesh(
        mesh.devices.reshape(ny, 2, nz, sizes["tp"]), ("fy", "pr", "ctx", "tp")
    )
    seqs = ("fy", "pr")
    rows = P(seqs, "ctx", None)
    marks = P(seqs, "ctx")
    gain = P(GROUP)
    tall = P(GROUP, "tp")
    wide = P("tp", GROUP)
    return jax.shard_map(
        functools.partial(on_device, ny, nz),
        mesh=inner,
        in_specs=(
            rows, marks, marks, gain, tall, tall, tall, wide, gain, tall, tall, wide, rows,
        ),
        out_specs=(rows, rows, gain, tall, tall, tall, wide, gain, tall, tall, wide),
        check_vma=False,
    )
```
